32 devices in a mesh: row: 4 (over z), col: 8 (over y, x, core).
Axes of the slice: x: 2, y: 2, z: 4, core: 2. Of those that a mesh axis runs over, the one named last changes fastest.
Arguments:
- object_field: bfloat16 [2, 2048, 4096], P(None, 'row', 'col'), may hold values from -6 to 6
- probe_modes: float32 [2, 2, 256, 256], replicated, may hold values from -6 to 6
- measured_amp: bfloat16 [4, 8, 8, 256, 256], P('row', 'col'), may hold values from 0.25 to 8
- scan_positions: int32 [4, 8, 2, 8], P('row', 'col'), may hold values from 0 to 512
- frame_counts: int32 [4, 8], P('row', 'col'), may hold values from 1 to 8, as said below
Outputs:
- object_grad: float32 [2, 2048, 4096], P(None, 'row', 'col')
- probe_grad: float32 [2, 2, 256, 256], replicated
The draws below stay inside these ranges and needn't reach their ends.
Inputs may be any that keep to these rules, and one draw needn't show every extreme that they name: `frame_counts`: live frames of a tile; slots at or past it are ignored; some tile has exactly 8.
All inputs are finite; a program needn't handle non-finite values.
Results may differ from the reference program's by a relative error of at most 0.0059.
The reference program's roundings to bfloat16 on the way count: a program that leaves them out, or rounds other values in their place, can miss the bound.
Values may be sent and summed in bfloat16 or wider, within the bound.
A program may use at most 64 MiB of HBM per device.

```python
import math
import jax
import jax.numpy as jnp
from jax import lax

FS = 256
MODES = 2
TILE = 512
HALO = 128
FR_MAX = 8
NR = 2048
NC = 4096
N_ROW = 4
N_COL = 8


def draw_frame_counts(key, part):
    first_key = jax.random.fold_in(key, 11)
    second_key = jax.random.fold_in(key, 12)
    third_key = jax.random.fold_in(key, 13)
    base_counts = jax.random.randint(first_key, (N_ROW * N_COL,), FR_MAX // 4 + 1, 3 * FR_MAX // 4 + 1)
    heavy = jax.random.randint(second_key, (N_ROW * N_COL,), 0, 4) == 0
    chosen = jax.random.randint(third_key, (), 0, N_ROW * N_COL)
    places = jnp.arange(N_ROW * N_COL, dtype=jnp.int32)
    counts_flat = jnp.where(heavy | (places == chosen), FR_MAX, base_counts)
    return counts_flat.reshape(N_ROW, N_COL).astype(jnp.int32)


def place_ends(drawn, rng, least, high):
    shape = drawn.shape
    place = [jax.random.randint(jax.random.fold_in(rng, axis), (), 0, shape[axis]) for axis in range(len(shape))]
    drawn = drawn.at[tuple(place)].set(least)
    longest = shape.index(max(shape))
    place[longest] = (place[longest] + 1) % shape[longest]
    return drawn.at[tuple(place)].set(high)


def block_levels(own_key, dims, split, least, top_value):
    gain, own = 1.0, jax.random.fold_in(own_key, 6)
    for dim, parts in split:
        heights = jnp.exp(jax.random.uniform(jax.random.fold_in(own, dim), (parts,), jnp.float32, least / len(split), top_value / len(split)))
        gain = gain * jnp.repeat(heights, dims[dim] // parts).reshape([-1 if axis == dim else 1 for axis in range(len(dims))])
    return gain


def scatter_about(key, shape, width, bound, cuts=(), held_as=jnp.bfloat16):
    gain = block_levels(key, shape, cuts, -0.22, 0.18) if cuts else 1.0
    entries = jax.random.normal(key, shape, jnp.float32) * width * gain
    return jnp.minimum(jnp.maximum(entries, -bound), bound).astype(held_as)


def setup_inputs(seed: int = 0) -> dict:
    seeds = jax.random.split(jax.random.key(seed), 6)
    object_field = scatter_about(seeds[0], (2, NR, NC), 1.0, 6.0, ((1, 4), (2, 8)))
    probe_modes = scatter_about(seeds[1], (2, MODES, FS, FS), 1.0, 6.0, (), jnp.float32)
    measured_amp = jnp.clip(jnp.exp(math.log(8.0) - 3.465736 * jax.random.uniform(seeds[2], (N_ROW, N_COL, FR_MAX, FS, FS), jnp.float32) ** block_levels(seeds[2], (N_ROW, N_COL, FR_MAX, FS, FS), ((0, 4), (1, 8)), -0.2, 0.2)), 0.25, 8.0).astype(jnp.bfloat16)
    scan_positions = place_ends(jax.random.randint(seeds[3], (N_ROW, N_COL, 2, FR_MAX), 0, TILE + 2 * HALO - FS + 1), jax.random.fold_in(seeds[3], 1), 0, TILE + 2 * HALO - FS).astype(jnp.int32)
    frame_counts = draw_frame_counts(jax.random.fold_in(seeds[5], 71), 0)
    return {"object_field": object_field, "probe_modes": probe_modes, "measured_amp": measured_amp, "scan_positions": scan_positions, "frame_counts": frame_counts}


def fourier_tables(frame_side):
    indices = jnp.arange(frame_side, dtype=jnp.int32)
    product = indices[:, None] * indices[None, :] % frame_side
    angles = 2.0 * math.pi / frame_side * product.astype(jnp.float32)
    norm_scale = 1.0 / math.sqrt(frame_side)
    return ((jnp.cos(angles) * norm_scale).astype(jnp.bfloat16), (-jnp.sin(angles) * norm_scale).astype(jnp.bfloat16))

def left_mul(table, data):
    return jnp.einsum('kn,mnj->mkj', table.astype(jnp.float32), data.astype(jnp.float32))

def right_mul(data, table):
    return jnp.einsum('mkn,nj->mkj', data.astype(jnp.float32), table.astype(jnp.float32))

def transform(real_part, imag_part, table_real, table_imag):
    first_real = (left_mul(table_real, real_part) - left_mul(table_imag, imag_part)).astype(jnp.bfloat16)
    first_imag = (left_mul(table_real, imag_part) + left_mul(table_imag, real_part)).astype(jnp.bfloat16)
    out_real = right_mul(first_real, table_real) - right_mul(first_imag, table_imag)
    out_imag = right_mul(first_real, table_imag) + right_mul(first_imag, table_real)
    return (out_real, out_imag)

def frame_terms(frame_patch, frame_amp, probe_modes, table_real, table_imag):
    probe_real = probe_modes[0]
    probe_imag = probe_modes[1]
    patch_real = frame_patch[0].astype(jnp.float32)
    patch_imag = frame_patch[1].astype(jnp.float32)
    exit_real = (probe_real * patch_real - probe_imag * patch_imag).astype(jnp.bfloat16)
    exit_imag = (probe_real * patch_imag + probe_imag * patch_real).astype(jnp.bfloat16)
    psi_real, psi_imag = transform(exit_real, exit_imag, table_real, table_imag)
    power = lax.optimization_barrier(jnp.sum(psi_real * psi_real + psi_imag * psi_imag, axis=0))
    factor = 1.0 - frame_amp.astype(jnp.float32) / jnp.maximum(jnp.sqrt(power), 0.5)
    chi_real = (psi_real * factor).astype(jnp.bfloat16)
    chi_imag = (psi_imag * factor).astype(jnp.bfloat16)
    back_real, back_imag = transform(chi_real, chi_imag, table_real, -table_imag)
    patch_grad = jnp.stack([lax.optimization_barrier(jnp.sum(probe_real * back_real + probe_imag * back_imag, axis=0)), lax.optimization_barrier(jnp.sum(probe_real * back_imag - probe_imag * back_real, axis=0))])
    probe_term = jnp.stack([patch_real * back_real + patch_imag * back_imag, patch_real * back_imag - patch_imag * back_real])
    return (patch_grad, probe_term)

def reference(object_field, probe_modes, measured_amp, scan_positions, frame_counts):
    table_real, table_imag = fourier_tables(FS)
    padded = jnp.pad(object_field, ((0, 0), (HALO, HALO), (HALO, HALO)))
    start_pair = (jnp.zeros(padded.shape, jnp.float32), jnp.zeros(probe_modes.shape, jnp.float32))

    def visit(position, state_pair):
        position = jnp.asarray(position).astype(jnp.int32)
        tile_row = position // (N_COL * FR_MAX)
        tile_col = position // FR_MAX % N_COL
        slot_at = position % FR_MAX

        def advance(inner_pair):
            gradient, probe_total = inner_pair
            row_at = (tile_row * TILE + scan_positions[tile_row, tile_col, 0, slot_at]).astype(jnp.int32)
            column_at = (tile_col * TILE + scan_positions[tile_row, tile_col, 1, slot_at]).astype(jnp.int32)
            zero_index = jnp.zeros((), jnp.int32)
            frame_patch = lax.dynamic_slice(padded, (zero_index, row_at, column_at), (2, FS, FS))
            patch_grad, probe_term = frame_terms(frame_patch, measured_amp[tile_row, tile_col, slot_at], probe_modes, table_real, table_imag)
            old_block = lax.dynamic_slice(gradient, (zero_index, row_at, column_at), (2, FS, FS))
            gradient = lax.dynamic_update_slice(gradient, old_block + patch_grad, (zero_index, row_at, column_at))
            return (gradient, probe_total + probe_term)
        return lax.cond(slot_at < frame_counts[tile_row, tile_col], advance, lambda unchanged: unchanged, state_pair)
    gradient, probe_total = lax.fori_loop(0, N_ROW * N_COL * FR_MAX, visit, start_pair)
    norm_scale = 1.0 / math.sqrt(N_ROW * N_COL * FR_MAX)
    return (gradient[:, HALO:HALO + N_ROW * TILE, HALO:HALO + N_COL * TILE], probe_total * norm_scale)
```

```python
import functools
import math

import jax
import jax.numpy as jnp
import numpy as np
from jax import lax
from jax.experimental import pallas as pl
from jax.experimental.pallas import tpu as pltpu
from jax.sharding import PartitionSpec as P

HALO = 128
LANES = 128
PARTS = 2
HALO_LIMIT = 20


MESH = pl.DeviceIdType.MESH
SIDES = [(dr, dc) for dr in (-1, 0, 1) for dc in (-1, 0, 1) if (dr, dc) != (0, 0)]


def position():
    return (
        lax.axis_index("row"),
        lax.axis_index("col"),
        lax.axis_size("row"),
        lax.axis_size("col"),
    )


def exists(side):
    row, col, rows, cols = position()
    dr, dc = side
    inside = jnp.bool_(True)
    if dr:
        inside = row + dr >= 0 if dr < 0 else row + dr < rows
    if dc:
        other = col + dc >= 0 if dc < 0 else col + dc < cols
        inside = jnp.logical_and(inside, other) if dr else other
    return inside


def at_side(side):
    row, col, _, _ = position()
    return (row + side[0], col + side[1])


def opposite(side):
    return (-side[0], -side[1])


def part(step, margin, inner):
    return {-1: slice(0, margin), 0: slice(margin, margin + inner), 1: slice(margin + inner, None)}[
        step
    ]


def edge(step, margin, inner):
    return {-1: slice(0, margin), 0: slice(0, inner), 1: slice(inner - margin, inner)}[step]


def to_side(side, index, source, landing, send_sems, recv_sems):
    return pltpu.make_async_remote_copy(
        src_ref=source,
        dst_ref=landing,
        send_sem=send_sems.at[index],
        recv_sem=recv_sems.at[index],
        device_id=at_side(side),
        device_id_type=MESH,
    )


DIRECT = 1


def halo_kernel(whole_ref, ext_ref, acc_ref, pacc_ref, *scratch):
    object_ref, load_sem, row_land, col_land, corner_land, relay_land = scratch[:6]
    row_sems, col_sems, corner_sems, relay_sems = scratch[6:]
    row, col, n_row, n_col = position()
    side_rows, side_cols = object_ref.shape[1:]
    load = pltpu.make_async_copy(whole_ref, object_ref, load_sem)
    load.start()
    steps = (-1, 1)
    pieces = (slice(0, HALO), slice(side_cols - HALO, side_cols), slice(HALO, side_cols - HALO))
    direct = DIRECT * side_rows // 4
    parts = (slice(0, direct), slice(direct, side_rows))

    def has(dr, dc):
        return exists((dr, dc))

    def turns(d):
        return jnp.logical_and(has(0, d), lax.rem(col, 4) == (3 if d > 0 else 0))

    def relays(d):
        other = col - 3 * d
        inside = jnp.logical_and(other >= 0, other < n_col)
        return jnp.logical_and(inside, lax.rem(col, 4) == (2 if d > 0 else 1))

    def lands_by_relay(d):
        return jnp.logical_and(has(0, -d), lax.rem(col, 4) == (0 if d > 0 else 3))

    links = []
    for d in steps:
        links.append((has(d, 0), (row + d, col)))
        links.append((has(0, d), (row, col + d)))
        links.append((turns(d), (row, col + 3 * d)))
        links.append((relays(d), (row, col - 3 * d)))
        links.append((relays(d), (row, col - 2 * d)))
        links.append((lands_by_relay(d), (row, col + 2 * d)))
    barrier = pltpu.get_barrier_semaphore()
    count = jnp.int32(0)
    for there, device in links:

        @pl.when(there)
        def _(device=device):
            pl.semaphore_signal(barrier, inc=1, device_id=device, device_id_type=MESH)

        count = count + there.astype(jnp.int32)
    pl.semaphore_wait(barrier, count)

    def remote(source, landing, sems, index, device):
        return pltpu.make_async_remote_copy(
            src_ref=source,
            dst_ref=landing,
            send_sem=sems.at[0, index],
            recv_sem=sems.at[1, index],
            device_id=device,
            device_id_type=MESH,
        )

    def row_copy(s, p):
        d = steps[s]
        source = whole_ref.at[:, edge(d, HALO, side_rows), pieces[p]]
        return remote(
            source, row_land.at[1 - s, :, :, pieces[p]], row_sems, 3 * s + p, (row + d, col)
        )

    def col_copy(s, p, to_relay=False):
        d = steps[s]
        source = whole_ref.at[:, parts[p], edge(d, HALO, side_cols)]
        if to_relay:
            return pltpu.make_async_remote_copy(
                src_ref=source,
                dst_ref=relay_land.at[s],
                send_sem=col_sems.at[0, 2 * s + p],
                recv_sem=relay_sems.at[1, s],
                device_id=(row, col + 3 * d),
                device_id_type=MESH,
            )
        return remote(
            source, col_land.at[1 - s, :, parts[p], :], col_sems, 2 * s + p, (row, col + d)
        )

    def relay_copy(s):
        d = steps[s]
        return pltpu.make_async_remote_copy(
            src_ref=relay_land.at[s],
            dst_ref=col_land.at[1 - s, :, parts[1], :],
            send_sem=relay_sems.at[0, s],
            recv_sem=col_sems.at[1, 2 * s + 1],
            device_id=(row, col - 2 * d),
            device_id_type=MESH,
        )

    def corner_copy(r, s):
        source = row_land.at[r, :, :, pieces[s]]
        return remote(
            source, corner_land.at[r, 1 - s], corner_sems, 2 * r + s, (row, col + steps[s])
        )

    def when(condition, action):
        @pl.when(condition)
        def _():
            action()

    for p in range(2):
        for s, d in enumerate(steps):
            when(has(d, 0), lambda s=s, p=p: row_copy(s, p).start())
    for p in (1, 0):
        for s, d in enumerate(steps):
            if p:
                when(turns(d), lambda s=s: col_copy(s, 1, True).start())
                straight = jnp.logical_and(has(0, d), jnp.logical_not(turns(d)))
                when(straight, lambda s=s: col_copy(s, 1).start())
            else:
                when(has(0, d), lambda s=s: col_copy(s, 0).start())
    for s, d in enumerate(steps):
        when(has(d, 0), lambda s=s: row_copy(s, 2).start())

    acc_ref[...] = jnp.zeros(acc_ref.shape, jnp.float32)
    pacc_ref[...] = jnp.zeros(pacc_ref.shape, jnp.float32)
    spare = ext_ref.shape[1] - 1
    ext_ref[:, spare] = jnp.zeros((2, ext_ref.shape[2], LANES), jnp.float32)
    margin, inner = HALO // LANES, side_cols // LANES

    def tiles_of(d):
        return range(spare)[part(d, margin, inner)]

    def fill(rows, tiles, height, source):
        for k, t in enumerate(tiles):
            if source is None:
                ext_ref[:, t, rows, :] = jnp.zeros((2, height, LANES), ext_ref.dtype)
            else:
                ext_ref[:, t, rows, :] = source[:, :, k * LANES : (k + 1) * LANES].astype(
                    jnp.float32
                )

    load.wait()
    fill(part(0, HALO, side_rows), tiles_of(0), side_rows, object_ref)

    for s, d in enumerate(steps):

        def pass_on(s=s):
            relay_copy_in = col_copy(s, 1, True)
            relay_copy_in.wait_recv()
            relay_copy(s).start()

        when(relays(d), pass_on)
    for r, dr in enumerate(steps):
        for s, dc in enumerate(steps):

            def hand_over(r=r, s=s, dc=dc):
                row_copy(1 - r, s).wait_recv()
                when(has(0, dc), lambda: corner_copy(r, s).start())

            when(has(dr, 0), hand_over)
    for s, d in enumerate(steps):
        rows = part(0, HALO, side_rows)
        here = s

        def take(s=s, d=d, rows=rows):
            col_copy(1 - s, 0).wait_recv()
            col_copy(1 - s, 1).wait_recv()
            fill(rows, tiles_of(d), side_rows, col_land.at[s])

        when(has(0, d), take)
        when(
            jnp.logical_not(has(0, d)), lambda d=d, rows=rows: fill(rows, tiles_of(d), side_rows, None)
        )
    for r, dr in enumerate(steps):
        rows = part(dr, HALO, side_rows)

        def take_rows(r=r, rows=rows):
            row_copy(1 - r, 2).wait_recv()
            fill(rows, tiles_of(0), HALO, row_land.at[r])

        when(has(dr, 0), take_rows)
        when(
            jnp.logical_not(has(dr, 0)), lambda rows=rows: fill(rows, tiles_of(0), HALO, None)
        )
    for r, dr in enumerate(steps):
        rows = part(dr, HALO, side_rows)
        for s, dc in enumerate(steps):

            def take_corner(r=r, s=s, dc=dc, rows=rows):
                corner_copy(r, 1 - s).wait_recv()
                fill(rows, tiles_of(dc), HALO, corner_land.at[r, s])

            when(has(dr, dc), take_corner)
            when(
                jnp.logical_not(has(dr, dc)),
                lambda dc=dc, rows=rows: fill(rows, tiles_of(dc), HALO, None),
            )

    for s, d in enumerate(steps):
        for p in range(3):
            when(has(d, 0), lambda s=s, p=p: row_copy(s, p).wait_send())
        for p in range(2):
            when(has(0, d), lambda s=s, p=p: col_copy(s, p).wait_send())
        when(relays(d), lambda s=s: relay_copy(s).wait_send())
        for r, dr in enumerate(steps):
            when(has(dr, d), lambda r=r, s=s: corner_copy(r, s).wait_send())


def halo_call(object_field, probe_size):
    planes, side_rows, side_cols = object_field.shape
    kind = object_field.dtype
    vmem = pl.BlockSpec(memory_space=pltpu.VMEM)
    tiled = jax.ShapeDtypeStruct(
        (planes, (side_cols + 2 * HALO) // LANES + 1, side_rows + 2 * HALO, LANES), jnp.float32
    )
    direct = DIRECT * side_rows // 4
    return pl.pallas_call(
        halo_kernel,
        out_shape=(tiled, tiled, jax.ShapeDtypeStruct((probe_size // LANES, LANES), jnp.float32)),
        in_specs=[pl.BlockSpec(memory_space=pltpu.HBM)],
        out_specs=(vmem, vmem, vmem),
        scratch_shapes=[
            pltpu.VMEM(object_field.shape, kind),
            pltpu.SemaphoreType.DMA,
            pltpu.VMEM((2, planes, HALO, side_cols), kind),
            pltpu.VMEM((2, planes, side_rows, HALO), kind),
            pltpu.VMEM((2, 2, planes, HALO, HALO), kind),
            pltpu.VMEM((2, planes, side_rows - direct, HALO), kind),
            pltpu.SemaphoreType.DMA((2, 6)),
            pltpu.SemaphoreType.DMA((2, 4)),
            pltpu.SemaphoreType.DMA((2, 4)),
            pltpu.SemaphoreType.DMA((2, 2)),
        ],
        compiler_params=pltpu.CompilerParams(
            collective_id=0, has_side_effects=True, vmem_limit_bytes=HALO_LIMIT * 1024 * 1024
        ),
        cost_estimate=pl.CostEstimate(flops=10**10, bytes_accessed=0, transcendentals=0),
        name="halo",
    )(pltpu.with_memory_space_constraint(object_field, pltpu.HBM))


def reduce_kernel(scale, acc_ref, pacc_ref, grad_ref, probe_ref, *scratch):
    count = len(SIDES)
    sends, landings, rest = scratch[:count], scratch[count : 2 * count], scratch[2 * count :]
    psend, pair_recv, merged, precv, sums, zbuf, full = rest[:7]
    side_sems, pair_sems, col_sems, row_sems = rest[7:]
    row, col, n_row, n_col = position()
    side_rows, side_cols = grad_ref.shape[1:]
    margin = HALO // LANES
    inner = side_cols // LANES
    part_rows = psend.shape[2]
    share = PARTS * part_rows
    chip, core = col // 2, lax.rem(col, 2)
    n_chip = n_col // 2
    sibling = (row, 2 * chip + 1 - core)

    barrier = pltpu.get_barrier_semaphore()
    waits = jnp.int32(n_row + n_chip - 1)
    pl.semaphore_signal(barrier, inc=1, device_id=sibling, device_id_type=MESH)
    for k in range(1, n_chip):
        peer = (row, 2 * lax.rem(chip + k, n_chip) + core)
        pl.semaphore_signal(barrier, inc=1, device_id=peer, device_id_type=MESH)
    for k in range(1, n_row):
        pl.semaphore_signal(
            barrier, inc=1, device_id=(lax.rem(row + k, n_row), col), device_id_type=MESH
        )
    for side in SIDES:
        if side[1]:

            @pl.when(exists(side))
            def _(side=side):
                pl.semaphore_signal(barrier, inc=1, device_id=at_side(side), device_id_type=MESH)

            waits = waits + exists(side).astype(jnp.int32)

    def stage_side(index):
        dr, dc = SIDES[index]
        tiles = range(inner + 2 * margin)[part(dc, margin, inner)]
        for k, t in enumerate(tiles):
            sends[index][:, k] = acc_ref[:, t, part(dr, HALO, side_rows), :].astype(jnp.bfloat16)

    def stage_sides(chosen):
        for index, side in enumerate(SIDES):
            if chosen(side):
                stage_side(index)

    def to_peer(source, landing, sems, which, k, device):
        return pltpu.make_async_remote_copy(
            src_ref=source,
            dst_ref=landing,
            send_sem=sems.at[which, k],
            recv_sem=sems.at[which + 1, k],
            device_id=device,
            device_id_type=MESH,
        )

    def chip_at(k):
        return lax.rem(chip + k, n_chip)

    def chip_from(k):
        return lax.rem(chip + n_chip - k, n_chip)

    def chip_peer(k):
        return (row, 2 * chip_at(k) + core)

    def rows_of(index, h):
        return pl.ds(pl.multiple_of(index * share + h * part_rows, part_rows), part_rows)

    def pair_copy(h, k):
        return to_peer(
            psend.at[h, k], pair_recv.at[h, k], pair_sems, 0, h * n_chip + k, sibling
        )

    def scatter_copy(h, k):
        at = h * (n_chip - 1) + k - 1
        return to_peer(merged.at[h, k - 1], precv.at[h, k - 1], col_sems, 0, at, chip_peer(k))

    def row_copy(h, k, owner):
        at = h * (n_row - 1) + k - 1
        peer = (lax.rem(row + k, n_row), col)
        return to_peer(zbuf.at[h, row], zbuf.at[h, owner], row_sems, 0, at, peer)

    def gather_copy(h, k, owner):
        at = h * (n_chip - 1) + k - 1
        source, landing = full.at[rows_of(col, h), :], full.at[rows_of(owner, h), :]
        return to_peer(source, landing, col_sems, 2, at, chip_peer(k))

    def forward_copy(h, k, side):
        source = full.at[rows_of(2 * chip_from(k) + core, h), :]
        landing = full.at[rows_of(2 * chip_from(k) + side, h), :]
        return to_peer(source, landing, pair_sems, 2, h * n_chip + k, sibling)

    def side_copy(index):
        return to_side(
            SIDES[index], index, sends[index], landings[index], side_sems.at[0], side_sems.at[1]
        )

    def start_sides(chosen):
        for index, side in enumerate(SIDES):
            if chosen(side):

                @pl.when(exists(side))
                def _(index=index):
                    side_copy(index).start()

    def add_sides(chosen):
        for index, side in enumerate(SIDES):
            if not chosen(side):
                continue
            dr, dc = opposite(side)
            rows = edge(dr, HALO, side_rows)
            tiles = range(inner)[edge(dc, margin, inner)]

            @pl.when(exists((dr, dc)))
            def _(index=index, rows=rows, tiles=tiles):
                side_copy(index).wait_recv()
                for k, t in enumerate(tiles):
                    grad_ref[:, rows, t * LANES : (t + 1) * LANES] += landings[index][
                        :, k
                    ].astype(jnp.float32)

    over_rows = lambda side: side[1] == 0
    over_cols = lambda side: side[0] == 0
    corners = lambda side: side[0] != 0 and side[1] != 0
    order = list(range(1, n_chip)) + [0]
    for h in range(PARTS):
        for k in order:
            psend[h, k] = pacc_ref[rows_of(2 * chip_at(k) + 1 - core, h), :].astype(jnp.bfloat16)
    stage_sides(over_rows)
    pl.semaphore_wait(barrier, waits)
    for h in range(PARTS):
        for k in order:
            pair_copy(h, k).start()
    start_sides(over_rows)
    stage_sides(over_cols)
    stage_sides(corners)

    def merge(h, k):
        pair_copy(h, k).wait_recv()
        own = pacc_ref[rows_of(2 * chip_at(k) + core, h), :]
        return own + pair_recv[h, k].astype(jnp.float32)

    for h in range(PARTS):
        for k in range(1, n_chip):
            merged[h, k - 1] = merge(h, k).astype(jnp.bfloat16)
            scatter_copy(h, k).start()
        sums[h] = merge(h, 0)
    start_sides(over_cols)
    for t in range(inner):
        grad_ref[:, :, t * LANES : (t + 1) * LANES] = acc_ref[
            :, margin + t, HALO : HALO + side_rows, :
        ]
    for h in range(PARTS):
        total = sums[h]
        for k in range(1, n_chip):
            scatter_copy(h, k).wait_recv()
            total = total + precv[h, k - 1].astype(jnp.float32)
        zbuf[h, row] = total.astype(jnp.bfloat16)
        for k in range(1, n_row):
            row_copy(h, k, row).start()
    start_sides(corners)
    for h in range(PARTS):
        for k in range(1, n_row):
            row_copy(h, k, lax.rem(row + n_row - k, n_row)).wait_recv()
        total = zbuf[h, 0].astype(jnp.float32)
        for k in range(1, n_row):
            total = total + zbuf[h, k].astype(jnp.float32)
        full[rows_of(col, h), :] = (total * scale).astype(jnp.bfloat16)
        for k in range(1, n_chip):
            gather_copy(h, k, col).start()
        forward_copy(h, 0, core).start()
    add_sides(over_rows)
    add_sides(over_cols)
    for h in range(PARTS):
        for k in range(1, n_chip):
            gather_copy(h, k, 2 * chip_from(k) + core).wait_recv()
            forward_copy(h, k, core).start()
    add_sides(corners)

    for h in range(PARTS):
        for k in range(n_chip):
            forward_copy(h, k, 1 - core).wait_recv()
    parts, modes, fs, width = probe_ref.shape
    at = 0
    for p in range(parts):
        for m in range(modes):
            for t in range(width // LANES):
                probe_ref[p, m, :, t * LANES : (t + 1) * LANES] = full[at : at + fs, :].astype(
                    jnp.float32
                )
                at += fs
    for h in range(PARTS):
        for k in range(1, n_chip):
            scatter_copy(h, k).wait_send()
            gather_copy(h, k, col).wait_send()
        for k in range(n_chip):
            pair_copy(h, k).wait_send()
            forward_copy(h, k, core).wait_send()
        for k in range(1, n_row):
            row_copy(h, k, row).wait_send()
    for index, side in enumerate(SIDES):

        @pl.when(exists(side))
        def _(index=index):
            side_copy(index).wait_send()


def reduce_call(acc, probe_flat, object_shape, probe_shape, scale):
    n_row, n_col = lax.axis_size("row"), lax.axis_size("col")
    _, side_rows, side_cols = object_shape
    inner = side_cols // LANES
    margin = HALO // LANES
    vmem = pl.BlockSpec(memory_space=pltpu.VMEM)
    buffers = []
    for dr, dc in SIDES:
        buffers.append(
            pltpu.VMEM(
                (2, margin if dc else inner, HALO if dr else side_rows, LANES), jnp.bfloat16
            )
        )
    total_rows = probe_flat.shape[0]
    piece = total_rows // n_col // PARTS
    n_chip = n_col // 2
    return pl.pallas_call(
        functools.partial(reduce_kernel, scale),
        out_shape=(
            jax.ShapeDtypeStruct(object_shape, jnp.float32),
            jax.ShapeDtypeStruct(probe_shape, jnp.float32),
        ),
        in_specs=[vmem, vmem],
        out_specs=(vmem, vmem),
        scratch_shapes=buffers
        + buffers
        + [
            pltpu.VMEM((PARTS, n_chip, piece, LANES), jnp.bfloat16),
            pltpu.VMEM((PARTS, n_chip, piece, LANES), jnp.bfloat16),
            pltpu.VMEM((PARTS, n_chip - 1, piece, LANES), jnp.bfloat16),
            pltpu.VMEM((PARTS, n_chip - 1, piece, LANES), jnp.bfloat16),
            pltpu.VMEM((PARTS, piece, LANES), jnp.float32),
            pltpu.VMEM((PARTS, n_row, piece, LANES), jnp.bfloat16),
            pltpu.VMEM((total_rows, LANES), jnp.bfloat16),
            pltpu.SemaphoreType.DMA((2, len(SIDES))),
            pltpu.SemaphoreType.DMA((4, PARTS * n_chip)),
            pltpu.SemaphoreType.DMA((4, PARTS * (n_chip - 1))),
            pltpu.SemaphoreType.DMA((2, PARTS * (n_row - 1))),
        ],
        compiler_params=pltpu.CompilerParams(
            collective_id=1, has_side_effects=True, vmem_limit_bytes=20 * 1024 * 1024
        ),
        name="reduce",
    )(acc, probe_flat)


def fourier_tables(frame_side):
    indices = np.arange(frame_side)
    product = indices[:, None] * indices[None, :] % frame_side
    angles = 2.0 * math.pi / frame_side * product
    norm_scale = 1.0 / math.sqrt(frame_side)
    real, imag = np.cos(angles) * norm_scale, -np.sin(angles) * norm_scale
    tables = (np.block([[real, -imag], [imag, real]]), np.block([[real, imag], [-imag, real]]))
    return tuple(jnp.asarray(table.astype(np.float32)).astype(jnp.bfloat16) for table in tables)


CHUNK = 32


def dot32(left, right):
    return jnp.dot(left, right, preferred_element_type=jnp.float32)


def frames_kernel(
    count_ref, at_ref, ext_ref, probe_ref, amp_ref, fwd, inv, zero_ref, pzero_ref,
    acc_ref, pacc_ref, *buffers,
):
    fs = probe_ref.shape[-1]
    modes = probe_ref.shape[1]
    lane_tiles = fs // LANES
    last_slot = amp_ref.shape[0] - 1
    live = count_ref[0]
    even, odd = buffers[:4], buffers[4:]
    odd[2][...] = jnp.zeros(odd[2].shape, jnp.float32)
    odd[3][...] = jnp.zeros(odd[3].shape, jnp.float32)

    def two_sided(buffer, left_table, right_table):
        stage, half, wide, _ = buffer
        for m in range(modes):
            both = dot32(left_table[...], stage[:, m * fs : (m + 1) * fs])
            half[m * fs : (m + 1) * fs, :fs] = both[:fs].astype(jnp.bfloat16)
            half[m * fs : (m + 1) * fs, fs:] = both[fs:].astype(jnp.bfloat16)
        wide[...] = dot32(half[...], right_table[...])

    def make_exit(buffer, slot):
        stage, _, _, patch = buffer
        row_at = at_ref[0, slot]
        col_at = at_ref[1, slot]
        tile_at = col_at // LANES
        shift = col_at % LANES
        back_shift = (LANES - shift) % LANES
        lane = lax.broadcasted_iota(jnp.int32, (CHUNK, LANES), 1)
        keep_low = lane < LANES - shift
        for r in range(0, fs, CHUNK):
            rows = slice(r, r + CHUNK)
            values = []
            for plane in range(2):
                rolled = [
                    pltpu.roll(
                        ext_ref[plane, tile_at + t, pl.ds(row_at + r, CHUNK), :], back_shift, 1
                    )
                    for t in range(lane_tiles + 1)
                ]
                values.append(
                    [jnp.where(keep_low, rolled[t], rolled[t + 1]) for t in range(lane_tiles)]
                )
            for t in range(lane_tiles):
                cols = slice(t * LANES, (t + 1) * LANES)
                patch_real, patch_imag = values[0][t], values[1][t]
                patch[0, rows, cols] = patch_real
                patch[1, rows, cols] = patch_imag
                for m in range(modes):
                    probe_real = probe_ref[0, m, rows, cols]
                    probe_imag = probe_ref[1, m, rows, cols]
                    out = slice(m * fs + t * LANES, m * fs + (t + 1) * LANES)
                    stage[rows, out] = (
                        probe_real * patch_real - probe_imag * patch_imag
                    ).astype(jnp.bfloat16)
                    stage[fs + r : fs + r + CHUNK, out] = (
                        probe_real * patch_imag + probe_imag * patch_real
                    ).astype(jnp.bfloat16)

    def make_chi(buffer, slot, valid):
        stage, _, wide, _ = buffer
        for r in range(0, fs, CHUNK):
            for t in range(lane_tiles):
                cols = slice(t * LANES, (t + 1) * LANES)
                imag_cols = slice(fs + t * LANES, fs + (t + 1) * LANES)
                psi = []
                power = None
                for m in range(modes):
                    rows = slice(m * fs + r, m * fs + r + CHUNK)
                    real, imag = wide[rows, cols], wide[rows, imag_cols]
                    psi.append((real, imag))
                    own = real * real + imag * imag
                    power = own if power is None else power + own
                amp = amp_ref[slot, r : r + CHUNK, cols].astype(jnp.float32)
                factor = 1.0 - amp * lax.rsqrt(jnp.maximum(power, 0.25))
                if valid is not None:
                    factor = jnp.where(valid, factor, 0.0)
                for m in range(modes):
                    out = slice(m * fs + t * LANES, m * fs + (t + 1) * LANES)
                    stage[r : r + CHUNK, out] = (psi[m][0] * factor).astype(jnp.bfloat16)
                    stage[fs + r : fs + r + CHUNK, out] = (psi[m][1] * factor).astype(jnp.bfloat16)

    def add_grads(buffer, slot):
        _, _, wide, patch = buffer
        row_at = at_ref[0, slot]
        col_at = at_ref[1, slot]
        tile_at = col_at // LANES
        shift = col_at % LANES
        lane = lax.broadcasted_iota(jnp.int32, (CHUNK, LANES), 1)
        from_same = lane >= shift
        for r in range(0, fs, CHUNK):
            grads = [[], []]
            for t in range(lane_tiles):
                cols = slice(t * LANES, (t + 1) * LANES)
                imag_cols = slice(fs + t * LANES, fs + (t + 1) * LANES)
                patch_real = patch[0, r : r + CHUNK, cols]
                patch_imag = patch[1, r : r + CHUNK, cols]
                total_real = total_imag = None
                for m in range(modes):
                    rows = slice(m * fs + r, m * fs + r + CHUNK)
                    real, imag = wide[rows, cols], wide[rows, imag_cols]
                    probe_real = probe_ref[0, m, r : r + CHUNK, cols]
                    probe_imag = probe_ref[1, m, r : r + CHUNK, cols]
                    own_real = probe_real * real + probe_imag * imag
                    own_imag = probe_real * imag - probe_imag * real
                    total_real = own_real if m == 0 else total_real + own_real
                    total_imag = own_imag if m == 0 else total_imag + own_imag
                    at = (m * lane_tiles + t) * fs + r
                    pacc_ref[at : at + CHUNK, :] += patch_real * real + patch_imag * imag
                    at += modes * lane_tiles * fs
                    pacc_ref[at : at + CHUNK, :] += patch_real * imag - patch_imag * real
                grads[0].append(pltpu.roll(total_real, shift, 1))
                grads[1].append(pltpu.roll(total_imag, shift, 1))
            for plane in range(2):
                rolled = grads[plane]
                for t in range(lane_tiles + 1):
                    same = rolled[t] if t < lane_tiles else 0.0
                    before = rolled[t - 1] if t > 0 else 0.0
                    where = (plane, tile_at + t, pl.ds(row_at + r, CHUNK), slice(None))
                    acc_ref[where] += jnp.where(from_same, same, before)

    def advance(pair, carry):
        first = 2 * pair
        second = jnp.minimum(first + 1, last_slot)
        make_exit(even, first)
        two_sided(even, fwd, inv)
        add_grads(odd, jnp.maximum(first - 1, 0))
        make_exit(odd, second)
        two_sided(odd, fwd, inv)
        make_chi(even, first, None)
        two_sided(even, inv, fwd)
        make_chi(odd, second, first + 1 < live)
        two_sided(odd, inv, fwd)
        add_grads(even, first)
        return carry

    pairs = (live + 1) // 2
    lax.fori_loop(0, pairs, advance, 0)
    add_grads(odd, jnp.minimum(2 * pairs - 1, last_slot))


def frames_call(extended, zeros, probe_modes, amplitudes, positions, live_count, tables):
    fs = probe_modes.shape[-1]
    modes = probe_modes.shape[1]
    tiled = extended.shape
    vmem = pl.BlockSpec(memory_space=pltpu.VMEM)
    smem = pl.BlockSpec(memory_space=pltpu.SMEM)
    return pl.pallas_call(
        frames_kernel,
        out_shape=(
            jax.ShapeDtypeStruct(tiled, jnp.float32),
            jax.ShapeDtypeStruct((probe_modes.size // LANES, LANES), jnp.float32),
        ),
        in_specs=[smem, smem] + 7 * [vmem],
        out_specs=(vmem, vmem),
        input_output_aliases={7: 0, 8: 1},
        scratch_shapes=2
        * [
            pltpu.VMEM((2 * fs, modes * fs), jnp.bfloat16),
            pltpu.VMEM((modes * fs, 2 * fs), jnp.bfloat16),
            pltpu.VMEM((modes * fs, 2 * fs), jnp.float32),
            pltpu.VMEM((2, fs, fs), jnp.float32),
        ],
        compiler_params=pltpu.CompilerParams(vmem_limit_bytes=26 * 1024 * 1024),
        name="frames",
    )(live_count.reshape(1), positions, extended, probe_modes, amplitudes, *tables, *zeros)


def shards(object_field, probe_modes, measured_amp, scan_positions, frame_counts):
    slot_count = measured_amp.shape[2]
    extended, *zeros = halo_call(object_field, probe_modes.size)
    acc, probe_flat = frames_call(
        extended,
        zeros,
        probe_modes,
        measured_amp[0, 0],
        scan_positions[0, 0],
        frame_counts[0, 0],
        fourier_tables(probe_modes.shape[-1]),
    )
    norm_scale = 1.0 / math.sqrt(lax.axis_size("row") * lax.axis_size("col") * slot_count)
    return reduce_call(acc, probe_flat, object_field.shape, probe_modes.shape, norm_scale)


def solution(mesh):
    in_specs = (
        P(None, "row", "col"),
        P(),
        P("row", "col", None, None, None),
        P("row", "col", None, None),
        P("row", "col"),
    )
    out_specs = (P(None, "row", "col"), P())
    return jax.shard_map(shards, mesh=mesh, in_specs=in_specs, out_specs=out_specs, check_vma=False)
```

```python
import functools
import math

import jax
import jax.numpy as jnp
import numpy as np
from jax import lax
from jax.experimental import pallas as pl
from jax.experimental.pallas import tpu as pltpu
from jax.sharding import PartitionSpec as P

HALO = 128
LANES = 128
PARTS = 2
HALO_LIMIT = 20


MESH = pl.DeviceIdType.MESH
SIDES = [(dr, dc) for dr in (-1, 0, 1) for dc in (-1, 0, 1) if (dr, dc) != (0, 0)]


def position():
    return (
        lax.axis_index("row"),
        lax.axis_index("col"),
        lax.axis_size("row"),
        lax.axis_size("col"),
    )


def exists(side):
    row, col, rows, cols = position()
    dr, dc = side
    inside = jnp.bool_(True)
    if dr:
        inside = row + dr >= 0 if dr < 0 else row + dr < rows
    if dc:
        other = col + dc >= 0 if dc < 0 else col + dc < cols
        inside = jnp.logical_and(inside, other) if dr else other
    return inside


def at_side(side):
    row, col, _, _ = position()
    return (row + side[0], col + side[1])


def opposite(side):
    return (-side[0], -side[1])


def part(step, margin, inner):
    return {-1: slice(0, margin), 0: slice(margin, margin + inner), 1: slice(margin + inner, None)}[
        step
    ]


def edge(step, margin, inner):
    return {-1: slice(0, margin), 0: slice(0, inner), 1: slice(inner - margin, inner)}[step]


def to_side(side, index, source, landing, send_sems, recv_sems):
    return pltpu.make_async_remote_copy(
        src_ref=source,
        dst_ref=landing,
        send_sem=send_sems.at[index],
        recv_sem=recv_sems.at[index],
        device_id=at_side(side),
        device_id_type=MESH,
    )


DIRECT = 1


def halo_kernel(whole_ref, ext_ref, acc_ref, pacc_ref, *scratch):
    object_ref, load_sem, row_land, col_land, corner_land, relay_land = scratch[:6]
    row_sems, col_sems, corner_sems, relay_sems = scratch[6:]
    row, col, n_row, n_col = position()
    side_rows, side_cols = object_ref.shape[1:]
    load = pltpu.make_async_copy(whole_ref, object_ref, load_sem)
    load.start()
    steps = (-1, 1)
    pieces = (slice(0, HALO), slice(side_cols - HALO, side_cols), slice(HALO, side_cols - HALO))
    direct = DIRECT * side_rows // 4
    parts = (slice(0, direct), slice(direct, side_rows))

    def has(dr, dc):
        return exists((dr, dc))

    def turns(d):
        return jnp.logical_and(has(0, d), lax.rem(col, 4) == (3 if d > 0 else 0))

    def relays(d):
        other = col - 3 * d
        inside = jnp.logical_and(other >= 0, other < n_col)
        return jnp.logical_and(inside, lax.rem(col, 4) == (2 if d > 0 else 1))

    def lands_by_relay(d):
        return jnp.logical_and(has(0, -d), lax.rem(col, 4) == (0 if d > 0 else 3))

    links = []
    for d in steps:
        links.append((has(d, 0), (row + d, col)))
        links.append((has(0, d), (row, col + d)))
        links.append((turns(d), (row, col + 3 * d)))
        links.append((relays(d), (row, col - 3 * d)))
        links.append((relays(d), (row, col - 2 * d)))
        links.append((lands_by_relay(d), (row, col + 2 * d)))
    barrier = pltpu.get_barrier_semaphore()
    count = jnp.int32(0)
    for there, device in links:

        @pl.when(there)
        def _(device=device):
            pl.semaphore_signal(barrier, inc=1, device_id=device, device_id_type=MESH)

        count = count + there.astype(jnp.int32)
    pl.semaphore_wait(barrier, count)

    def remote(source, landing, sems, index, device):
        return pltpu.make_async_remote_copy(
            src_ref=source,
            dst_ref=landing,
            send_sem=sems.at[0, index],
            recv_sem=sems.at[1, index],
            device_id=device,
            device_id_type=MESH,
        )

    def row_copy(s, p):
        d = steps[s]
        source = whole_ref.at[:, edge(d, HALO, side_rows), pieces[p]]
        return remote(
            source, row_land.at[1 - s, :, :, pieces[p]], row_sems, 3 * s + p, (row + d, col)
        )

    def col_copy(s, p, to_relay=False):
        d = steps[s]
        source = whole_ref.at[:, parts[p], edge(d, HALO, side_cols)]
        if to_relay:
            return pltpu.make_async_remote_copy(
                src_ref=source,
                dst_ref=relay_land.at[s],
                send_sem=col_sems.at[0, 2 * s + p],
                recv_sem=relay_sems.at[1, s],
                device_id=(row, col + 3 * d),
                device_id_type=MESH,
            )
        return remote(
            source, col_land.at[1 - s, :, parts[p], :], col_sems, 2 * s + p, (row, col + d)
        )

    def relay_copy(s):
        d = steps[s]
        return pltpu.make_async_remote_copy(
            src_ref=relay_land.at[s],
            dst_ref=col_land.at[1 - s, :, parts[1], :],
            send_sem=relay_sems.at[0, s],
            recv_sem=col_sems.at[1, 2 * s + 1],
            device_id=(row, col - 2 * d),
            device_id_type=MESH,
        )

    def corner_copy(r, s):
        source = row_land.at[r, :, :, pieces[s]]
        return remote(
            source, corner_land.at[r, 1 - s], corner_sems, 2 * r + s, (row, col + steps[s])
        )

    def when(condition, action):
        @pl.when(condition)
        def _():
            action()

    for p in range(2):
        for s, d in enumerate(steps):
            when(has(d, 0), lambda s=s, p=p: row_copy(s, p).start())
    for p in (1, 0):
        for s, d in enumerate(steps):
            if p:
                when(turns(d), lambda s=s: col_copy(s, 1, True).start())
                straight = jnp.logical_and(has(0, d), jnp.logical_not(turns(d)))
                when(straight, lambda s=s: col_copy(s, 1).start())
            else:
                when(has(0, d), lambda s=s: col_copy(s, 0).start())
    for s, d in enumerate(steps):
        when(has(d, 0), lambda s=s: row_copy(s, 2).start())

    acc_ref[...] = jnp.zeros(acc_ref.shape, jnp.float32)
    pacc_ref[...] = jnp.zeros(pacc_ref.shape, jnp.float32)
    spare = ext_ref.shape[1] - 1
    ext_ref[:, spare] = jnp.zeros((2, ext_ref.shape[2], LANES), jnp.float32)
    margin, inner = HALO // LANES, side_cols // LANES

    def tiles_of(d):
        return range(spare)[part(d, margin, inner)]

    def fill(rows, tiles, height, source):
        for k, t in enumerate(tiles):
            if source is None:
                ext_ref[:, t, rows, :] = jnp.zeros((2, height, LANES), ext_ref.dtype)
            else:
                ext_ref[:, t, rows, :] = source[:, :, k * LANES : (k + 1) * LANES].astype(
                    jnp.float32
                )

    load.wait()
    fill(part(0, HALO, side_rows), tiles_of(0), side_rows, object_ref)

    for s, d in enumerate(steps):

        def pass_on(s=s):
            relay_copy_in = col_copy(s, 1, True)
            relay_copy_in.wait_recv()
            relay_copy(s).start()

        when(relays(d), pass_on)
    for r, dr in enumerate(steps):
        for s, dc in enumerate(steps):

            def hand_over(r=r, s=s, dc=dc):
                row_copy(1 - r, s).wait_recv()
                when(has(0, dc), lambda: corner_copy(r, s).start())

            when(has(dr, 0), hand_over)
    for s, d in enumerate(steps):
        rows = part(0, HALO, side_rows)
        here = s

        def take(s=s, d=d, rows=rows):
            col_copy(1 - s, 0).wait_recv()
            col_copy(1 - s, 1).wait_recv()
            fill(rows, tiles_of(d), side_rows, col_land.at[s])

        when(has(0, d), take)
        when(
            jnp.logical_not(has(0, d)), lambda d=d, rows=rows: fill(rows, tiles_of(d), side_rows, None)
        )
    for r, dr in enumerate(steps):
        rows = part(dr, HALO, side_rows)

        def take_rows(r=r, rows=rows):
            row_copy(1 - r, 2).wait_recv()
            fill(rows, tiles_of(0), HALO, row_land.at[r])

        when(has(dr, 0), take_rows)
        when(
            jnp.logical_not(has(dr, 0)), lambda rows=rows: fill(rows, tiles_of(0), HALO, None)
        )
    for r, dr in enumerate(steps):
        rows = part(dr, HALO, side_rows)
        for s, dc in enumerate(steps):

            def take_corner(r=r, s=s, dc=dc, rows=rows):
                corner_copy(r, 1 - s).wait_recv()
                fill(rows, tiles_of(dc), HALO, corner_land.at[r, s])

            when(has(dr, dc), take_corner)
            when(
                jnp.logical_not(has(dr, dc)),
                lambda dc=dc, rows=rows: fill(rows, tiles_of(dc), HALO, None),
            )

    for s, d in enumerate(steps):
        for p in range(3):
            when(has(d, 0), lambda s=s, p=p: row_copy(s, p).wait_send())
        for p in range(2):
            when(has(0, d), lambda s=s, p=p: col_copy(s, p).wait_send())
        when(relays(d), lambda s=s: relay_copy(s).wait_send())
        for r, dr in enumerate(steps):
            when(has(dr, d), lambda r=r, s=s: corner_copy(r, s).wait_send())


def halo_call(object_field, probe_size):
    planes, side_rows, side_cols = object_field.shape
    kind = object_field.dtype
    vmem = pl.BlockSpec(memory_space=pltpu.VMEM)
    tiled = jax.ShapeDtypeStruct(
        (planes, (side_cols + 2 * HALO) // LANES + 1, side_rows + 2 * HALO, LANES), jnp.float32
    )
    direct = DIRECT * side_rows // 4
    return pl.pallas_call(
        halo_kernel,
        out_shape=(
            tiled,
            tiled,
            jax.ShapeDtypeStruct((probe_size // LANES, LANES), jnp.float32),
        ),
        in_specs=[pl.BlockSpec(memory_space=pltpu.HBM)],
        out_specs=3 * (vmem,),
        scratch_shapes=[
            pltpu.VMEM(object_field.shape, kind),
            pltpu.SemaphoreType.DMA,
            pltpu.VMEM((2, planes, HALO, side_cols), kind),
            pltpu.VMEM((2, planes, side_rows, HALO), kind),
            pltpu.VMEM((2, 2, planes, HALO, HALO), kind),
            pltpu.VMEM((2, planes, side_rows - direct, HALO), kind),
            pltpu.SemaphoreType.DMA((2, 6)),
            pltpu.SemaphoreType.DMA((2, 4)),
            pltpu.SemaphoreType.DMA((2, 4)),
            pltpu.SemaphoreType.DMA((2, 2)),
        ],
        compiler_params=pltpu.CompilerParams(
            collective_id=0, has_side_effects=True, vmem_limit_bytes=HALO_LIMIT * 1024 * 1024
        ),
        cost_estimate=pl.CostEstimate(flops=10**10, bytes_accessed=0, transcendentals=0),
        name="halo",
    )(pltpu.with_memory_space_constraint(object_field, pltpu.HBM))


def reduce_kernel(scale, acc_ref, pacc_ref, grad_ref, full, *scratch):
    count = len(SIDES)
    sends, landings, rest = scratch[:count], scratch[count : 2 * count], scratch[2 * count :]
    psend, pair_recv, merged, precv, sums, zbuf = rest[:6]
    side_sems, pair_sems, col_sems, row_sems = rest[6:]
    row, col, n_row, n_col = position()
    side_rows, side_cols = grad_ref.shape[1:]
    margin = HALO // LANES
    inner = side_cols // LANES
    part_rows = psend.shape[2]
    share = PARTS * part_rows
    chip, core = col // 2, lax.rem(col, 2)
    n_chip = n_col // 2
    sibling = (row, 2 * chip + 1 - core)

    barrier = pltpu.get_barrier_semaphore()
    waits = jnp.int32(n_row + n_chip - 1)
    pl.semaphore_signal(barrier, inc=1, device_id=sibling, device_id_type=MESH)
    for k in range(1, n_chip):
        peer = (row, 2 * lax.rem(chip + k, n_chip) + core)
        pl.semaphore_signal(barrier, inc=1, device_id=peer, device_id_type=MESH)
    for k in range(1, n_row):
        pl.semaphore_signal(
            barrier, inc=1, device_id=(lax.rem(row + k, n_row), col), device_id_type=MESH
        )
    for side in SIDES:
        if side[1]:

            @pl.when(exists(side))
            def _(side=side):
                pl.semaphore_signal(barrier, inc=1, device_id=at_side(side), device_id_type=MESH)

            waits = waits + exists(side).astype(jnp.int32)

    def stage_side(index):
        dr, dc = SIDES[index]
        tiles = range(inner + 2 * margin)[part(dc, margin, inner)]
        for k, t in enumerate(tiles):
            sends[index][:, k] = acc_ref[:, t, part(dr, HALO, side_rows), :].astype(jnp.bfloat16)

    def stage_sides(chosen):
        for index, side in enumerate(SIDES):
            if chosen(side):
                stage_side(index)

    def to_peer(source, landing, sems, which, k, device):
        return pltpu.make_async_remote_copy(
            src_ref=source,
            dst_ref=landing,
            send_sem=sems.at[which, k],
            recv_sem=sems.at[which + 1, k],
            device_id=device,
            device_id_type=MESH,
        )

    def chip_at(k):
        return lax.rem(chip + k, n_chip)

    def chip_from(k):
        return lax.rem(chip + n_chip - k, n_chip)

    def chip_peer(k):
        return (row, 2 * chip_at(k) + core)

    def rows_of(index, h):
        return pl.ds(pl.multiple_of(index * share + h * part_rows, part_rows), part_rows)

    def pair_copy(h, k):
        return to_peer(
            psend.at[h, k], pair_recv.at[h, k], pair_sems, 0, h * n_chip + k, sibling
        )

    def scatter_copy(h, k):
        at = h * (n_chip - 1) + k - 1
        return to_peer(merged.at[h, k - 1], precv.at[h, k - 1], col_sems, 0, at, chip_peer(k))

    def row_copy(h, k, owner):
        at = h * (n_row - 1) + k - 1
        peer = (lax.rem(row + k, n_row), col)
        return to_peer(zbuf.at[h, row], zbuf.at[h, owner], row_sems, 0, at, peer)

    def gather_copy(h, k, owner):
        at = h * (n_chip - 1) + k - 1
        source, landing = full.at[rows_of(col, h), :], full.at[rows_of(owner, h), :]
        return to_peer(source, landing, col_sems, 2, at, chip_peer(k))

    def forward_copy(h, k, side):
        source = full.at[rows_of(2 * chip_from(k) + core, h), :]
        landing = full.at[rows_of(2 * chip_from(k) + side, h), :]
        return to_peer(source, landing, pair_sems, 2, h * n_chip + k, sibling)

    def side_copy(index):
        return to_side(
            SIDES[index], index, sends[index], landings[index], side_sems.at[0], side_sems.at[1]
        )

    def start_sides(chosen):
        for index, side in enumerate(SIDES):
            if chosen(side):

                @pl.when(exists(side))
                def _(index=index):
                    side_copy(index).start()

    def add_sides(chosen):
        for index, side in enumerate(SIDES):
            if not chosen(side):
                continue
            dr, dc = opposite(side)
            rows = edge(dr, HALO, side_rows)
            tiles = range(inner)[edge(dc, margin, inner)]

            @pl.when(exists((dr, dc)))
            def _(index=index, rows=rows, tiles=tiles):
                side_copy(index).wait_recv()
                for k, t in enumerate(tiles):
                    grad_ref[:, rows, t * LANES : (t + 1) * LANES] += landings[index][
                        :, k
                    ].astype(jnp.float32)

    over_rows = lambda side: side[1] == 0
    over_cols = lambda side: side[0] == 0
    corners = lambda side: side[0] != 0 and side[1] != 0
    order = list(range(1, n_chip)) + [0]
    for h in range(PARTS):
        for k in order:
            psend[h, k] = pacc_ref[rows_of(2 * chip_at(k) + 1 - core, h), :].astype(jnp.bfloat16)
    stage_sides(over_rows)
    pl.semaphore_wait(barrier, waits)
    for h in range(PARTS):
        for k in order:
            pair_copy(h, k).start()
    start_sides(over_rows)
    stage_sides(over_cols)
    stage_sides(corners)

    def merge(h, k):
        pair_copy(h, k).wait_recv()
        own = pacc_ref[rows_of(2 * chip_at(k) + core, h), :]
        return own + pair_recv[h, k].astype(jnp.float32)

    for h in range(PARTS):
        for k in range(1, n_chip):
            merged[h, k - 1] = merge(h, k).astype(jnp.bfloat16)
            scatter_copy(h, k).start()
        sums[h] = merge(h, 0)
    start_sides(over_cols)
    for t in range(inner):
        grad_ref[:, :, t * LANES : (t + 1) * LANES] = acc_ref[
            :, margin + t, HALO : HALO + side_rows, :
        ]
    for h in range(PARTS):
        total = sums[h]
        for k in range(1, n_chip):
            scatter_copy(h, k).wait_recv()
            total = total + precv[h, k - 1].astype(jnp.float32)
        zbuf[h, row] = total.astype(jnp.bfloat16)
        for k in range(1, n_row):
            row_copy(h, k, row).start()
    start_sides(corners)
    for h in range(PARTS):
        for k in range(1, n_row):
            row_copy(h, k, lax.rem(row + n_row - k, n_row)).wait_recv()
        total = zbuf[h, 0].astype(jnp.float32)
        for k in range(1, n_row):
            total = total + zbuf[h, k].astype(jnp.float32)
        full[rows_of(col, h), :] = (total * scale).astype(jnp.bfloat16)
        for k in range(1, n_chip):
            gather_copy(h, k, col).start()
        forward_copy(h, 0, core).start()
    add_sides(over_rows)
    add_sides(over_cols)
    for h in range(PARTS):
        for k in range(1, n_chip):
            gather_copy(h, k, 2 * chip_from(k) + core).wait_recv()
            forward_copy(h, k, core).start()
    add_sides(corners)

    for h in range(PARTS):
        for k in range(n_chip):
            forward_copy(h, k, 1 - core).wait_recv()
    for h in range(PARTS):
        for k in range(1, n_chip):
            scatter_copy(h, k).wait_send()
            gather_copy(h, k, col).wait_send()
        for k in range(n_chip):
            pair_copy(h, k).wait_send()
            forward_copy(h, k, core).wait_send()
        for k in range(1, n_row):
            row_copy(h, k, row).wait_send()
    for index, side in enumerate(SIDES):

        @pl.when(exists(side))
        def _(index=index):
            side_copy(index).wait_send()


def reduce_call(acc, probe_flat, object_shape, scale):
    n_row, n_col = lax.axis_size("row"), lax.axis_size("col")
    _, side_rows, side_cols = object_shape
    inner = side_cols // LANES
    margin = HALO // LANES
    vmem = pl.BlockSpec(memory_space=pltpu.VMEM)
    buffers = []
    for dr, dc in SIDES:
        buffers.append(
            pltpu.VMEM(
                (2, margin if dc else inner, HALO if dr else side_rows, LANES), jnp.bfloat16
            )
        )
    total_rows = probe_flat.shape[0]
    piece = total_rows // n_col // PARTS
    n_chip = n_col // 2
    return pl.pallas_call(
        functools.partial(reduce_kernel, scale),
        out_shape=(
            jax.ShapeDtypeStruct(object_shape, jnp.float32),
            jax.ShapeDtypeStruct(probe_flat.shape, jnp.bfloat16),
        ),
        in_specs=[vmem, vmem],
        out_specs=(vmem, vmem),
        scratch_shapes=buffers
        + buffers
        + [
            pltpu.VMEM((PARTS, n_chip, piece, LANES), jnp.bfloat16),
            pltpu.VMEM((PARTS, n_chip, piece, LANES), jnp.bfloat16),
            pltpu.VMEM((PARTS, n_chip - 1, piece, LANES), jnp.bfloat16),
            pltpu.VMEM((PARTS, n_chip - 1, piece, LANES), jnp.bfloat16),
            pltpu.VMEM((PARTS, piece, LANES), jnp.float32),
            pltpu.VMEM((PARTS, n_row, piece, LANES), jnp.bfloat16),
            pltpu.SemaphoreType.DMA((2, len(SIDES))),
            pltpu.SemaphoreType.DMA((4, PARTS * n_chip)),
            pltpu.SemaphoreType.DMA((4, PARTS * (n_chip - 1))),
            pltpu.SemaphoreType.DMA((2, PARTS * (n_row - 1))),
        ],
        compiler_params=pltpu.CompilerParams(
            collective_id=1, has_side_effects=True, vmem_limit_bytes=20 * 1024 * 1024
        ),
        name="reduce",
    )(acc, probe_flat)


def write_kernel(grad_in, flat_ref, grad_ref, probe_ref, probe_out, sems):
    grad_copy = pltpu.make_async_copy(grad_in, grad_ref, sems.at[0])
    grad_copy.start()
    parts, modes, fs, width = probe_out.shape
    copies = []
    at = 0
    for p in range(parts):
        for m in range(modes):
            for t in range(width // LANES):
                probe_out[p, m, :, t * LANES : (t + 1) * LANES] = flat_ref[at : at + fs, :].astype(
                    jnp.float32
                )
                at += fs
            copies.append(
                pltpu.make_async_copy(
                    probe_out.at[p, m], probe_ref.at[p, m], sems.at[1 + p * modes + m]
                )
            )
            copies[-1].start()
    for copy in copies:
        copy.wait()
    grad_copy.wait()


def write_call(grad, probe_flat, probe_shape):
    vmem = pl.BlockSpec(memory_space=pltpu.VMEM)
    hbm = pl.BlockSpec(memory_space=pltpu.HBM)
    return pl.pallas_call(
        write_kernel,
        out_shape=(
            jax.ShapeDtypeStruct(grad.shape, grad.dtype),
            jax.ShapeDtypeStruct(probe_shape, jnp.float32),
        ),
        in_specs=[vmem, vmem],
        out_specs=(hbm, hbm),
        scratch_shapes=[
            pltpu.VMEM(probe_shape, jnp.float32),
            pltpu.SemaphoreType.DMA((1 + probe_shape[0] * probe_shape[1],)),
        ],
        compiler_params=pltpu.CompilerParams(vmem_limit_bytes=8 * 1024 * 1024),
        name="write",
    )(grad, probe_flat)


def fourier_tables(frame_side):
    indices = np.arange(frame_side)
    product = indices[:, None] * indices[None, :] % frame_side
    angles = 2.0 * math.pi / frame_side * product
    norm_scale = 1.0 / math.sqrt(frame_side)
    real, imag = np.cos(angles) * norm_scale, -np.sin(angles) * norm_scale
    tables = (np.block([[real, -imag], [imag, real]]), np.block([[real, imag], [-imag, real]]))
    return tuple(jnp.asarray(table.astype(np.float32)).astype(jnp.bfloat16) for table in tables)


CHUNK = 32


def dot32(left, right):
    return jnp.dot(left, right, preferred_element_type=jnp.float32)


def frames_kernel(
    count_ref, at_ref, ext_ref, probe_ref, amp_ref, fwd, inv, zero_ref, pzero_ref,
    acc_ref, pacc_ref, *buffers,
):
    fs = probe_ref.shape[-1]
    modes = probe_ref.shape[1]
    lane_tiles = fs // LANES
    last_slot = amp_ref.shape[0] - 1
    live = count_ref[0, 0]
    even, odd = buffers[:4], buffers[4:]
    odd[2][...] = jnp.zeros(odd[2].shape, jnp.float32)
    odd[3][...] = jnp.zeros(odd[3].shape, jnp.float32)

    def two_sided(buffer, left_table, right_table):
        stage, half, wide, _ = buffer
        for m in range(modes):
            both = dot32(left_table[...], stage[:, m * fs : (m + 1) * fs])
            half[m * fs : (m + 1) * fs, :fs] = both[:fs].astype(jnp.bfloat16)
            half[m * fs : (m + 1) * fs, fs:] = both[fs:].astype(jnp.bfloat16)
        wide[...] = dot32(half[...], right_table[...])

    def make_exit(buffer, slot):
        stage, _, _, patch = buffer
        row_at = at_ref[0, slot]
        col_at = at_ref[1, slot]
        tile_at = col_at // LANES
        shift = col_at % LANES
        back_shift = (LANES - shift) % LANES
        lane = lax.broadcasted_iota(jnp.int32, (CHUNK, LANES), 1)
        keep_low = lane < LANES - shift
        for r in range(0, fs, CHUNK):
            rows = slice(r, r + CHUNK)
            values = []
            for plane in range(2):
                rolled = [
                    pltpu.roll(
                        ext_ref[plane, tile_at + t, pl.ds(row_at + r, CHUNK), :], back_shift, 1
                    )
                    for t in range(lane_tiles + 1)
                ]
                values.append(
                    [jnp.where(keep_low, rolled[t], rolled[t + 1]) for t in range(lane_tiles)]
                )
            for t in range(lane_tiles):
                cols = slice(t * LANES, (t + 1) * LANES)
                patch_real, patch_imag = values[0][t], values[1][t]
                patch[0, rows, cols] = patch_real
                patch[1, rows, cols] = patch_imag
                for m in range(modes):
                    probe_real = probe_ref[0, m, rows, cols]
                    probe_imag = probe_ref[1, m, rows, cols]
                    out = slice(m * fs + t * LANES, m * fs + (t + 1) * LANES)
                    stage[rows, out] = (
                        probe_real * patch_real - probe_imag * patch_imag
                    ).astype(jnp.bfloat16)
                    stage[fs + r : fs + r + CHUNK, out] = (
                        probe_real * patch_imag + probe_imag * patch_real
                    ).astype(jnp.bfloat16)

    def make_chi(buffer, slot, valid):
        stage, _, wide, _ = buffer
        for r in range(0, fs, CHUNK):
            for t in range(lane_tiles):
                cols = slice(t * LANES, (t + 1) * LANES)
                imag_cols = slice(fs + t * LANES, fs + (t + 1) * LANES)
                psi = []
                power = None
                for m in range(modes):
                    rows = slice(m * fs + r, m * fs + r + CHUNK)
                    real, imag = wide[rows, cols], wide[rows, imag_cols]
                    psi.append((real, imag))
                    own = real * real + imag * imag
                    power = own if power is None else power + own
                amp = amp_ref[slot, r : r + CHUNK, cols].astype(jnp.float32)
                factor = 1.0 - amp * lax.rsqrt(jnp.maximum(power, 0.25))
                if valid is not None:
                    factor = jnp.where(valid, factor, 0.0)
                for m in range(modes):
                    out = slice(m * fs + t * LANES, m * fs + (t + 1) * LANES)
                    stage[r : r + CHUNK, out] = (psi[m][0] * factor).astype(jnp.bfloat16)
                    stage[fs + r : fs + r + CHUNK, out] = (psi[m][1] * factor).astype(jnp.bfloat16)

    def add_grads(buffer, slot):
        _, _, wide, patch = buffer
        row_at = at_ref[0, slot]
        col_at = at_ref[1, slot]
        tile_at = col_at // LANES
        shift = col_at % LANES
        lane = lax.broadcasted_iota(jnp.int32, (CHUNK, LANES), 1)
        from_same = lane >= shift
        for r in range(0, fs, CHUNK):
            grads = [[], []]
            for t in range(lane_tiles):
                cols = slice(t * LANES, (t + 1) * LANES)
                imag_cols = slice(fs + t * LANES, fs + (t + 1) * LANES)
                patch_real = patch[0, r : r + CHUNK, cols]
                patch_imag = patch[1, r : r + CHUNK, cols]
                total_real = total_imag = None
                for m in range(modes):
                    rows = slice(m * fs + r, m * fs + r + CHUNK)
                    real, imag = wide[rows, cols], wide[rows, imag_cols]
                    probe_real = probe_ref[0, m, r : r + CHUNK, cols]
                    probe_imag = probe_ref[1, m, r : r + CHUNK, cols]
                    own_real = probe_real * real + probe_imag * imag
                    own_imag = probe_real * imag - probe_imag * real
                    total_real = own_real if m == 0 else total_real + own_real
                    total_imag = own_imag if m == 0 else total_imag + own_imag
                    at = (m * lane_tiles + t) * fs + r
                    pacc_ref[at : at + CHUNK, :] += patch_real * real + patch_imag * imag
                    at += modes * lane_tiles * fs
                    pacc_ref[at : at + CHUNK, :] += patch_real * imag - patch_imag * real
                grads[0].append(pltpu.roll(total_real, shift, 1))
                grads[1].append(pltpu.roll(total_imag, shift, 1))
            for plane in range(2):
                rolled = grads[plane]
                for t in range(lane_tiles + 1):
                    same = rolled[t] if t < lane_tiles else 0.0
                    before = rolled[t - 1] if t > 0 else 0.0
                    where = (plane, tile_at + t, pl.ds(row_at + r, CHUNK), slice(None))
                    acc_ref[where] += jnp.where(from_same, same, before)

    def advance(pair, carry):
        first = 2 * pair
        second = jnp.minimum(first + 1, last_slot)
        make_exit(even, first)
        two_sided(even, fwd, inv)
        add_grads(odd, jnp.maximum(first - 1, 0))
        make_exit(odd, second)
        two_sided(odd, fwd, inv)
        make_chi(even, first, None)
        two_sided(even, inv, fwd)
        make_chi(odd, second, first + 1 < live)
        two_sided(odd, inv, fwd)
        add_grads(even, first)
        return carry

    pairs = (live + 1) // 2
    lax.fori_loop(0, pairs, advance, 0)
    add_grads(odd, jnp.minimum(2 * pairs - 1, last_slot))


def frames_call(extended, zeros, probe_modes, amplitudes, positions, live_count, tables):
    fs = probe_modes.shape[-1]
    modes = probe_modes.shape[1]
    tiled = extended.shape
    vmem = pl.BlockSpec(memory_space=pltpu.VMEM)
    smem = pl.BlockSpec(memory_space=pltpu.SMEM)
    return pl.pallas_call(
        frames_kernel,
        out_shape=(
            jax.ShapeDtypeStruct(tiled, jnp.float32),
            jax.ShapeDtypeStruct((probe_modes.size // LANES, LANES), jnp.float32),
        ),
        in_specs=[smem, smem] + 7 * [vmem],
        out_specs=(vmem, vmem),
        input_output_aliases={7: 0, 8: 1},
        scratch_shapes=2
        * [
            pltpu.VMEM((2 * fs, modes * fs), jnp.bfloat16),
            pltpu.VMEM((modes * fs, 2 * fs), jnp.bfloat16),
            pltpu.VMEM((modes * fs, 2 * fs), jnp.float32),
            pltpu.VMEM((2, fs, fs), jnp.float32),
        ],
        compiler_params=pltpu.CompilerParams(vmem_limit_bytes=26 * 1024 * 1024),
        name="frames",
    )(live_count, positions, extended, probe_modes, amplitudes, *tables, *zeros)


def shards(object_field, probe_modes, measured_amp, scan_positions, frame_counts):
    slot_count = measured_amp.shape[2]
    extended, *zeros = halo_call(object_field, probe_modes.size)
    acc, probe_flat = frames_call(
        extended,
        zeros,
        probe_modes,
        measured_amp[0, 0],
        scan_positions[0, 0],
        frame_counts,
        fourier_tables(probe_modes.shape[-1]),
    )
    norm_scale = 1.0 / math.sqrt(lax.axis_size("row") * lax.axis_size("col") * slot_count)
    grad, probe_sum = reduce_call(acc, probe_flat, object_field.shape, norm_scale)
    return write_call(grad, probe_sum, probe_modes.shape)


def solution(mesh):
    in_specs = (
        P(None, "row", "col"),
        P(),
        P("row", "col", None, None, None),
        P("row", "col", None, None),
        P("row", "col"),
    )
    out_specs = (P(None, "row", "col"), P())
    return jax.shard_map(shards, mesh=mesh, in_specs=in_specs, out_specs=out_specs, check_vma=False)
```

```python
import functools
import math

import jax
import jax.numpy as jnp
import numpy as np
from jax import lax
from jax.experimental import pallas as pl
from jax.experimental.pallas import tpu as pltpu
from jax.sharding import PartitionSpec as P

HALO = 128
LANES = 128
PARTS = 2
HALO_LIMIT = 20


MESH = pl.DeviceIdType.MESH
SIDES = [(dr, dc) for dr in (-1, 0, 1) for dc in (-1, 0, 1) if (dr, dc) != (0, 0)]


def position():
    return (
        lax.axis_index("row"),
        lax.axis_index("col"),
        lax.axis_size("row"),
        lax.axis_size("col"),
    )


def exists(side):
    row, col, rows, cols = position()
    dr, dc = side
    inside = jnp.bool_(True)
    if dr:
        inside = row + dr >= 0 if dr < 0 else row + dr < rows
    if dc:
        other = col + dc >= 0 if dc < 0 else col + dc < cols
        inside = jnp.logical_and(inside, other) if dr else other
    return inside


def at_side(side):
    row, col, _, _ = position()
    return (row + side[0], col + side[1])


def opposite(side):
    return (-side[0], -side[1])


def part(step, margin, inner):
    return {-1: slice(0, margin), 0: slice(margin, margin + inner), 1: slice(margin + inner, None)}[
        step
    ]


def edge(step, margin, inner):
    return {-1: slice(0, margin), 0: slice(0, inner), 1: slice(inner - margin, inner)}[step]


def to_side(side, index, source, landing, send_sems, recv_sems):
    return pltpu.make_async_remote_copy(
        src_ref=source,
        dst_ref=landing,
        send_sem=send_sems.at[index],
        recv_sem=recv_sems.at[index],
        device_id=at_side(side),
        device_id_type=MESH,
    )


DIRECT = 1


def halo_kernel(whole_ref, ext_ref, acc_ref, pacc_ref, *scratch):
    object_ref, load_sem, row_land, col_land, corner_land, relay_land = scratch[:6]
    row_sems, col_sems, corner_sems, relay_sems = scratch[6:]
    row, col, n_row, n_col = position()
    side_rows, side_cols = object_ref.shape[1:]
    load = pltpu.make_async_copy(whole_ref, object_ref, load_sem)
    load.start()
    steps = (-1, 1)
    pieces = (slice(0, HALO), slice(side_cols - HALO, side_cols), slice(HALO, side_cols - HALO))
    direct = DIRECT * side_rows // 4
    parts = (slice(0, direct), slice(direct, side_rows))

    def has(dr, dc):
        return exists((dr, dc))

    def turns(d):
        return jnp.logical_and(has(0, d), lax.rem(col, 4) == (3 if d > 0 else 0))

    def relays(d):
        other = col - 3 * d
        inside = jnp.logical_and(other >= 0, other < n_col)
        return jnp.logical_and(inside, lax.rem(col, 4) == (2 if d > 0 else 1))

    def lands_by_relay(d):
        return jnp.logical_and(has(0, -d), lax.rem(col, 4) == (0 if d > 0 else 3))

    links = []
    for d in steps:
        links.append((has(d, 0), (row + d, col)))
        links.append((has(0, d), (row, col + d)))
        links.append((turns(d), (row, col + 3 * d)))
        links.append((relays(d), (row, col - 3 * d)))
        links.append((relays(d), (row, col - 2 * d)))
        links.append((lands_by_relay(d), (row, col + 2 * d)))
    barrier = pltpu.get_barrier_semaphore()
    count = jnp.int32(0)
    for there, device in links:

        @pl.when(there)
        def _(device=device):
            pl.semaphore_signal(barrier, inc=1, device_id=device, device_id_type=MESH)

        count = count + there.astype(jnp.int32)
    pl.semaphore_wait(barrier, count)

    def remote(source, landing, sems, index, device):
        return pltpu.make_async_remote_copy(
            src_ref=source,
            dst_ref=landing,
            send_sem=sems.at[0, index],
            recv_sem=sems.at[1, index],
            device_id=device,
            device_id_type=MESH,
        )

    def row_copy(s, p):
        d = steps[s]
        source = whole_ref.at[:, edge(d, HALO, side_rows), pieces[p]]
        return remote(
            source, row_land.at[1 - s, :, :, pieces[p]], row_sems, 3 * s + p, (row + d, col)
        )

    def col_copy(s, p, to_relay=False):
        d = steps[s]
        source = whole_ref.at[:, parts[p], edge(d, HALO, side_cols)]
        if to_relay:
            return pltpu.make_async_remote_copy(
                src_ref=source,
                dst_ref=relay_land.at[s],
                send_sem=col_sems.at[0, 2 * s + p],
                recv_sem=relay_sems.at[1, s],
                device_id=(row, col + 3 * d),
                device_id_type=MESH,
            )
        return remote(
            source, col_land.at[1 - s, :, parts[p], :], col_sems, 2 * s + p, (row, col + d)
        )

    def relay_copy(s):
        d = steps[s]
        return pltpu.make_async_remote_copy(
            src_ref=relay_land.at[s],
            dst_ref=col_land.at[1 - s, :, parts[1], :],
            send_sem=relay_sems.at[0, s],
            recv_sem=col_sems.at[1, 2 * s + 1],
            device_id=(row, col - 2 * d),
            device_id_type=MESH,
        )

    def corner_copy(r, s):
        source = row_land.at[r, :, :, pieces[s]]
        return remote(
            source, corner_land.at[r, 1 - s], corner_sems, 2 * r + s, (row, col + steps[s])
        )

    def when(condition, action):
        @pl.when(condition)
        def _():
            action()

    for p in range(2):
        for s, d in enumerate(steps):
            when(has(d, 0), lambda s=s, p=p: row_copy(s, p).start())
    for p in (1, 0):
        for s, d in enumerate(steps):
            if p:
                when(turns(d), lambda s=s: col_copy(s, 1, True).start())
                straight = jnp.logical_and(has(0, d), jnp.logical_not(turns(d)))
                when(straight, lambda s=s: col_copy(s, 1).start())
            else:
                when(has(0, d), lambda s=s: col_copy(s, 0).start())
    for s, d in enumerate(steps):
        when(has(d, 0), lambda s=s: row_copy(s, 2).start())

    acc_ref[...] = jnp.zeros(acc_ref.shape, jnp.float32)
    pacc_ref[...] = jnp.zeros(pacc_ref.shape, jnp.float32)
    spare = ext_ref.shape[1] - 1
    ext_ref[:, spare] = jnp.zeros((2, ext_ref.shape[2], LANES), jnp.float32)
    margin, inner = HALO // LANES, side_cols // LANES

    def tiles_of(d):
        return range(spare)[part(d, margin, inner)]

    def fill(rows, tiles, height, source):
        for k, t in enumerate(tiles):
            if source is None:
                ext_ref[:, t, rows, :] = jnp.zeros((2, height, LANES), ext_ref.dtype)
            else:
                ext_ref[:, t, rows, :] = source[:, :, k * LANES : (k + 1) * LANES].astype(
                    jnp.float32
                )

    load.wait()
    fill(part(0, HALO, side_rows), tiles_of(0), side_rows, object_ref)

    for s, d in enumerate(steps):

        def pass_on(s=s):
            relay_copy_in = col_copy(s, 1, True)
            relay_copy_in.wait_recv()
            relay_copy(s).start()

        when(relays(d), pass_on)
    for r, dr in enumerate(steps):
        for s, dc in enumerate(steps):

            def hand_over(r=r, s=s, dc=dc):
                row_copy(1 - r, s).wait_recv()
                when(has(0, dc), lambda: corner_copy(r, s).start())

            when(has(dr, 0), hand_over)
    for s, d in enumerate(steps):
        rows = part(0, HALO, side_rows)
        here = s

        def take(s=s, d=d, rows=rows):
            col_copy(1 - s, 0).wait_recv()
            col_copy(1 - s, 1).wait_recv()
            fill(rows, tiles_of(d), side_rows, col_land.at[s])

        when(has(0, d), take)
        when(
            jnp.logical_not(has(0, d)), lambda d=d, rows=rows: fill(rows, tiles_of(d), side_rows, None)
        )
    for r, dr in enumerate(steps):
        rows = part(dr, HALO, side_rows)

        def take_rows(r=r, rows=rows):
            row_copy(1 - r, 2).wait_recv()
            fill(rows, tiles_of(0), HALO, row_land.at[r])

        when(has(dr, 0), take_rows)
        when(
            jnp.logical_not(has(dr, 0)), lambda rows=rows: fill(rows, tiles_of(0), HALO, None)
        )
    for r, dr in enumerate(steps):
        rows = part(dr, HALO, side_rows)
        for s, dc in enumerate(steps):

            def take_corner(r=r, s=s, dc=dc, rows=rows):
                corner_copy(r, 1 - s).wait_recv()
                fill(rows, tiles_of(dc), HALO, corner_land.at[r, s])

            when(has(dr, dc), take_corner)
            when(
                jnp.logical_not(has(dr, dc)),
                lambda dc=dc, rows=rows: fill(rows, tiles_of(dc), HALO, None),
            )

    for s, d in enumerate(steps):
        for p in range(3):
            when(has(d, 0), lambda s=s, p=p: row_copy(s, p).wait_send())
        for p in range(2):
            when(has(0, d), lambda s=s, p=p: col_copy(s, p).wait_send())
        when(relays(d), lambda s=s: relay_copy(s).wait_send())
        for r, dr in enumerate(steps):
            when(has(dr, d), lambda r=r, s=s: corner_copy(r, s).wait_send())


def halo_call(object_field, probe_size):
    planes, side_rows, side_cols = object_field.shape
    kind = object_field.dtype
    vmem = pl.BlockSpec(memory_space=pltpu.VMEM)
    tiled = jax.ShapeDtypeStruct(
        (planes, (side_cols + 2 * HALO) // LANES + 1, side_rows + 2 * HALO, LANES), jnp.float32
    )
    direct = DIRECT * side_rows // 4
    return pl.pallas_call(
        halo_kernel,
        out_shape=(
            tiled,
            tiled,
            jax.ShapeDtypeStruct((probe_size // LANES, LANES), jnp.float32),
        ),
        in_specs=[pl.BlockSpec(memory_space=pltpu.HBM)],
        out_specs=3 * (vmem,),
        scratch_shapes=[
            pltpu.VMEM(object_field.shape, kind),
            pltpu.SemaphoreType.DMA,
            pltpu.VMEM((2, planes, HALO, side_cols), kind),
            pltpu.VMEM((2, planes, side_rows, HALO), kind),
            pltpu.VMEM((2, 2, planes, HALO, HALO), kind),
            pltpu.VMEM((2, planes, side_rows - direct, HALO), kind),
            pltpu.SemaphoreType.DMA((2, 6)),
            pltpu.SemaphoreType.DMA((2, 4)),
            pltpu.SemaphoreType.DMA((2, 4)),
            pltpu.SemaphoreType.DMA((2, 2)),
        ],
        compiler_params=pltpu.CompilerParams(
            collective_id=0, has_side_effects=True, vmem_limit_bytes=HALO_LIMIT * 1024 * 1024
        ),
        cost_estimate=pl.CostEstimate(flops=10**10, bytes_accessed=0, transcendentals=0),
        name="halo",
    )(pltpu.with_memory_space_constraint(object_field, pltpu.HBM))


def reduce_kernel(scale, acc_ref, pacc_ref, grad_ref, full, *scratch):
    count = len(SIDES)
    sends, landings, rest = scratch[:count], scratch[count : 2 * count], scratch[2 * count :]
    psend, pair_recv, merged, precv, sums, zbuf = rest[:6]
    side_sems, pair_sems, col_sems, row_sems = rest[6:]
    row, col, n_row, n_col = position()
    side_rows, side_cols = grad_ref.shape[1:]
    margin = HALO // LANES
    inner = side_cols // LANES
    part_rows = psend.shape[2]
    share = PARTS * part_rows
    chip, core = col // 2, lax.rem(col, 2)
    n_chip = n_col // 2
    sibling = (row, 2 * chip + 1 - core)

    barrier = pltpu.get_barrier_semaphore()
    levels = n_row.bit_length() - 1
    assert n_row == 2**levels
    waits = jnp.int32(levels + n_chip)
    pl.semaphore_signal(barrier, inc=1, device_id=sibling, device_id_type=MESH)
    for k in range(1, n_chip):
        peer = (row, 2 * lax.rem(chip + k, n_chip) + core)
        pl.semaphore_signal(barrier, inc=1, device_id=peer, device_id_type=MESH)
    for k in range(levels):
        size = 2**k
        peer = (row + size - 2 * size * lax.rem(row // size, 2), col)
        pl.semaphore_signal(barrier, inc=1, device_id=peer, device_id_type=MESH)
    for side in SIDES:

        @pl.when(exists(side))
        def _(side=side):
            pl.semaphore_signal(barrier, inc=1, device_id=at_side(side), device_id_type=MESH)

        waits = waits + exists(side).astype(jnp.int32)

    def stage_side(index):
        dr, dc = SIDES[index]
        tiles = range(inner + 2 * margin)[part(dc, margin, inner)]
        for k, t in enumerate(tiles):
            sends[index][:, k] = acc_ref[:, t, part(dr, HALO, side_rows), :].astype(jnp.bfloat16)

    def stage_sides(chosen):
        for index, side in enumerate(SIDES):
            if chosen(side):
                stage_side(index)

    def to_peer(source, landing, sems, which, k, device):
        return pltpu.make_async_remote_copy(
            src_ref=source,
            dst_ref=landing,
            send_sem=sems.at[which, k],
            recv_sem=sems.at[which + 1, k],
            device_id=device,
            device_id_type=MESH,
        )

    def chip_at(k):
        return lax.rem(chip + k, n_chip)

    def chip_from(k):
        return lax.rem(chip + n_chip - k, n_chip)

    def chip_peer(k):
        return (row, 2 * chip_at(k) + core)

    def rows_of(index, h):
        return pl.ds(pl.multiple_of(index * share + h * part_rows, part_rows), part_rows)

    def pair_copy(h, k):
        return to_peer(
            psend.at[h, k], pair_recv.at[h, k], pair_sems, 0, h * n_chip + k, sibling
        )

    def scatter_copy(h, k):
        at = h * (n_chip - 1) + k - 1
        return to_peer(merged.at[h, k - 1], precv.at[h, k - 1], col_sems, 0, at, chip_peer(k))

    def row_peer(k):
        size = 2**k
        return row + size - 2 * size * lax.rem(row // size, 2)

    def row_copy(h, k):
        source, landing = zbuf.at[h, 2 * k], zbuf.at[h, 2 * k + 1]
        return to_peer(source, landing, row_sems, 0, h * levels + k, (row_peer(k), col))

    def gather_copy(h, k, owner):
        at = h * (n_chip - 1) + k - 1
        source, landing = full.at[rows_of(col, h), :], full.at[rows_of(owner, h), :]
        return to_peer(source, landing, col_sems, 2, at, chip_peer(k))

    def forward_copy(h, k, side):
        source = full.at[rows_of(2 * chip_from(k) + core, h), :]
        landing = full.at[rows_of(2 * chip_from(k) + side, h), :]
        return to_peer(source, landing, pair_sems, 2, h * n_chip + k, sibling)

    def side_copy(index):
        return to_side(
            SIDES[index], index, sends[index], landings[index], side_sems.at[0], side_sems.at[1]
        )

    def start_sides(chosen):
        for index, side in enumerate(SIDES):
            if chosen(side):

                @pl.when(exists(side))
                def _(index=index):
                    side_copy(index).start()

    def add_sides(chosen):
        for index, side in enumerate(SIDES):
            if not chosen(side):
                continue
            dr, dc = opposite(side)
            rows = edge(dr, HALO, side_rows)
            tiles = range(inner)[edge(dc, margin, inner)]

            @pl.when(exists((dr, dc)))
            def _(index=index, rows=rows, tiles=tiles):
                side_copy(index).wait_recv()
                for k, t in enumerate(tiles):
                    grad_ref[:, rows, t * LANES : (t + 1) * LANES] += landings[index][
                        :, k
                    ].astype(jnp.float32)

    over_rows = lambda side: side[1] == 0
    over_cols = lambda side: side[0] == 0
    corners = lambda side: side[0] != 0 and side[1] != 0
    order = list(range(1, n_chip)) + [0]
    for h in range(PARTS):
        for k in order:
            psend[h, k] = pacc_ref[rows_of(2 * chip_at(k) + 1 - core, h), :].astype(jnp.bfloat16)
    stage_sides(over_rows)
    pl.semaphore_wait(barrier, waits)
    for h in range(PARTS):
        for k in order:
            pair_copy(h, k).start()
    start_sides(over_rows)
    stage_sides(over_cols)
    stage_sides(corners)

    def merge(h, k):
        pair_copy(h, k).wait_recv()
        own = pacc_ref[rows_of(2 * chip_at(k) + core, h), :]
        return own + pair_recv[h, k].astype(jnp.float32)

    for h in range(PARTS):
        for k in range(1, n_chip):
            merged[h, k - 1] = merge(h, k).astype(jnp.bfloat16)
            scatter_copy(h, k).start()
        sums[h] = merge(h, 0)
    start_sides(over_cols)
    for t in range(inner):
        grad_ref[:, :, t * LANES : (t + 1) * LANES] = acc_ref[
            :, margin + t, HALO : HALO + side_rows, :
        ]
    for h in range(PARTS):
        total = sums[h]
        for k in range(1, n_chip):
            scatter_copy(h, k).wait_recv()
            total = total + precv[h, k - 1].astype(jnp.float32)
        zbuf[h, 0] = total.astype(jnp.bfloat16)
        row_copy(h, 0).start()
    for k in range(levels):
        for h in range(PARTS):
            row_copy(h, k).wait_recv()
            total = zbuf[h, 2 * k].astype(jnp.float32) + zbuf[h, 2 * k + 1].astype(jnp.float32)
            if k + 1 < levels:
                zbuf[h, 2 * k + 2] = total.astype(jnp.bfloat16)
                row_copy(h, k + 1).start()
                continue
            full[rows_of(col, h), :] = (total * scale).astype(jnp.bfloat16)
            for peer in range(1, n_chip):
                gather_copy(h, peer, col).start()
            forward_copy(h, 0, core).start()
    start_sides(corners)
    add_sides(over_rows)
    add_sides(over_cols)
    for h in range(PARTS):
        for k in range(1, n_chip):
            gather_copy(h, k, 2 * chip_from(k) + core).wait_recv()
            forward_copy(h, k, core).start()
    add_sides(corners)

    for h in range(PARTS):
        for k in range(n_chip):
            forward_copy(h, k, 1 - core).wait_recv()
    for h in range(PARTS):
        for k in range(1, n_chip):
            scatter_copy(h, k).wait_send()
            gather_copy(h, k, col).wait_send()
        for k in range(n_chip):
            pair_copy(h, k).wait_send()
            forward_copy(h, k, core).wait_send()
        for k in range(levels):
            row_copy(h, k).wait_send()
    for index, side in enumerate(SIDES):

        @pl.when(exists(side))
        def _(index=index):
            side_copy(index).wait_send()


def reduce_call(acc, probe_flat, object_shape, scale):
    n_row, n_col = lax.axis_size("row"), lax.axis_size("col")
    _, side_rows, side_cols = object_shape
    inner = side_cols // LANES
    margin = HALO // LANES
    vmem = pl.BlockSpec(memory_space=pltpu.VMEM)
    buffers = []
    for dr, dc in SIDES:
        buffers.append(
            pltpu.VMEM(
                (2, margin if dc else inner, HALO if dr else side_rows, LANES), jnp.bfloat16
            )
        )
    total_rows = probe_flat.shape[0]
    piece = total_rows // n_col // PARTS
    n_chip = n_col // 2
    levels = n_row.bit_length() - 1
    return pl.pallas_call(
        functools.partial(reduce_kernel, scale),
        out_shape=(
            jax.ShapeDtypeStruct(object_shape, jnp.float32),
            jax.ShapeDtypeStruct(probe_flat.shape, jnp.bfloat16),
        ),
        in_specs=[vmem, vmem],
        out_specs=(vmem, vmem),
        scratch_shapes=buffers
        + buffers
        + [
            pltpu.VMEM((PARTS, n_chip, piece, LANES), jnp.bfloat16),
            pltpu.VMEM((PARTS, n_chip, piece, LANES), jnp.bfloat16),
            pltpu.VMEM((PARTS, n_chip - 1, piece, LANES), jnp.bfloat16),
            pltpu.VMEM((PARTS, n_chip - 1, piece, LANES), jnp.bfloat16),
            pltpu.VMEM((PARTS, piece, LANES), jnp.float32),
            pltpu.VMEM((PARTS, 2 * levels, piece, LANES), jnp.bfloat16),
            pltpu.SemaphoreType.DMA((2, len(SIDES))),
            pltpu.SemaphoreType.DMA((4, PARTS * n_chip)),
            pltpu.SemaphoreType.DMA((4, PARTS * (n_chip - 1))),
            pltpu.SemaphoreType.DMA((2, PARTS * levels)),
        ],
        compiler_params=pltpu.CompilerParams(
            collective_id=1, has_side_effects=True, vmem_limit_bytes=20 * 1024 * 1024
        ),
        name="reduce",
    )(acc, probe_flat)


def write_kernel(grad_in, flat_ref, grad_ref, probe_ref, probe_out, sems):
    grad_copy = pltpu.make_async_copy(grad_in, grad_ref, sems.at[0])
    grad_copy.start()
    parts, modes, fs, width = probe_out.shape
    copies = []
    at = 0
    for p in range(parts):
        for m in range(modes):
            for t in range(width // LANES):
                probe_out[p, m, :, t * LANES : (t + 1) * LANES] = flat_ref[at : at + fs, :].astype(
                    jnp.float32
                )
                at += fs
            copies.append(
                pltpu.make_async_copy(
                    probe_out.at[p, m], probe_ref.at[p, m], sems.at[1 + p * modes + m]
                )
            )
            copies[-1].start()
    for copy in copies:
        copy.wait()
    grad_copy.wait()


def write_call(grad, probe_flat, probe_shape):
    vmem = pl.BlockSpec(memory_space=pltpu.VMEM)
    hbm = pl.BlockSpec(memory_space=pltpu.HBM)
    return pl.pallas_call(
        write_kernel,
        out_shape=(
            jax.ShapeDtypeStruct(grad.shape, grad.dtype),
            jax.ShapeDtypeStruct(probe_shape, jnp.float32),
        ),
        in_specs=[vmem, vmem],
        out_specs=(hbm, hbm),
        scratch_shapes=[
            pltpu.VMEM(probe_shape, jnp.float32),
            pltpu.SemaphoreType.DMA((1 + probe_shape[0] * probe_shape[1],)),
        ],
        compiler_params=pltpu.CompilerParams(vmem_limit_bytes=8 * 1024 * 1024),
        name="write",
    )(grad, probe_flat)


def fourier_tables(frame_side):
    indices = np.arange(frame_side)
    product = indices[:, None] * indices[None, :] % frame_side
    angles = 2.0 * math.pi / frame_side * product
    norm_scale = 1.0 / math.sqrt(frame_side)
    real, imag = np.cos(angles) * norm_scale, -np.sin(angles) * norm_scale
    tables = (np.block([[real, -imag], [imag, real]]), np.block([[real, imag], [-imag, real]]))
    return tuple(jnp.asarray(table.astype(np.float32)).astype(jnp.bfloat16) for table in tables)


CHUNK = 32


def dot32(left, right):
    return jnp.dot(left, right, preferred_element_type=jnp.float32)


def frames_kernel(
    count_ref, at_ref, ext_ref, probe_ref, amp_ref, fwd, inv, zero_ref, pzero_ref,
    acc_ref, pacc_ref, *buffers,
):
    fs = probe_ref.shape[-1]
    modes = probe_ref.shape[1]
    lane_tiles = fs // LANES
    last_slot = amp_ref.shape[0] - 1
    live = count_ref[0, 0]
    even, odd = buffers[:4], buffers[4:]
    odd[2][...] = jnp.zeros(odd[2].shape, jnp.float32)
    odd[3][...] = jnp.zeros(odd[3].shape, jnp.float32)

    def two_sided(buffer, left_table, right_table):
        stage, half, wide, _ = buffer
        for m in range(modes):
            both = dot32(left_table[...], stage[:, m * fs : (m + 1) * fs])
            half[m * fs : (m + 1) * fs, :fs] = both[:fs].astype(jnp.bfloat16)
            half[m * fs : (m + 1) * fs, fs:] = both[fs:].astype(jnp.bfloat16)
        wide[...] = dot32(half[...], right_table[...])

    def make_exit(buffer, slot):
        stage, _, _, patch = buffer
        row_at = at_ref[0, slot]
        col_at = at_ref[1, slot]
        tile_at = col_at // LANES
        shift = col_at % LANES
        back_shift = (LANES - shift) % LANES
        lane = lax.broadcasted_iota(jnp.int32, (CHUNK, LANES), 1)
        keep_low = lane < LANES - shift
        for r in range(0, fs, CHUNK):
            rows = slice(r, r + CHUNK)
            values = []
            for plane in range(2):
                rolled = [
                    pltpu.roll(
                        ext_ref[plane, tile_at + t, pl.ds(row_at + r, CHUNK), :], back_shift, 1
                    )
                    for t in range(lane_tiles + 1)
                ]
                values.append(
                    [jnp.where(keep_low, rolled[t], rolled[t + 1]) for t in range(lane_tiles)]
                )
            for t in range(lane_tiles):
                cols = slice(t * LANES, (t + 1) * LANES)
                patch_real, patch_imag = values[0][t], values[1][t]
                patch[0, rows, cols] = patch_real
                patch[1, rows, cols] = patch_imag
                for m in range(modes):
                    probe_real = probe_ref[0, m, rows, cols]
                    probe_imag = probe_ref[1, m, rows, cols]
                    out = slice(m * fs + t * LANES, m * fs + (t + 1) * LANES)
                    stage[rows, out] = (
                        probe_real * patch_real - probe_imag * patch_imag
                    ).astype(jnp.bfloat16)
                    stage[fs + r : fs + r + CHUNK, out] = (
                        probe_real * patch_imag + probe_imag * patch_real
                    ).astype(jnp.bfloat16)

    def make_chi(buffer, slot, valid):
        stage, _, wide, _ = buffer
        for r in range(0, fs, CHUNK):
            for t in range(lane_tiles):
                cols = slice(t * LANES, (t + 1) * LANES)
                imag_cols = slice(fs + t * LANES, fs + (t + 1) * LANES)
                psi = []
                power = None
                for m in range(modes):
                    rows = slice(m * fs + r, m * fs + r + CHUNK)
                    real, imag = wide[rows, cols], wide[rows, imag_cols]
                    psi.append((real, imag))
                    own = real * real + imag * imag
                    power = own if power is None else power + own
                amp = amp_ref[slot, r : r + CHUNK, cols].astype(jnp.float32)
                factor = 1.0 - amp * lax.rsqrt(jnp.maximum(power, 0.25))
                if valid is not None:
                    factor = jnp.where(valid, factor, 0.0)
                for m in range(modes):
                    out = slice(m * fs + t * LANES, m * fs + (t + 1) * LANES)
                    stage[r : r + CHUNK, out] = (psi[m][0] * factor).astype(jnp.bfloat16)
                    stage[fs + r : fs + r + CHUNK, out] = (psi[m][1] * factor).astype(jnp.bfloat16)

    def add_grads(buffer, slot):
        _, _, wide, patch = buffer
        row_at = at_ref[0, slot]
        col_at = at_ref[1, slot]
        tile_at = col_at // LANES
        shift = col_at % LANES
        lane = lax.broadcasted_iota(jnp.int32, (CHUNK, LANES), 1)
        from_same = lane >= shift
        for r in range(0, fs, CHUNK):
            grads = [[], []]
            for t in range(lane_tiles):
                cols = slice(t * LANES, (t + 1) * LANES)
                imag_cols = slice(fs + t * LANES, fs + (t + 1) * LANES)
                patch_real = patch[0, r : r + CHUNK, cols]
                patch_imag = patch[1, r : r + CHUNK, cols]
                total_real = total_imag = None
                for m in range(modes):
                    rows = slice(m * fs + r, m * fs + r + CHUNK)
                    real, imag = wide[rows, cols], wide[rows, imag_cols]
                    probe_real = probe_ref[0, m, r : r + CHUNK, cols]
                    probe_imag = probe_ref[1, m, r : r + CHUNK, cols]
                    own_real = probe_real * real + probe_imag * imag
                    own_imag = probe_real * imag - probe_imag * real
                    total_real = own_real if m == 0 else total_real + own_real
                    total_imag = own_imag if m == 0 else total_imag + own_imag
                    at = (m * lane_tiles + t) * fs + r
                    pacc_ref[at : at + CHUNK, :] += patch_real * real + patch_imag * imag
                    at += modes * lane_tiles * fs
                    pacc_ref[at : at + CHUNK, :] += patch_real * imag - patch_imag * real
                grads[0].append(pltpu.roll(total_real, shift, 1))
                grads[1].append(pltpu.roll(total_imag, shift, 1))
            for plane in range(2):
                rolled = grads[plane]
                for t in range(lane_tiles + 1):
                    same = rolled[t] if t < lane_tiles else 0.0
                    before = rolled[t - 1] if t > 0 else 0.0
                    where = (plane, tile_at + t, pl.ds(row_at + r, CHUNK), slice(None))
                    acc_ref[where] += jnp.where(from_same, same, before)

    def advance(pair, carry):
        first = 2 * pair
        second = jnp.minimum(first + 1, last_slot)
        make_exit(even, first)
        two_sided(even, fwd, inv)
        add_grads(odd, jnp.maximum(first - 1, 0))
        make_exit(odd, second)
        two_sided(odd, fwd, inv)
        make_chi(even, first, None)
        two_sided(even, inv, fwd)
        make_chi(odd, second, first + 1 < live)
        two_sided(odd, inv, fwd)
        add_grads(even, first)
        return carry

    pairs = (live + 1) // 2
    lax.fori_loop(0, pairs, advance, 0)
    add_grads(odd, jnp.minimum(2 * pairs - 1, last_slot))


def frames_call(extended, zeros, probe_modes, amplitudes, positions, live_count, tables):
    fs = probe_modes.shape[-1]
    modes = probe_modes.shape[1]
    tiled = extended.shape
    vmem = pl.BlockSpec(memory_space=pltpu.VMEM)
    smem = pl.BlockSpec(memory_space=pltpu.SMEM)
    return pl.pallas_call(
        frames_kernel,
        out_shape=(
            jax.ShapeDtypeStruct(tiled, jnp.float32),
            jax.ShapeDtypeStruct((probe_modes.size // LANES, LANES), jnp.float32),
        ),
        in_specs=[smem, smem] + 7 * [vmem],
        out_specs=(vmem, vmem),
        input_output_aliases={7: 0, 8: 1},
        scratch_shapes=2
        * [
            pltpu.VMEM((2 * fs, modes * fs), jnp.bfloat16),
            pltpu.VMEM((modes * fs, 2 * fs), jnp.bfloat16),
            pltpu.VMEM((modes * fs, 2 * fs), jnp.float32),
            pltpu.VMEM((2, fs, fs), jnp.float32),
        ],
        compiler_params=pltpu.CompilerParams(vmem_limit_bytes=26 * 1024 * 1024),
        name="frames",
    )(live_count, positions, extended, probe_modes, amplitudes, *tables, *zeros)


def shards(object_field, probe_modes, measured_amp, scan_positions, frame_counts):
    slot_count = measured_amp.shape[2]
    extended, *zeros = halo_call(object_field, probe_modes.size)
    acc, probe_flat = frames_call(
        extended,
        zeros,
        probe_modes,
        measured_amp[0, 0],
        scan_positions[0, 0],
        frame_counts,
        fourier_tables(probe_modes.shape[-1]),
    )
    norm_scale = 1.0 / math.sqrt(lax.axis_size("row") * lax.axis_size("col") * slot_count)
    grad, probe_sum = reduce_call(acc, probe_flat, object_field.shape, norm_scale)
    return write_call(grad, probe_sum, probe_modes.shape)


def solution(mesh):
    in_specs = (
        P(None, "row", "col"),
        P(),
        P("row", "col", None, None, None),
        P("row", "col", None, None),
        P("row", "col"),
    )
    out_specs = (P(None, "row", "col"), P())
    return jax.shard_map(shards, mesh=mesh, in_specs=in_specs, out_specs=out_specs, check_vma=False)
```

```python
import functools
import math

import jax
import jax.numpy as jnp
import numpy as np
from jax import lax
from jax.experimental import pallas as pl
from jax.experimental.pallas import tpu as pltpu
from jax.sharding import PartitionSpec as P

HALO = 128
LANES = 128
PARTS = 2
HALO_LIMIT = 20


MESH = pl.DeviceIdType.MESH
SIDES = [(dr, dc) for dr in (-1, 0, 1) for dc in (-1, 0, 1) if (dr, dc) != (0, 0)]


def position():
    return (
        lax.axis_index("row"),
        lax.axis_index("col"),
        lax.axis_size("row"),
        lax.axis_size("col"),
    )


def exists(side):
    row, col, rows, cols = position()
    dr, dc = side
    inside = jnp.bool_(True)
    if dr:
        inside = row + dr >= 0 if dr < 0 else row + dr < rows
    if dc:
        other = col + dc >= 0 if dc < 0 else col + dc < cols
        inside = jnp.logical_and(inside, other) if dr else other
    return inside


def at_side(side):
    row, col, _, _ = position()
    return (row + side[0], col + side[1])


def opposite(side):
    return (-side[0], -side[1])


def part(step, margin, inner):
    return {-1: slice(0, margin), 0: slice(margin, margin + inner), 1: slice(margin + inner, None)}[
        step
    ]


def edge(step, margin, inner):
    return {-1: slice(0, margin), 0: slice(0, inner), 1: slice(inner - margin, inner)}[step]


def to_side(side, index, source, landing, send_sems, recv_sems):
    return pltpu.make_async_remote_copy(
        src_ref=source,
        dst_ref=landing,
        send_sem=send_sems.at[index],
        recv_sem=recv_sems.at[index],
        device_id=at_side(side),
        device_id_type=MESH,
    )


DIRECT = 2
WRITES = 4


def halo_kernel(whole_ref, ext_ref, acc_ref, pacc_ref, *scratch):
    object_ref, load_sem, row_land, col_land, corner_land, relay_land = scratch[:6]
    row_sems, col_sems, corner_sems, relay_sems = scratch[6:]
    row, col, n_row, n_col = position()
    side_rows, side_cols = object_ref.shape[1:]
    load = pltpu.make_async_copy(whole_ref, object_ref, load_sem)
    load.start()
    steps = (-1, 1)
    pieces = (slice(0, HALO), slice(side_cols - HALO, side_cols), slice(HALO, side_cols - HALO))
    direct = DIRECT * side_rows // 4
    parts = (slice(0, direct), slice(direct, side_rows))

    def has(dr, dc):
        return exists((dr, dc))

    def turns(d):
        return jnp.logical_and(has(0, d), lax.rem(col, 4) == (3 if d > 0 else 0))

    def relays(d):
        other = col - 3 * d
        inside = jnp.logical_and(other >= 0, other < n_col)
        return jnp.logical_and(inside, lax.rem(col, 4) == (2 if d > 0 else 1))

    def lands_by_relay(d):
        return jnp.logical_and(has(0, -d), lax.rem(col, 4) == (0 if d > 0 else 3))

    links = []
    for d in steps:
        links.append((has(d, 0), (row + d, col)))
        links.append((has(0, d), (row, col + d)))
        links.append((turns(d), (row, col + 3 * d)))
        links.append((relays(d), (row, col - 3 * d)))
        links.append((relays(d), (row, col - 2 * d)))
        links.append((lands_by_relay(d), (row, col + 2 * d)))
    barrier = pltpu.get_barrier_semaphore()
    count = jnp.int32(0)
    for there, device in links:

        @pl.when(there)
        def _(device=device):
            pl.semaphore_signal(barrier, inc=1, device_id=device, device_id_type=MESH)

        count = count + there.astype(jnp.int32)
    pl.semaphore_wait(barrier, count)

    def remote(source, landing, sems, index, device):
        return pltpu.make_async_remote_copy(
            src_ref=source,
            dst_ref=landing,
            send_sem=sems.at[0, index],
            recv_sem=sems.at[1, index],
            device_id=device,
            device_id_type=MESH,
        )

    def row_copy(s, p):
        d = steps[s]
        source = whole_ref.at[:, edge(d, HALO, side_rows), pieces[p]]
        return remote(
            source, row_land.at[1 - s, :, :, pieces[p]], row_sems, 3 * s + p, (row + d, col)
        )

    def col_copy(s, p, to_relay=False):
        d = steps[s]
        source = whole_ref.at[:, parts[p], edge(d, HALO, side_cols)]
        if to_relay:
            return pltpu.make_async_remote_copy(
                src_ref=source,
                dst_ref=relay_land.at[s],
                send_sem=col_sems.at[0, 2 * s + p],
                recv_sem=relay_sems.at[1, s],
                device_id=(row, col + 3 * d),
                device_id_type=MESH,
            )
        return remote(
            source, col_land.at[1 - s, :, parts[p], :], col_sems, 2 * s + p, (row, col + d)
        )

    def relay_copy(s):
        d = steps[s]
        return pltpu.make_async_remote_copy(
            src_ref=relay_land.at[s],
            dst_ref=col_land.at[1 - s, :, parts[1], :],
            send_sem=relay_sems.at[0, s],
            recv_sem=col_sems.at[1, 2 * s + 1],
            device_id=(row, col - 2 * d),
            device_id_type=MESH,
        )

    def corner_copy(r, s):
        source = row_land.at[r, :, :, pieces[s]]
        return remote(
            source, corner_land.at[r, 1 - s], corner_sems, 2 * r + s, (row, col + steps[s])
        )

    def when(condition, action):
        @pl.when(condition)
        def _():
            action()

    for p in range(2):
        for s, d in enumerate(steps):
            when(has(d, 0), lambda s=s, p=p: row_copy(s, p).start())
    for p in (1, 0):
        for s, d in enumerate(steps):
            if p:
                when(turns(d), lambda s=s: col_copy(s, 1, True).start())
                straight = jnp.logical_and(has(0, d), jnp.logical_not(turns(d)))
                when(straight, lambda s=s: col_copy(s, 1).start())
            else:
                when(has(0, d), lambda s=s: col_copy(s, 0).start())
    for s, d in enumerate(steps):
        when(has(d, 0), lambda s=s: row_copy(s, 2).start())

    acc_ref[...] = jnp.zeros(acc_ref.shape, jnp.float32)
    pacc_ref[...] = jnp.zeros(pacc_ref.shape, jnp.float32)
    spare = ext_ref.shape[1] - 1
    ext_ref[:, spare] = jnp.zeros((2, ext_ref.shape[2], LANES), jnp.float32)
    margin, inner = HALO // LANES, side_cols // LANES

    def tiles_of(d):
        return range(spare)[part(d, margin, inner)]

    def fill(rows, tiles, height, source):
        for k, t in enumerate(tiles):
            if source is None:
                ext_ref[:, t, rows, :] = jnp.zeros((2, height, LANES), ext_ref.dtype)
            else:
                ext_ref[:, t, rows, :] = source[:, :, k * LANES : (k + 1) * LANES].astype(
                    jnp.float32
                )

    load.wait()
    fill(part(0, HALO, side_rows), tiles_of(0), side_rows, object_ref)

    for s, d in enumerate(steps):

        def pass_on(s=s):
            relay_copy_in = col_copy(s, 1, True)
            relay_copy_in.wait_recv()
            relay_copy(s).start()

        when(relays(d), pass_on)
    for r, dr in enumerate(steps):
        for s, dc in enumerate(steps):

            def hand_over(r=r, s=s, dc=dc):
                row_copy(1 - r, s).wait_recv()
                when(has(0, dc), lambda: corner_copy(r, s).start())

            when(has(dr, 0), hand_over)
    for s, d in enumerate(steps):
        rows = part(0, HALO, side_rows)
        here = s

        def take(s=s, d=d, rows=rows):
            col_copy(1 - s, 0).wait_recv()
            col_copy(1 - s, 1).wait_recv()
            fill(rows, tiles_of(d), side_rows, col_land.at[s])

        when(has(0, d), take)
        when(
            jnp.logical_not(has(0, d)), lambda d=d, rows=rows: fill(rows, tiles_of(d), side_rows, None)
        )
    for r, dr in enumerate(steps):
        rows = part(dr, HALO, side_rows)

        def take_rows(r=r, rows=rows):
            row_copy(1 - r, 2).wait_recv()
            fill(rows, tiles_of(0), HALO, row_land.at[r])

        when(has(dr, 0), take_rows)
        when(
            jnp.logical_not(has(dr, 0)), lambda rows=rows: fill(rows, tiles_of(0), HALO, None)
        )
    for r, dr in enumerate(steps):
        rows = part(dr, HALO, side_rows)
        for s, dc in enumerate(steps):

            def take_corner(r=r, s=s, dc=dc, rows=rows):
                corner_copy(r, 1 - s).wait_recv()
                fill(rows, tiles_of(dc), HALO, corner_land.at[r, s])

            when(has(dr, dc), take_corner)
            when(
                jnp.logical_not(has(dr, dc)),
                lambda dc=dc, rows=rows: fill(rows, tiles_of(dc), HALO, None),
            )

    for s, d in enumerate(steps):
        for p in range(3):
            when(has(d, 0), lambda s=s, p=p: row_copy(s, p).wait_send())
        for p in range(2):
            when(has(0, d), lambda s=s, p=p: col_copy(s, p).wait_send())
        when(relays(d), lambda s=s: relay_copy(s).wait_send())
        for r, dr in enumerate(steps):
            when(has(dr, d), lambda r=r, s=s: corner_copy(r, s).wait_send())


def halo_call(object_field, probe_size):
    planes, side_rows, side_cols = object_field.shape
    kind = object_field.dtype
    vmem = pl.BlockSpec(memory_space=pltpu.VMEM)
    tiled = jax.ShapeDtypeStruct(
        (planes, (side_cols + 2 * HALO) // LANES + 1, side_rows + 2 * HALO, LANES), jnp.float32
    )
    direct = DIRECT * side_rows // 4
    return pl.pallas_call(
        halo_kernel,
        out_shape=(
            tiled,
            tiled,
            jax.ShapeDtypeStruct((probe_size // LANES, LANES), jnp.float32),
        ),
        in_specs=[pl.BlockSpec(memory_space=pltpu.HBM)],
        out_specs=3 * (vmem,),
        scratch_shapes=[
            pltpu.VMEM(object_field.shape, kind),
            pltpu.SemaphoreType.DMA,
            pltpu.VMEM((2, planes, HALO, side_cols), kind),
            pltpu.VMEM((2, planes, side_rows, HALO), kind),
            pltpu.VMEM((2, 2, planes, HALO, HALO), kind),
            pltpu.VMEM((2, planes, side_rows - direct, HALO), kind),
            pltpu.SemaphoreType.DMA((2, 6)),
            pltpu.SemaphoreType.DMA((2, 4)),
            pltpu.SemaphoreType.DMA((2, 4)),
            pltpu.SemaphoreType.DMA((2, 2)),
        ],
        compiler_params=pltpu.CompilerParams(
            collective_id=0, has_side_effects=True, vmem_limit_bytes=HALO_LIMIT * 1024 * 1024
        ),
        cost_estimate=pl.CostEstimate(flops=10**10, bytes_accessed=0, transcendentals=0),
        name="halo",
    )(pltpu.with_memory_space_constraint(object_field, pltpu.HBM))


def reduce_kernel(scale, acc_ref, pacc_ref, grad_ref, full, *scratch):
    count = len(SIDES)
    sends, landings, rest = scratch[:count], scratch[count : 2 * count], scratch[2 * count :]
    psend, pair_recv, merged, precv, sums, zbuf = rest[:6]
    side_sems, pair_sems, col_sems, row_sems = rest[6:]
    row, col, n_row, n_col = position()
    side_rows, side_cols = grad_ref.shape[1:]
    margin = HALO // LANES
    inner = side_cols // LANES
    part_rows = psend.shape[2]
    share = PARTS * part_rows
    chip, core = col // 2, lax.rem(col, 2)
    n_chip = n_col // 2
    sibling = (row, 2 * chip + 1 - core)

    barrier = pltpu.get_barrier_semaphore()
    waits = jnp.int32(n_row + n_chip - 1)
    pl.semaphore_signal(barrier, inc=1, device_id=sibling, device_id_type=MESH)
    for k in range(1, n_chip):
        peer = (row, 2 * lax.rem(chip + k, n_chip) + core)
        pl.semaphore_signal(barrier, inc=1, device_id=peer, device_id_type=MESH)
    for k in range(1, n_row):
        pl.semaphore_signal(
            barrier, inc=1, device_id=(lax.rem(row + k, n_row), col), device_id_type=MESH
        )
    for side in SIDES:
        if side[1]:

            @pl.when(exists(side))
            def _(side=side):
                pl.semaphore_signal(barrier, inc=1, device_id=at_side(side), device_id_type=MESH)

            waits = waits + exists(side).astype(jnp.int32)

    def stage_side(index):
        dr, dc = SIDES[index]
        tiles = range(inner + 2 * margin)[part(dc, margin, inner)]
        for k, t in enumerate(tiles):
            sends[index][:, k] = acc_ref[:, t, part(dr, HALO, side_rows), :].astype(jnp.bfloat16)

    def stage_sides(chosen):
        for index, side in enumerate(SIDES):
            if chosen(side):
                stage_side(index)

    def to_peer(source, landing, sems, which, k, device):
        return pltpu.make_async_remote_copy(
            src_ref=source,
            dst_ref=landing,
            send_sem=sems.at[which, k],
            recv_sem=sems.at[which + 1, k],
            device_id=device,
            device_id_type=MESH,
        )

    def chip_at(k):
        return lax.rem(chip + k, n_chip)

    def chip_from(k):
        return lax.rem(chip + n_chip - k, n_chip)

    def chip_peer(k):
        return (row, 2 * chip_at(k) + core)

    def rows_of(index, h):
        return pl.ds(pl.multiple_of(index * share + h * part_rows, part_rows), part_rows)

    def pair_copy(h, k):
        return to_peer(
            psend.at[h, k], pair_recv.at[h, k], pair_sems, 0, h * n_chip + k, sibling
        )

    def scatter_copy(h, k):
        at = h * (n_chip - 1) + k - 1
        return to_peer(merged.at[h, k - 1], precv.at[h, k - 1], col_sems, 0, at, chip_peer(k))

    def row_copy(h, k, owner):
        at = h * (n_row - 1) + k - 1
        peer = (lax.rem(row + k, n_row), col)
        return to_peer(zbuf.at[h, row], zbuf.at[h, owner], row_sems, 0, at, peer)

    def gather_copy(h, k, owner):
        at = h * (n_chip - 1) + k - 1
        source, landing = full.at[rows_of(col, h), :], full.at[rows_of(owner, h), :]
        return to_peer(source, landing, col_sems, 2, at, chip_peer(k))

    def forward_copy(h, k, side):
        source = full.at[rows_of(2 * chip_from(k) + core, h), :]
        landing = full.at[rows_of(2 * chip_from(k) + side, h), :]
        return to_peer(source, landing, pair_sems, 2, h * n_chip + k, sibling)

    def side_copy(index):
        return to_side(
            SIDES[index], index, sends[index], landings[index], side_sems.at[0], side_sems.at[1]
        )

    def start_sides(chosen):
        for index, side in enumerate(SIDES):
            if chosen(side):

                @pl.when(exists(side))
                def _(index=index):
                    side_copy(index).start()

    def add_sides(chosen):
        for index, side in enumerate(SIDES):
            if not chosen(side):
                continue
            dr, dc = opposite(side)
            rows = edge(dr, HALO, side_rows)
            tiles = range(inner)[edge(dc, margin, inner)]

            @pl.when(exists((dr, dc)))
            def _(index=index, rows=rows, tiles=tiles):
                side_copy(index).wait_recv()
                for k, t in enumerate(tiles):
                    grad_ref[:, rows, t * LANES : (t + 1) * LANES] += landings[index][
                        :, k
                    ].astype(jnp.float32)

    over_rows = lambda side: side[1] == 0
    over_cols = lambda side: side[0] == 0
    corners = lambda side: side[0] != 0 and side[1] != 0
    order = list(range(1, n_chip)) + [0]
    for h in range(PARTS):
        for k in order:
            psend[h, k] = pacc_ref[rows_of(2 * chip_at(k) + 1 - core, h), :].astype(jnp.bfloat16)
    stage_sides(over_rows)
    pl.semaphore_wait(barrier, waits)
    for h in range(PARTS):
        for k in order:
            pair_copy(h, k).start()
    start_sides(over_rows)
    stage_sides(over_cols)
    stage_sides(corners)

    def merge(h, k):
        pair_copy(h, k).wait_recv()
        own = pacc_ref[rows_of(2 * chip_at(k) + core, h), :]
        return own + pair_recv[h, k].astype(jnp.float32)

    for h in range(PARTS):
        for k in range(1, n_chip):
            merged[h, k - 1] = merge(h, k).astype(jnp.bfloat16)
            scatter_copy(h, k).start()
        sums[h] = merge(h, 0)
    start_sides(over_cols)
    for t in range(inner):
        grad_ref[:, :, t * LANES : (t + 1) * LANES] = acc_ref[
            :, margin + t, HALO : HALO + side_rows, :
        ]
    for h in range(PARTS):
        total = sums[h]
        for k in range(1, n_chip):
            scatter_copy(h, k).wait_recv()
            total = total + precv[h, k - 1].astype(jnp.float32)
        zbuf[h, row] = total.astype(jnp.bfloat16)
        for k in range(1, n_row):
            row_copy(h, k, row).start()
    start_sides(corners)
    for h in range(PARTS):
        for k in range(1, n_row):
            row_copy(h, k, lax.rem(row + n_row - k, n_row)).wait_recv()
        total = zbuf[h, 0].astype(jnp.float32)
        for k in range(1, n_row):
            total = total + zbuf[h, k].astype(jnp.float32)
        full[rows_of(col, h), :] = (total * scale).astype(jnp.bfloat16)
        for k in range(1, n_chip):
            gather_copy(h, k, col).start()
        forward_copy(h, 0, core).start()
    add_sides(over_rows)
    add_sides(over_cols)
    for h in range(PARTS):
        for k in range(1, n_chip):
            gather_copy(h, k, 2 * chip_from(k) + core).wait_recv()
            forward_copy(h, k, core).start()
    add_sides(corners)

    for h in range(PARTS):
        for k in range(n_chip):
            forward_copy(h, k, 1 - core).wait_recv()
    for h in range(PARTS):
        for k in range(1, n_chip):
            scatter_copy(h, k).wait_send()
            gather_copy(h, k, col).wait_send()
        for k in range(n_chip):
            pair_copy(h, k).wait_send()
            forward_copy(h, k, core).wait_send()
        for k in range(1, n_row):
            row_copy(h, k, row).wait_send()
    for index, side in enumerate(SIDES):

        @pl.when(exists(side))
        def _(index=index):
            side_copy(index).wait_send()


def reduce_call(acc, probe_flat, object_shape, scale):
    n_row, n_col = lax.axis_size("row"), lax.axis_size("col")
    _, side_rows, side_cols = object_shape
    inner = side_cols // LANES
    margin = HALO // LANES
    vmem = pl.BlockSpec(memory_space=pltpu.VMEM)
    buffers = []
    for dr, dc in SIDES:
        buffers.append(
            pltpu.VMEM(
                (2, margin if dc else inner, HALO if dr else side_rows, LANES), jnp.bfloat16
            )
        )
    total_rows = probe_flat.shape[0]
    piece = total_rows // n_col // PARTS
    n_chip = n_col // 2
    return pl.pallas_call(
        functools.partial(reduce_kernel, scale),
        out_shape=(
            jax.ShapeDtypeStruct(object_shape, jnp.float32),
            jax.ShapeDtypeStruct(probe_flat.shape, jnp.bfloat16),
        ),
        in_specs=[vmem, vmem],
        out_specs=(vmem, vmem),
        scratch_shapes=buffers
        + buffers
        + [
            pltpu.VMEM((PARTS, n_chip, piece, LANES), jnp.bfloat16),
            pltpu.VMEM((PARTS, n_chip, piece, LANES), jnp.bfloat16),
            pltpu.VMEM((PARTS, n_chip - 1, piece, LANES), jnp.bfloat16),
            pltpu.VMEM((PARTS, n_chip - 1, piece, LANES), jnp.bfloat16),
            pltpu.VMEM((PARTS, piece, LANES), jnp.float32),
            pltpu.VMEM((PARTS, n_row, piece, LANES), jnp.bfloat16),
            pltpu.SemaphoreType.DMA((2, len(SIDES))),
            pltpu.SemaphoreType.DMA((4, PARTS * n_chip)),
            pltpu.SemaphoreType.DMA((4, PARTS * (n_chip - 1))),
            pltpu.SemaphoreType.DMA((2, PARTS * (n_row - 1))),
        ],
        compiler_params=pltpu.CompilerParams(
            collective_id=1, has_side_effects=True, vmem_limit_bytes=20 * 1024 * 1024
        ),
        name="reduce",
    )(acc, probe_flat)


def write_kernel(grad_in, flat_ref, grad_ref, probe_ref, probe_out, sems):
    parts, modes, fs, width = probe_out.shape
    planes, side_rows, _ = grad_in.shape
    height = side_rows // WRITES
    copies = []
    for p in range(planes):
        for k in range(WRITES):
            block = (p, slice(k * height, (k + 1) * height))
            sem = sems.at[parts * modes + p * WRITES + k]
            copies.append(pltpu.make_async_copy(grad_in.at[block], grad_ref.at[block], sem))
            copies[-1].start()
    at = 0
    for p in range(parts):
        for m in range(modes):
            for t in range(width // LANES):
                probe_out[p, m, :, t * LANES : (t + 1) * LANES] = flat_ref[at : at + fs, :].astype(
                    jnp.float32
                )
                at += fs
            copies.append(
                pltpu.make_async_copy(
                    probe_out.at[p, m], probe_ref.at[p, m], sems.at[p * modes + m]
                )
            )
            copies[-1].start()
    for copy in copies:
        copy.wait()


def write_call(grad, probe_flat, probe_shape):
    vmem = pl.BlockSpec(memory_space=pltpu.VMEM)
    hbm = pl.BlockSpec(memory_space=pltpu.HBM)
    return pl.pallas_call(
        write_kernel,
        out_shape=(
            jax.ShapeDtypeStruct(grad.shape, grad.dtype),
            jax.ShapeDtypeStruct(probe_shape, jnp.float32),
        ),
        in_specs=[vmem, vmem],
        out_specs=(hbm, hbm),
        scratch_shapes=[
            pltpu.VMEM(probe_shape, jnp.float32),
            pltpu.SemaphoreType.DMA((probe_shape[0] * probe_shape[1] + grad.shape[0] * WRITES,)),
        ],
        compiler_params=pltpu.CompilerParams(vmem_limit_bytes=8 * 1024 * 1024),
        name="write",
    )(grad, probe_flat)


def fourier_tables(frame_side):
    indices = np.arange(frame_side)
    product = indices[:, None] * indices[None, :] % frame_side
    angles = 2.0 * math.pi / frame_side * product
    norm_scale = 1.0 / math.sqrt(frame_side)
    real, imag = np.cos(angles) * norm_scale, -np.sin(angles) * norm_scale
    tables = (np.block([[real, -imag], [imag, real]]), np.block([[real, imag], [-imag, real]]))
    return tuple(jnp.asarray(table.astype(np.float32)).astype(jnp.bfloat16) for table in tables)


CHUNK = 32


def dot32(left, right):
    return jnp.dot(left, right, preferred_element_type=jnp.float32)


def frames_kernel(
    count_ref, at_ref, ext_ref, probe_ref, amp_ref, fwd, inv, zero_ref, pzero_ref,
    acc_ref, pacc_ref, *buffers,
):
    fs = probe_ref.shape[-1]
    modes = probe_ref.shape[1]
    lane_tiles = fs // LANES
    last_slot = amp_ref.shape[0] - 1
    live = count_ref[0, 0]
    even, odd = buffers[:4], buffers[4:]
    odd[2][...] = jnp.zeros(odd[2].shape, jnp.float32)
    odd[3][...] = jnp.zeros(odd[3].shape, jnp.float32)

    def two_sided(buffer, left_table, right_table):
        stage, half, wide, _ = buffer
        for m in range(modes):
            both = dot32(left_table[...], stage[:, m * fs : (m + 1) * fs])
            half[m * fs : (m + 1) * fs, :fs] = both[:fs].astype(jnp.bfloat16)
            half[m * fs : (m + 1) * fs, fs:] = both[fs:].astype(jnp.bfloat16)
        wide[...] = dot32(half[...], right_table[...])

    def make_exit(buffer, slot):
        stage, _, _, patch = buffer
        row_at = at_ref[0, slot]
        col_at = at_ref[1, slot]
        tile_at = col_at // LANES
        shift = col_at % LANES
        back_shift = (LANES - shift) % LANES
        lane = lax.broadcasted_iota(jnp.int32, (CHUNK, LANES), 1)
        keep_low = lane < LANES - shift
        for r in range(0, fs, CHUNK):
            rows = slice(r, r + CHUNK)
            values = []
            for plane in range(2):
                rolled = [
                    pltpu.roll(
                        ext_ref[plane, tile_at + t, pl.ds(row_at + r, CHUNK), :], back_shift, 1
                    )
                    for t in range(lane_tiles + 1)
                ]
                values.append(
                    [jnp.where(keep_low, rolled[t], rolled[t + 1]) for t in range(lane_tiles)]
                )
            for t in range(lane_tiles):
                cols = slice(t * LANES, (t + 1) * LANES)
                patch_real, patch_imag = values[0][t], values[1][t]
                patch[0, rows, cols] = patch_real
                patch[1, rows, cols] = patch_imag
                for m in range(modes):
                    probe_real = probe_ref[0, m, rows, cols]
                    probe_imag = probe_ref[1, m, rows, cols]
                    out = slice(m * fs + t * LANES, m * fs + (t + 1) * LANES)
                    stage[rows, out] = (
                        probe_real * patch_real - probe_imag * patch_imag
                    ).astype(jnp.bfloat16)
                    stage[fs + r : fs + r + CHUNK, out] = (
                        probe_real * patch_imag + probe_imag * patch_real
                    ).astype(jnp.bfloat16)

    def make_chi(buffer, slot, valid):
        stage, _, wide, _ = buffer
        for r in range(0, fs, CHUNK):
            for t in range(lane_tiles):
                cols = slice(t * LANES, (t + 1) * LANES)
                imag_cols = slice(fs + t * LANES, fs + (t + 1) * LANES)
                psi = []
                power = None
                for m in range(modes):
                    rows = slice(m * fs + r, m * fs + r + CHUNK)
                    real, imag = wide[rows, cols], wide[rows, imag_cols]
                    psi.append((real, imag))
                    own = real * real + imag * imag
                    power = own if power is None else power + own
                amp = amp_ref[slot, r : r + CHUNK, cols].astype(jnp.float32)
                factor = 1.0 - amp * lax.rsqrt(jnp.maximum(power, 0.25))
                if valid is not None:
                    factor = jnp.where(valid, factor, 0.0)
                for m in range(modes):
                    out = slice(m * fs + t * LANES, m * fs + (t + 1) * LANES)
                    stage[r : r + CHUNK, out] = (psi[m][0] * factor).astype(jnp.bfloat16)
                    stage[fs + r : fs + r + CHUNK, out] = (psi[m][1] * factor).astype(jnp.bfloat16)

    def add_grads(buffer, slot):
        _, _, wide, patch = buffer
        row_at = at_ref[0, slot]
        col_at = at_ref[1, slot]
        tile_at = col_at // LANES
        shift = col_at % LANES
        lane = lax.broadcasted_iota(jnp.int32, (CHUNK, LANES), 1)
        from_same = lane >= shift
        for r in range(0, fs, CHUNK):
            grads = [[], []]
            for t in range(lane_tiles):
                cols = slice(t * LANES, (t + 1) * LANES)
                imag_cols = slice(fs + t * LANES, fs + (t + 1) * LANES)
                patch_real = patch[0, r : r + CHUNK, cols]
                patch_imag = patch[1, r : r + CHUNK, cols]
                total_real = total_imag = None
                for m in range(modes):
                    rows = slice(m * fs + r, m * fs + r + CHUNK)
                    real, imag = wide[rows, cols], wide[rows, imag_cols]
                    probe_real = probe_ref[0, m, r : r + CHUNK, cols]
                    probe_imag = probe_ref[1, m, r : r + CHUNK, cols]
                    own_real = probe_real * real + probe_imag * imag
                    own_imag = probe_real * imag - probe_imag * real
                    total_real = own_real if m == 0 else total_real + own_real
                    total_imag = own_imag if m == 0 else total_imag + own_imag
                    at = (m * lane_tiles + t) * fs + r
                    pacc_ref[at : at + CHUNK, :] += patch_real * real + patch_imag * imag
                    at += modes * lane_tiles * fs
                    pacc_ref[at : at + CHUNK, :] += patch_real * imag - patch_imag * real
                grads[0].append(pltpu.roll(total_real, shift, 1))
                grads[1].append(pltpu.roll(total_imag, shift, 1))
            for plane in range(2):
                rolled = grads[plane]
                for t in range(lane_tiles + 1):
                    same = rolled[t] if t < lane_tiles else 0.0
                    before = rolled[t - 1] if t > 0 else 0.0
                    where = (plane, tile_at + t, pl.ds(row_at + r, CHUNK), slice(None))
                    acc_ref[where] += jnp.where(from_same, same, before)

    def advance(pair, carry):
        first = 2 * pair
        second = jnp.minimum(first + 1, last_slot)
        make_exit(even, first)
        two_sided(even, fwd, inv)
        add_grads(odd, jnp.maximum(first - 1, 0))
        make_exit(odd, second)
        two_sided(odd, fwd, inv)
        make_chi(even, first, None)
        two_sided(even, inv, fwd)
        make_chi(odd, second, first + 1 < live)
        two_sided(odd, inv, fwd)
        add_grads(even, first)
        return carry

    pairs = (live + 1) // 2
    lax.fori_loop(0, pairs, advance, 0)
    add_grads(odd, jnp.minimum(2 * pairs - 1, last_slot))


def frames_call(extended, zeros, probe_modes, amplitudes, positions, live_count, tables):
    fs = probe_modes.shape[-1]
    modes = probe_modes.shape[1]
    tiled = extended.shape
    vmem = pl.BlockSpec(memory_space=pltpu.VMEM)
    smem = pl.BlockSpec(memory_space=pltpu.SMEM)
    return pl.pallas_call(
        frames_kernel,
        out_shape=(
            jax.ShapeDtypeStruct(tiled, jnp.float32),
            jax.ShapeDtypeStruct((probe_modes.size // LANES, LANES), jnp.float32),
        ),
        in_specs=[smem, smem] + 7 * [vmem],
        out_specs=(vmem, vmem),
        input_output_aliases={7: 0, 8: 1},
        scratch_shapes=2
        * [
            pltpu.VMEM((2 * fs, modes * fs), jnp.bfloat16),
            pltpu.VMEM((modes * fs, 2 * fs), jnp.bfloat16),
            pltpu.VMEM((modes * fs, 2 * fs), jnp.float32),
            pltpu.VMEM((2, fs, fs), jnp.float32),
        ],
        compiler_params=pltpu.CompilerParams(vmem_limit_bytes=26 * 1024 * 1024),
        name="frames",
    )(live_count, positions, extended, probe_modes, amplitudes, *tables, *zeros)


def shards(object_field, probe_modes, measured_amp, scan_positions, frame_counts):
    slot_count = measured_amp.shape[2]
    extended, *zeros = halo_call(object_field, probe_modes.size)
    acc, probe_flat = frames_call(
        extended,
        zeros,
        probe_modes,
        measured_amp[0, 0],
        scan_positions[0, 0],
        frame_counts,
        fourier_tables(probe_modes.shape[-1]),
    )
    norm_scale = 1.0 / math.sqrt(lax.axis_size("row") * lax.axis_size("col") * slot_count)
    grad, probe_sum = reduce_call(acc, probe_flat, object_field.shape, norm_scale)
    return write_call(grad, probe_sum, probe_modes.shape)


def solution(mesh):
    in_specs = (
        P(None, "row", "col"),
        P(),
        P("row", "col", None, None, None),
        P("row", "col", None, None),
        P("row", "col"),
    )
    out_specs = (P(None, "row", "col"), P())
    return jax.shard_map(shards, mesh=mesh, in_specs=in_specs, out_specs=out_specs, check_vma=False)
```

```python
import functools
import math

import jax
import jax.numpy as jnp
import numpy as np
from jax import lax
from jax.experimental import pallas as pl
from jax.experimental.pallas import tpu as pltpu
from jax.sharding import PartitionSpec as P

HALO = 128
LANES = 128
PARTS = 2
HALO_LIMIT = 20


MESH = pl.DeviceIdType.MESH
SIDES = [(dr, dc) for dr in (-1, 0, 1) for dc in (-1, 0, 1) if (dr, dc) != (0, 0)]


def position():
    return (
        lax.axis_index("row"),
        lax.axis_index("col"),
        lax.axis_size("row"),
        lax.axis_size("col"),
    )


def exists(side):
    row, col, rows, cols = position()
    dr, dc = side
    inside = jnp.bool_(True)
    if dr:
        inside = row + dr >= 0 if dr < 0 else row + dr < rows
    if dc:
        other = col + dc >= 0 if dc < 0 else col + dc < cols
        inside = jnp.logical_and(inside, other) if dr else other
    return inside


def at_side(side):
    row, col, _, _ = position()
    return (row + side[0], col + side[1])


def opposite(side):
    return (-side[0], -side[1])


def part(step, margin, inner):
    return {-1: slice(0, margin), 0: slice(margin, margin + inner), 1: slice(margin + inner, None)}[
        step
    ]


def edge(step, margin, inner):
    return {-1: slice(0, margin), 0: slice(0, inner), 1: slice(inner - margin, inner)}[step]


def to_side(side, index, source, landing, send_sems, recv_sems):
    return pltpu.make_async_remote_copy(
        src_ref=source,
        dst_ref=landing,
        send_sem=send_sems.at[index],
        recv_sem=recv_sems.at[index],
        device_id=at_side(side),
        device_id_type=MESH,
    )


DIRECT = 2


def halo_kernel(whole_ref, ext_ref, acc_ref, pacc_ref, *scratch):
    object_ref, load_sem, row_land, col_land, corner_land, relay_land = scratch[:6]
    row_sems, col_sems, corner_sems, relay_sems = scratch[6:]
    row, col, n_row, n_col = position()
    side_rows, side_cols = object_ref.shape[1:]
    load = pltpu.make_async_copy(whole_ref, object_ref, load_sem)
    load.start()
    steps = (-1, 1)
    pieces = (slice(0, HALO), slice(side_cols - HALO, side_cols), slice(HALO, side_cols - HALO))
    direct = DIRECT * side_rows // 4
    parts = (slice(0, direct), slice(direct, side_rows))

    def has(dr, dc):
        return exists((dr, dc))

    def turns(d):
        return jnp.logical_and(has(0, d), lax.rem(col, 4) == (3 if d > 0 else 0))

    def relays(d):
        other = col - 3 * d
        inside = jnp.logical_and(other >= 0, other < n_col)
        return jnp.logical_and(inside, lax.rem(col, 4) == (2 if d > 0 else 1))

    def lands_by_relay(d):
        return jnp.logical_and(has(0, -d), lax.rem(col, 4) == (0 if d > 0 else 3))

    links = []
    for d in steps:
        links.append((has(d, 0), (row + d, col)))
        links.append((has(0, d), (row, col + d)))
        links.append((turns(d), (row, col + 3 * d)))
        links.append((relays(d), (row, col - 3 * d)))
        links.append((relays(d), (row, col - 2 * d)))
        links.append((lands_by_relay(d), (row, col + 2 * d)))
    barrier = pltpu.get_barrier_semaphore()
    count = jnp.int32(0)
    for there, device in links:

        @pl.when(there)
        def _(device=device):
            pl.semaphore_signal(barrier, inc=1, device_id=device, device_id_type=MESH)

        count = count + there.astype(jnp.int32)
    pl.semaphore_wait(barrier, count)

    def remote(source, landing, sems, index, device):
        return pltpu.make_async_remote_copy(
            src_ref=source,
            dst_ref=landing,
            send_sem=sems.at[0, index],
            recv_sem=sems.at[1, index],
            device_id=device,
            device_id_type=MESH,
        )

    def row_copy(s, p):
        d = steps[s]
        source = whole_ref.at[:, edge(d, HALO, side_rows), pieces[p]]
        return remote(
            source, row_land.at[1 - s, :, :, pieces[p]], row_sems, 3 * s + p, (row + d, col)
        )

    def col_copy(s, p, to_relay=False):
        d = steps[s]
        source = whole_ref.at[:, parts[p], edge(d, HALO, side_cols)]
        if to_relay:
            return pltpu.make_async_remote_copy(
                src_ref=source,
                dst_ref=relay_land.at[s],
                send_sem=col_sems.at[0, 2 * s + p],
                recv_sem=relay_sems.at[1, s],
                device_id=(row, col + 3 * d),
                device_id_type=MESH,
            )
        return remote(
            source, col_land.at[1 - s, :, parts[p], :], col_sems, 2 * s + p, (row, col + d)
        )

    def relay_copy(s):
        d = steps[s]
        return pltpu.make_async_remote_copy(
            src_ref=relay_land.at[s],
            dst_ref=col_land.at[1 - s, :, parts[1], :],
            send_sem=relay_sems.at[0, s],
            recv_sem=col_sems.at[1, 2 * s + 1],
            device_id=(row, col - 2 * d),
            device_id_type=MESH,
        )

    def corner_copy(r, s):
        source = row_land.at[r, :, :, pieces[s]]
        return remote(
            source, corner_land.at[r, 1 - s], corner_sems, 2 * r + s, (row, col + steps[s])
        )

    def when(condition, action):
        @pl.when(condition)
        def _():
            action()

    for p in range(2):
        for s, d in enumerate(steps):
            when(has(d, 0), lambda s=s, p=p: row_copy(s, p).start())
    for p in (1, 0):
        for s, d in enumerate(steps):
            if p:
                when(turns(d), lambda s=s: col_copy(s, 1, True).start())
                straight = jnp.logical_and(has(0, d), jnp.logical_not(turns(d)))
                when(straight, lambda s=s: col_copy(s, 1).start())
            else:
                when(has(0, d), lambda s=s: col_copy(s, 0).start())
    for s, d in enumerate(steps):
        when(has(d, 0), lambda s=s: row_copy(s, 2).start())

    acc_ref[...] = jnp.zeros(acc_ref.shape, jnp.float32)
    pacc_ref[...] = jnp.zeros(pacc_ref.shape, jnp.float32)
    spare = ext_ref.shape[1] - 1
    ext_ref[:, spare] = jnp.zeros((2, ext_ref.shape[2], LANES), jnp.float32)
    margin, inner = HALO // LANES, side_cols // LANES

    def tiles_of(d):
        return range(spare)[part(d, margin, inner)]

    def fill(rows, tiles, height, source):
        for k, t in enumerate(tiles):
            if source is None:
                ext_ref[:, t, rows, :] = jnp.zeros((2, height, LANES), ext_ref.dtype)
            else:
                ext_ref[:, t, rows, :] = source[:, :, k * LANES : (k + 1) * LANES].astype(
                    jnp.float32
                )

    load.wait()
    fill(part(0, HALO, side_rows), tiles_of(0), side_rows, object_ref)

    for s, d in enumerate(steps):

        def pass_on(s=s):
            relay_copy_in = col_copy(s, 1, True)
            relay_copy_in.wait_recv()
            relay_copy(s).start()

        when(relays(d), pass_on)
    for r, dr in enumerate(steps):
        for s, dc in enumerate(steps):

            def hand_over(r=r, s=s, dc=dc):
                row_copy(1 - r, s).wait_recv()
                when(has(0, dc), lambda: corner_copy(r, s).start())

            when(has(dr, 0), hand_over)
    for s, d in enumerate(steps):
        rows = part(0, HALO, side_rows)
        here = s

        def take(s=s, d=d, rows=rows):
            col_copy(1 - s, 0).wait_recv()
            col_copy(1 - s, 1).wait_recv()
            fill(rows, tiles_of(d), side_rows, col_land.at[s])

        when(has(0, d), take)
        when(
            jnp.logical_not(has(0, d)), lambda d=d, rows=rows: fill(rows, tiles_of(d), side_rows, None)
        )
    for r, dr in enumerate(steps):
        rows = part(dr, HALO, side_rows)

        def take_rows(r=r, rows=rows):
            row_copy(1 - r, 2).wait_recv()
            fill(rows, tiles_of(0), HALO, row_land.at[r])

        when(has(dr, 0), take_rows)
        when(
            jnp.logical_not(has(dr, 0)), lambda rows=rows: fill(rows, tiles_of(0), HALO, None)
        )
    for r, dr in enumerate(steps):
        rows = part(dr, HALO, side_rows)
        for s, dc in enumerate(steps):

            def take_corner(r=r, s=s, dc=dc, rows=rows):
                corner_copy(r, 1 - s).wait_recv()
                fill(rows, tiles_of(dc), HALO, corner_land.at[r, s])

            when(has(dr, dc), take_corner)
            when(
                jnp.logical_not(has(dr, dc)),
                lambda dc=dc, rows=rows: fill(rows, tiles_of(dc), HALO, None),
            )

    for s, d in enumerate(steps):
        for p in range(3):
            when(has(d, 0), lambda s=s, p=p: row_copy(s, p).wait_send())
        for p in range(2):
            when(has(0, d), lambda s=s, p=p: col_copy(s, p).wait_send())
        when(relays(d), lambda s=s: relay_copy(s).wait_send())
        for r, dr in enumerate(steps):
            when(has(dr, d), lambda r=r, s=s: corner_copy(r, s).wait_send())


def halo_call(object_field, probe_size):
    planes, side_rows, side_cols = object_field.shape
    kind = object_field.dtype
    vmem = pl.BlockSpec(memory_space=pltpu.VMEM)
    tiled = jax.ShapeDtypeStruct(
        (planes, (side_cols + 2 * HALO) // LANES + 1, side_rows + 2 * HALO, LANES), jnp.float32
    )
    direct = DIRECT * side_rows // 4
    return pl.pallas_call(
        halo_kernel,
        out_shape=(
            tiled,
            tiled,
            jax.ShapeDtypeStruct((probe_size // LANES, LANES), jnp.float32),
        ),
        in_specs=[pl.BlockSpec(memory_space=pltpu.HBM)],
        out_specs=3 * (vmem,),
        scratch_shapes=[
            pltpu.VMEM(object_field.shape, kind),
            pltpu.SemaphoreType.DMA,
            pltpu.VMEM((2, planes, HALO, side_cols), kind),
            pltpu.VMEM((2, planes, side_rows, HALO), kind),
            pltpu.VMEM((2, 2, planes, HALO, HALO), kind),
            pltpu.VMEM((2, planes, side_rows - direct, HALO), kind),
            pltpu.SemaphoreType.DMA((2, 6)),
            pltpu.SemaphoreType.DMA((2, 4)),
            pltpu.SemaphoreType.DMA((2, 4)),
            pltpu.SemaphoreType.DMA((2, 2)),
        ],
        compiler_params=pltpu.CompilerParams(
            collective_id=0, has_side_effects=True, vmem_limit_bytes=HALO_LIMIT * 1024 * 1024
        ),
        cost_estimate=pl.CostEstimate(flops=10**10, bytes_accessed=0, transcendentals=0),
        name="halo",
    )(pltpu.with_memory_space_constraint(object_field, pltpu.HBM))


def reduce_kernel(scale, acc_ref, pacc_ref, grad_ref, flat_ref, *scratch):
    count = len(SIDES)
    sends, landings, rest = scratch[:count], scratch[count : 2 * count], scratch[2 * count :]
    psend, pair_recv, merged, precv, sums, zbuf, full = rest[:7]
    side_sems, strip_sems, pair_sems, col_sems, row_sems = rest[7:]
    row, col, n_row, n_col = position()
    side_rows, side_cols = grad_ref.shape[1:]
    margin = HALO // LANES
    inner = side_cols // LANES
    part_rows = psend.shape[2]
    share = PARTS * part_rows
    chip, core = col // 2, lax.rem(col, 2)
    n_chip = n_col // 2
    sibling = (row, 2 * chip + 1 - core)

    barrier = pltpu.get_barrier_semaphore()
    waits = jnp.int32(n_row + n_chip - 1)
    pl.semaphore_signal(barrier, inc=1, device_id=sibling, device_id_type=MESH)
    for k in range(1, n_chip):
        peer = (row, 2 * lax.rem(chip + k, n_chip) + core)
        pl.semaphore_signal(barrier, inc=1, device_id=peer, device_id_type=MESH)
    for k in range(1, n_row):
        pl.semaphore_signal(
            barrier, inc=1, device_id=(lax.rem(row + k, n_row), col), device_id_type=MESH
        )
    for side in SIDES:
        if side[0] == 0:

            @pl.when(exists(side))
            def _(side=side):
                pl.semaphore_signal(barrier, inc=1, device_id=at_side(side), device_id_type=MESH)

            waits = waits + exists(side).astype(jnp.int32)

    def stage_side(index):
        dr, dc = SIDES[index]
        tiles = range(inner + 2 * margin)[part(dc, margin, inner)]
        for k, t in enumerate(tiles):
            sends[index][:, k] = acc_ref[:, t, part(dr, HALO, side_rows), :].astype(jnp.bfloat16)

    def stage_sides(chosen):
        for index, side in enumerate(SIDES):
            if chosen(side):
                stage_side(index)

    def to_peer(source, landing, sems, which, k, device):
        return pltpu.make_async_remote_copy(
            src_ref=source,
            dst_ref=landing,
            send_sem=sems.at[which, k],
            recv_sem=sems.at[which + 1, k],
            device_id=device,
            device_id_type=MESH,
        )

    def chip_at(k):
        return lax.rem(chip + k, n_chip)

    def chip_from(k):
        return lax.rem(chip + n_chip - k, n_chip)

    def chip_peer(k):
        return (row, 2 * chip_at(k) + core)

    def rows_of(index, h):
        return pl.ds(pl.multiple_of(index * share + h * part_rows, part_rows), part_rows)

    def pair_copy(h, k):
        return to_peer(
            psend.at[h, k], pair_recv.at[h, k], pair_sems, 0, h * n_chip + k, sibling
        )

    def scatter_copy(h, k):
        at = h * (n_chip - 1) + k - 1
        return to_peer(merged.at[h, k - 1], precv.at[h, k - 1], col_sems, 0, at, chip_peer(k))

    def row_copy(h, k, owner):
        at = h * (n_row - 1) + k - 1
        peer = (lax.rem(row + k, n_row), col)
        return to_peer(zbuf.at[h, row], zbuf.at[h, owner], row_sems, 0, at, peer)

    def gather_copy(h, k, owner):
        at = h * (n_chip - 1) + k - 1
        source, landing = full.at[rows_of(col, h), :], full.at[rows_of(owner, h), :]
        return to_peer(source, landing, col_sems, 2, at, chip_peer(k))

    def forward_copy(h, k, side):
        source = full.at[rows_of(2 * chip_from(k) + core, h), :]
        landing = full.at[rows_of(2 * chip_from(k) + side, h), :]
        return to_peer(source, landing, pair_sems, 2, h * n_chip + k, sibling)

    def side_copy(index):
        side = (0, SIDES[index][1])
        return to_side(
            side, index, sends[index], landings[index], side_sems.at[0], side_sems.at[1]
        )

    strips = [index for index, side in enumerate(SIDES) if side[1] == 0]
    pieces = (slice(margin, inner - margin), slice(0, margin), slice(inner - margin, inner))

    def strip_copy(r, p):
        index = strips[r]
        source, landing = sends[index].at[:, pieces[p]], landings[index].at[:, pieces[p]]
        return to_peer(source, landing, strip_sems, 0, 3 * r + p, at_side(SIDES[index]))

    def start_middles():
        for r, index in enumerate(strips):
            dr = SIDES[index][0]
            for k in range(margin, inner - margin):
                sends[index][:, k] = acc_ref[:, margin + k, part(dr, HALO, side_rows), :].astype(
                    jnp.bfloat16
                )

            @pl.when(exists(SIDES[index]))
            def _(r=r):
                strip_copy(r, 0).start()

    def start_edges():
        for r, index in enumerate(strips):
            dr = SIDES[index][0]
            for p, dc in ((1, -1), (2, 1)):
                corner = SIDES.index((dr, -dc))
                tiles = range(inner)[pieces[p]]
                rows = part(dr, HALO, side_rows)

                @pl.when(exists((dr, dc)))
                def _(index=index, corner=corner, tiles=tiles, rows=rows):
                    side_copy(corner).wait_recv()
                    for k, t in enumerate(tiles):
                        own = acc_ref[:, margin + t, rows, :]
                        sends[index][:, t] = (
                            own + landings[corner][:, k].astype(jnp.float32)
                        ).astype(jnp.bfloat16)

                @pl.when(jnp.logical_and(exists((dr, 0)), jnp.logical_not(exists((0, dc)))))
                def _(index=index, tiles=tiles, rows=rows):
                    for t in tiles:
                        sends[index][:, t] = acc_ref[:, margin + t, rows, :].astype(jnp.bfloat16)

                @pl.when(exists((dr, 0)))
                def _(r=r, p=p):
                    strip_copy(r, p).start()

    def add_rows():
        for r, index in enumerate(strips):
            dr = -SIDES[index][0]
            rows = edge(dr, HALO, side_rows)

            @pl.when(exists((dr, 0)))
            def _(r=r, index=index, rows=rows):
                for p in range(3):
                    strip_copy(r, p).wait_recv()
                for t in range(inner):
                    grad_ref[:, rows, t * LANES : (t + 1) * LANES] += landings[index][
                        :, t
                    ].astype(jnp.float32)

    def start_sides(chosen):
        for index, side in enumerate(SIDES):
            if chosen(side):

                @pl.when(exists(side))
                def _(index=index):
                    side_copy(index).start()

    def add_sides(chosen):
        for index, side in enumerate(SIDES):
            if not chosen(side):
                continue
            dr, dc = opposite(side)
            rows = edge(dr, HALO, side_rows)
            tiles = range(inner)[edge(dc, margin, inner)]

            @pl.when(exists((dr, dc)))
            def _(index=index, rows=rows, tiles=tiles):
                side_copy(index).wait_recv()
                for k, t in enumerate(tiles):
                    grad_ref[:, rows, t * LANES : (t + 1) * LANES] += landings[index][
                        :, k
                    ].astype(jnp.float32)

    over_cols = lambda side: side[0] == 0
    corners = lambda side: side[0] != 0 and side[1] != 0
    order = list(range(1, n_chip)) + [0]
    for h in range(PARTS):
        for k in order:
            psend[h, k] = pacc_ref[rows_of(2 * chip_at(k) + 1 - core, h), :].astype(jnp.bfloat16)
    stage_sides(corners)
    pl.semaphore_wait(barrier, waits)
    for h in range(PARTS):
        for k in order:
            pair_copy(h, k).start()
    start_sides(corners)
    start_middles()
    stage_sides(over_cols)

    def merge(h, k):
        pair_copy(h, k).wait_recv()
        own = pacc_ref[rows_of(2 * chip_at(k) + core, h), :]
        return own + pair_recv[h, k].astype(jnp.float32)

    for h in range(PARTS):
        for k in range(1, n_chip):
            merged[h, k - 1] = merge(h, k).astype(jnp.bfloat16)
            scatter_copy(h, k).start()
        sums[h] = merge(h, 0)
    start_edges()
    start_sides(over_cols)
    for t in range(inner):
        grad_ref[:, :, t * LANES : (t + 1) * LANES] = acc_ref[
            :, margin + t, HALO : HALO + side_rows, :
        ]
    for h in range(PARTS):
        total = sums[h]
        for k in range(1, n_chip):
            scatter_copy(h, k).wait_recv()
            total = total + precv[h, k - 1].astype(jnp.float32)
        zbuf[h, row] = total.astype(jnp.bfloat16)
        for k in range(1, n_row):
            row_copy(h, k, row).start()
    for h in range(PARTS):
        for k in range(1, n_row):
            row_copy(h, k, lax.rem(row + n_row - k, n_row)).wait_recv()
        total = zbuf[h, 0].astype(jnp.float32)
        for k in range(1, n_row):
            total = total + zbuf[h, k].astype(jnp.float32)
        full[rows_of(col, h), :] = (total * scale).astype(jnp.bfloat16)
        for k in range(1, n_chip):
            gather_copy(h, k, col).start()
        forward_copy(h, 0, core).start()

    def unpack(h, k, side):
        rows = rows_of(2 * chip_from(k) + side, h)
        flat_ref[rows, :] = full[rows, :].astype(jnp.float32)

    add_rows()
    add_sides(over_cols)
    for h in range(PARTS):
        unpack(h, 0, core)
        for k in range(1, n_chip):
            gather_copy(h, k, 2 * chip_from(k) + core).wait_recv()
            forward_copy(h, k, core).start()
            unpack(h, k, core)
    for h in range(PARTS):
        for k in range(n_chip):
            forward_copy(h, k, 1 - core).wait_recv()
            unpack(h, k, 1 - core)
    for h in range(PARTS):
        for k in range(1, n_chip):
            scatter_copy(h, k).wait_send()
            gather_copy(h, k, col).wait_send()
        for k in range(n_chip):
            pair_copy(h, k).wait_send()
            forward_copy(h, k, core).wait_send()
        for k in range(1, n_row):
            row_copy(h, k, row).wait_send()
    for index, side in enumerate(SIDES):

        @pl.when(exists(side))
        def _(index=index):
            if index in strips:
                for p in range(3):
                    strip_copy(strips.index(index), p).wait_send()
            else:
                side_copy(index).wait_send()


def reduce_call(acc, probe_flat, object_shape, scale):
    n_row, n_col = lax.axis_size("row"), lax.axis_size("col")
    _, side_rows, side_cols = object_shape
    inner = side_cols // LANES
    margin = HALO // LANES
    vmem = pl.BlockSpec(memory_space=pltpu.VMEM)
    buffers = []
    for dr, dc in SIDES:
        buffers.append(
            pltpu.VMEM(
                (2, margin if dc else inner, HALO if dr else side_rows, LANES), jnp.bfloat16
            )
        )
    total_rows = probe_flat.shape[0]
    piece = total_rows // n_col // PARTS
    n_chip = n_col // 2
    return pl.pallas_call(
        functools.partial(reduce_kernel, scale),
        out_shape=(
            jax.ShapeDtypeStruct(object_shape, jnp.float32),
            jax.ShapeDtypeStruct(probe_flat.shape, jnp.float32),
        ),
        in_specs=[vmem, vmem],
        out_specs=(vmem, vmem),
        scratch_shapes=buffers
        + buffers
        + [
            pltpu.VMEM((PARTS, n_chip, piece, LANES), jnp.bfloat16),
            pltpu.VMEM((PARTS, n_chip, piece, LANES), jnp.bfloat16),
            pltpu.VMEM((PARTS, n_chip - 1, piece, LANES), jnp.bfloat16),
            pltpu.VMEM((PARTS, n_chip - 1, piece, LANES), jnp.bfloat16),
            pltpu.VMEM((PARTS, piece, LANES), jnp.float32),
            pltpu.VMEM((PARTS, n_row, piece, LANES), jnp.bfloat16),
            pltpu.VMEM((total_rows, LANES), jnp.bfloat16),
            pltpu.SemaphoreType.DMA((2, len(SIDES))),
            pltpu.SemaphoreType.DMA((2, 6)),
            pltpu.SemaphoreType.DMA((4, PARTS * n_chip)),
            pltpu.SemaphoreType.DMA((4, PARTS * (n_chip - 1))),
            pltpu.SemaphoreType.DMA((2, PARTS * (n_row - 1))),
        ],
        compiler_params=pltpu.CompilerParams(
            collective_id=1, has_side_effects=True, vmem_limit_bytes=20 * 1024 * 1024
        ),
        name="reduce",
    )(acc, probe_flat)


def write_kernel(grad_in, flat_ref, grad_ref, probe_ref, sems):
    parts, modes, fs, width = probe_ref.shape
    copies = []
    for p in range(parts):
        for m in range(modes):
            for t in range(width // LANES):
                at = len(copies) * fs
                target = probe_ref.at[p, m, :, t * LANES : (t + 1) * LANES]
                sem = sems.at[len(copies)]
                copies.append(pltpu.make_async_copy(flat_ref.at[at : at + fs, :], target, sem))
    for p in range(grad_in.shape[0]):
        copies.append(pltpu.make_async_copy(grad_in.at[p], grad_ref.at[p], sems.at[len(copies)]))
    for copy in copies:
        copy.start()
    for copy in copies:
        copy.wait()


def write_call(grad, probe_flat, probe_shape):
    vmem = pl.BlockSpec(memory_space=pltpu.VMEM)
    hbm = pl.BlockSpec(memory_space=pltpu.HBM)
    count = probe_flat.shape[0] // probe_shape[2] + grad.shape[0]
    return pl.pallas_call(
        write_kernel,
        out_shape=(
            jax.ShapeDtypeStruct(grad.shape, grad.dtype),
            jax.ShapeDtypeStruct(probe_shape, jnp.float32),
        ),
        in_specs=[vmem, vmem],
        out_specs=(hbm, hbm),
        scratch_shapes=[pltpu.SemaphoreType.DMA((count,))],
        compiler_params=pltpu.CompilerParams(vmem_limit_bytes=8 * 1024 * 1024),
        name="write",
    )(grad, probe_flat)


def fourier_tables(frame_side):
    indices = np.arange(frame_side)
    product = indices[:, None] * indices[None, :] % frame_side
    angles = 2.0 * math.pi / frame_side * product
    norm_scale = 1.0 / math.sqrt(frame_side)
    real, imag = np.cos(angles) * norm_scale, -np.sin(angles) * norm_scale
    tables = (np.block([[real, -imag], [imag, real]]), np.block([[real, imag], [-imag, real]]))
    return tuple(jnp.asarray(table.astype(np.float32)).astype(jnp.bfloat16) for table in tables)


CHUNK = 32


def dot32(left, right):
    return jnp.dot(left, right, preferred_element_type=jnp.float32)


def frames_kernel(
    count_ref, at_ref, ext_ref, probe_ref, amp_ref, fwd, inv, zero_ref, pzero_ref,
    acc_ref, pacc_ref, *buffers,
):
    fs = probe_ref.shape[-1]
    modes = probe_ref.shape[1]
    lane_tiles = fs // LANES
    last_slot = amp_ref.shape[0] - 1
    live = count_ref[0, 0]
    even, odd = buffers[:4], buffers[4:]
    odd[2][...] = jnp.zeros(odd[2].shape, jnp.float32)
    odd[3][...] = jnp.zeros(odd[3].shape, jnp.float32)

    def two_sided(buffer, left_table, right_table):
        stage, half, wide, _ = buffer
        for m in range(modes):
            both = dot32(left_table[...], stage[:, m * fs : (m + 1) * fs])
            half[m * fs : (m + 1) * fs, :fs] = both[:fs].astype(jnp.bfloat16)
            half[m * fs : (m + 1) * fs, fs:] = both[fs:].astype(jnp.bfloat16)
        wide[...] = dot32(half[...], right_table[...])

    def make_exit(buffer, slot):
        stage, _, _, patch = buffer
        row_at = at_ref[0, slot]
        col_at = at_ref[1, slot]
        tile_at = col_at // LANES
        shift = col_at % LANES
        back_shift = (LANES - shift) % LANES
        lane = lax.broadcasted_iota(jnp.int32, (CHUNK, LANES), 1)
        keep_low = lane < LANES - shift
        for r in range(0, fs, CHUNK):
            rows = slice(r, r + CHUNK)
            values = []
            for plane in range(2):
                rolled = [
                    pltpu.roll(
                        ext_ref[plane, tile_at + t, pl.ds(row_at + r, CHUNK), :], back_shift, 1
                    )
                    for t in range(lane_tiles + 1)
                ]
                values.append(
                    [jnp.where(keep_low, rolled[t], rolled[t + 1]) for t in range(lane_tiles)]
                )
            for t in range(lane_tiles):
                cols = slice(t * LANES, (t + 1) * LANES)
                patch_real, patch_imag = values[0][t], values[1][t]
                patch[0, rows, cols] = patch_real
                patch[1, rows, cols] = patch_imag
                for m in range(modes):
                    probe_real = probe_ref[0, m, rows, cols]
                    probe_imag = probe_ref[1, m, rows, cols]
                    out = slice(m * fs + t * LANES, m * fs + (t + 1) * LANES)
                    stage[rows, out] = (
                        probe_real * patch_real - probe_imag * patch_imag
                    ).astype(jnp.bfloat16)
                    stage[fs + r : fs + r + CHUNK, out] = (
                        probe_real * patch_imag + probe_imag * patch_real
                    ).astype(jnp.bfloat16)

    def make_chi(buffer, slot, valid):
        stage, _, wide, _ = buffer
        for r in range(0, fs, CHUNK):
            for t in range(lane_tiles):
                cols = slice(t * LANES, (t + 1) * LANES)
                imag_cols = slice(fs + t * LANES, fs + (t + 1) * LANES)
                psi = []
                power = None
                for m in range(modes):
                    rows = slice(m * fs + r, m * fs + r + CHUNK)
                    real, imag = wide[rows, cols], wide[rows, imag_cols]
                    psi.append((real, imag))
                    own = real * real + imag * imag
                    power = own if power is None else power + own
                amp = amp_ref[slot, r : r + CHUNK, cols].astype(jnp.float32)
                factor = 1.0 - amp * lax.rsqrt(jnp.maximum(power, 0.25))
                if valid is not None:
                    factor = jnp.where(valid, factor, 0.0)
                for m in range(modes):
                    out = slice(m * fs + t * LANES, m * fs + (t + 1) * LANES)
                    stage[r : r + CHUNK, out] = (psi[m][0] * factor).astype(jnp.bfloat16)
                    stage[fs + r : fs + r + CHUNK, out] = (psi[m][1] * factor).astype(jnp.bfloat16)

    def add_grads(buffer, slot):
        _, _, wide, patch = buffer
        row_at = at_ref[0, slot]
        col_at = at_ref[1, slot]
        tile_at = col_at // LANES
        shift = col_at % LANES
        lane = lax.broadcasted_iota(jnp.int32, (CHUNK, LANES), 1)
        from_same = lane >= shift
        for r in range(0, fs, CHUNK):
            grads = [[], []]
            for t in range(lane_tiles):
                cols = slice(t * LANES, (t + 1) * LANES)
                imag_cols = slice(fs + t * LANES, fs + (t + 1) * LANES)
                patch_real = patch[0, r : r + CHUNK, cols]
                patch_imag = patch[1, r : r + CHUNK, cols]
                total_real = total_imag = None
                for m in range(modes):
                    rows = slice(m * fs + r, m * fs + r + CHUNK)
                    real, imag = wide[rows, cols], wide[rows, imag_cols]
                    probe_real = probe_ref[0, m, r : r + CHUNK, cols]
                    probe_imag = probe_ref[1, m, r : r + CHUNK, cols]
                    own_real = probe_real * real + probe_imag * imag
                    own_imag = probe_real * imag - probe_imag * real
                    total_real = own_real if m == 0 else total_real + own_real
                    total_imag = own_imag if m == 0 else total_imag + own_imag
                    at = (m * lane_tiles + t) * fs + r
                    pacc_ref[at : at + CHUNK, :] += patch_real * real + patch_imag * imag
                    at += modes * lane_tiles * fs
                    pacc_ref[at : at + CHUNK, :] += patch_real * imag - patch_imag * real
                grads[0].append(pltpu.roll(total_real, shift, 1))
                grads[1].append(pltpu.roll(total_imag, shift, 1))
            for plane in range(2):
                rolled = grads[plane]
                for t in range(lane_tiles + 1):
                    same = rolled[t] if t < lane_tiles else 0.0
                    before = rolled[t - 1] if t > 0 else 0.0
                    where = (plane, tile_at + t, pl.ds(row_at + r, CHUNK), slice(None))
                    acc_ref[where] += jnp.where(from_same, same, before)

    def advance(pair, carry):
        first = 2 * pair
        second = jnp.minimum(first + 1, last_slot)
        make_exit(even, first)
        two_sided(even, fwd, inv)
        add_grads(odd, jnp.maximum(first - 1, 0))
        make_exit(odd, second)
        two_sided(odd, fwd, inv)
        make_chi(even, first, None)
        two_sided(even, inv, fwd)
        make_chi(odd, second, first + 1 < live)
        two_sided(odd, inv, fwd)
        add_grads(even, first)
        return carry

    pairs = (live + 1) // 2
    lax.fori_loop(0, pairs, advance, 0)
    add_grads(odd, jnp.minimum(2 * pairs - 1, last_slot))


def frames_call(extended, zeros, probe_modes, amplitudes, positions, live_count, tables):
    fs = probe_modes.shape[-1]
    modes = probe_modes.shape[1]
    tiled = extended.shape
    vmem = pl.BlockSpec(memory_space=pltpu.VMEM)
    smem = pl.BlockSpec(memory_space=pltpu.SMEM)
    return pl.pallas_call(
        frames_kernel,
        out_shape=(
            jax.ShapeDtypeStruct(tiled, jnp.float32),
            jax.ShapeDtypeStruct((probe_modes.size // LANES, LANES), jnp.float32),
        ),
        in_specs=[smem, smem] + 7 * [vmem],
        out_specs=(vmem, vmem),
        input_output_aliases={7: 0, 8: 1},
        scratch_shapes=2
        * [
            pltpu.VMEM((2 * fs, modes * fs), jnp.bfloat16),
            pltpu.VMEM((modes * fs, 2 * fs), jnp.bfloat16),
            pltpu.VMEM((modes * fs, 2 * fs), jnp.float32),
            pltpu.VMEM((2, fs, fs), jnp.float32),
        ],
        compiler_params=pltpu.CompilerParams(vmem_limit_bytes=26 * 1024 * 1024),
        name="frames",
    )(live_count, positions, extended, probe_modes, amplitudes, *tables, *zeros)


def shards(object_field, probe_modes, measured_amp, scan_positions, frame_counts):
    slot_count = measured_amp.shape[2]
    extended, *zeros = halo_call(object_field, probe_modes.size)
    acc, probe_flat = frames_call(
        extended,
        zeros,
        probe_modes,
        measured_amp[0, 0],
        scan_positions[0, 0],
        frame_counts,
        fourier_tables(probe_modes.shape[-1]),
    )
    norm_scale = 1.0 / math.sqrt(lax.axis_size("row") * lax.axis_size("col") * slot_count)
    grad, probe_sum = reduce_call(acc, probe_flat, object_field.shape, norm_scale)
    return write_call(grad, probe_sum, probe_modes.shape)


def solution(mesh):
    in_specs = (
        P(None, "row", "col"),
        P(),
        P("row", "col", None, None, None),
        P("row", "col", None, None),
        P("row", "col"),
    )
    out_specs = (P(None, "row", "col"), P())
    return jax.shard_map(shards, mesh=mesh, in_specs=in_specs, out_specs=out_specs, check_vma=False)
```

```python
import functools
import math

import jax
import jax.numpy as jnp
import numpy as np
from jax import lax
from jax.experimental import pallas as pl
from jax.experimental.pallas import tpu as pltpu
from jax.sharding import PartitionSpec as P

HALO = 128
LANES = 128
PARTS = 2
HALO_LIMIT = 20


MESH = pl.DeviceIdType.MESH
SIDES = [(dr, dc) for dr in (-1, 0, 1) for dc in (-1, 0, 1) if (dr, dc) != (0, 0)]


def position():
    return (
        lax.axis_index("row"),
        lax.axis_index("col"),
        lax.axis_size("row"),
        lax.axis_size("col"),
    )


def exists(side):
    row, col, rows, cols = position()
    dr, dc = side
    inside = jnp.bool_(True)
    if dr:
        inside = row + dr >= 0 if dr < 0 else row + dr < rows
    if dc:
        other = col + dc >= 0 if dc < 0 else col + dc < cols
        inside = jnp.logical_and(inside, other) if dr else other
    return inside


def at_side(side):
    row, col, _, _ = position()
    return (row + side[0], col + side[1])


def opposite(side):
    return (-side[0], -side[1])


def part(step, margin, inner):
    return {-1: slice(0, margin), 0: slice(margin, margin + inner), 1: slice(margin + inner, None)}[
        step
    ]


def edge(step, margin, inner):
    return {-1: slice(0, margin), 0: slice(0, inner), 1: slice(inner - margin, inner)}[step]


def to_side(side, index, source, landing, send_sems, recv_sems):
    return pltpu.make_async_remote_copy(
        src_ref=source,
        dst_ref=landing,
        send_sem=send_sems.at[index],
        recv_sem=recv_sems.at[index],
        device_id=at_side(side),
        device_id_type=MESH,
    )


DIRECT = 2


def halo_kernel(whole_ref, ext_ref, acc_ref, pacc_ref, *scratch):
    object_ref, load_sem, row_land, col_land, corner_land, relay_land = scratch[:6]
    row_sems, col_sems, corner_sems, relay_sems = scratch[6:]
    row, col, n_row, n_col = position()
    side_rows, side_cols = object_ref.shape[1:]
    load = pltpu.make_async_copy(whole_ref, object_ref, load_sem)
    load.start()
    steps = (-1, 1)
    pieces = (slice(0, HALO), slice(side_cols - HALO, side_cols), slice(HALO, side_cols - HALO))
    direct = DIRECT * side_rows // 4
    parts = (slice(0, direct), slice(direct, side_rows))

    def has(dr, dc):
        return exists((dr, dc))

    def turns(d):
        return jnp.logical_and(has(0, d), lax.rem(col, 4) == (3 if d > 0 else 0))

    def relays(d):
        other = col - 3 * d
        inside = jnp.logical_and(other >= 0, other < n_col)
        return jnp.logical_and(inside, lax.rem(col, 4) == (2 if d > 0 else 1))

    def lands_by_relay(d):
        return jnp.logical_and(has(0, -d), lax.rem(col, 4) == (0 if d > 0 else 3))

    links = []
    for d in steps:
        links.append((has(d, 0), (row + d, col)))
        links.append((has(0, d), (row, col + d)))
        links.append((turns(d), (row, col + 3 * d)))
        links.append((relays(d), (row, col - 3 * d)))
        links.append((relays(d), (row, col - 2 * d)))
        links.append((lands_by_relay(d), (row, col + 2 * d)))
    barrier = pltpu.get_barrier_semaphore()
    count = jnp.int32(0)
    for there, device in links:

        @pl.when(there)
        def _(device=device):
            pl.semaphore_signal(barrier, inc=1, device_id=device, device_id_type=MESH)

        count = count + there.astype(jnp.int32)
    pl.semaphore_wait(barrier, count)

    def remote(source, landing, sems, index, device):
        return pltpu.make_async_remote_copy(
            src_ref=source,
            dst_ref=landing,
            send_sem=sems.at[0, index],
            recv_sem=sems.at[1, index],
            device_id=device,
            device_id_type=MESH,
        )

    def row_copy(s, p):
        d = steps[s]
        source = whole_ref.at[:, edge(d, HALO, side_rows), pieces[p]]
        return remote(
            source, row_land.at[1 - s, :, :, pieces[p]], row_sems, 3 * s + p, (row + d, col)
        )

    def col_copy(s, p, to_relay=False):
        d = steps[s]
        source = whole_ref.at[:, parts[p], edge(d, HALO, side_cols)]
        if to_relay:
            return pltpu.make_async_remote_copy(
                src_ref=source,
                dst_ref=relay_land.at[s],
                send_sem=col_sems.at[0, 2 * s + p],
                recv_sem=relay_sems.at[1, s],
                device_id=(row, col + 3 * d),
                device_id_type=MESH,
            )
        return remote(
            source, col_land.at[1 - s, :, parts[p], :], col_sems, 2 * s + p, (row, col + d)
        )

    def relay_copy(s):
        d = steps[s]
        return pltpu.make_async_remote_copy(
            src_ref=relay_land.at[s],
            dst_ref=col_land.at[1 - s, :, parts[1], :],
            send_sem=relay_sems.at[0, s],
            recv_sem=col_sems.at[1, 2 * s + 1],
            device_id=(row, col - 2 * d),
            device_id_type=MESH,
        )

    def corner_copy(r, s):
        source = row_land.at[r, :, :, pieces[s]]
        return remote(
            source, corner_land.at[r, 1 - s], corner_sems, 2 * r + s, (row, col + steps[s])
        )

    def when(condition, action):
        @pl.when(condition)
        def _():
            action()

    for p in range(2):
        for s, d in enumerate(steps):
            when(has(d, 0), lambda s=s, p=p: row_copy(s, p).start())
    for p in (1, 0):
        for s, d in enumerate(steps):
            if p:
                when(turns(d), lambda s=s: col_copy(s, 1, True).start())
                straight = jnp.logical_and(has(0, d), jnp.logical_not(turns(d)))
                when(straight, lambda s=s: col_copy(s, 1).start())
            else:
                when(has(0, d), lambda s=s: col_copy(s, 0).start())
    for s, d in enumerate(steps):
        when(has(d, 0), lambda s=s: row_copy(s, 2).start())

    acc_ref[...] = jnp.zeros(acc_ref.shape, jnp.float32)
    pacc_ref[...] = jnp.zeros(pacc_ref.shape, jnp.float32)
    spare = ext_ref.shape[1] - 1
    ext_ref[:, spare] = jnp.zeros((2, ext_ref.shape[2], LANES), jnp.float32)
    margin, inner = HALO // LANES, side_cols // LANES

    def tiles_of(d):
        return range(spare)[part(d, margin, inner)]

    def fill(rows, tiles, height, source):
        for k, t in enumerate(tiles):
            if source is None:
                ext_ref[:, t, rows, :] = jnp.zeros((2, height, LANES), ext_ref.dtype)
            else:
                ext_ref[:, t, rows, :] = source[:, :, k * LANES : (k + 1) * LANES].astype(
                    jnp.float32
                )

    load.wait()
    fill(part(0, HALO, side_rows), tiles_of(0), side_rows, object_ref)

    for s, d in enumerate(steps):

        def pass_on(s=s):
            relay_copy_in = col_copy(s, 1, True)
            relay_copy_in.wait_recv()
            relay_copy(s).start()

        when(relays(d), pass_on)
    for r, dr in enumerate(steps):
        for s, dc in enumerate(steps):

            def hand_over(r=r, s=s, dc=dc):
                row_copy(1 - r, s).wait_recv()
                when(has(0, dc), lambda: corner_copy(r, s).start())

            when(has(dr, 0), hand_over)
    for s, d in enumerate(steps):
        rows = part(0, HALO, side_rows)
        here = s

        def take(s=s, d=d, rows=rows):
            col_copy(1 - s, 0).wait_recv()
            col_copy(1 - s, 1).wait_recv()
            fill(rows, tiles_of(d), side_rows, col_land.at[s])

        when(has(0, d), take)
        when(
            jnp.logical_not(has(0, d)), lambda d=d, rows=rows: fill(rows, tiles_of(d), side_rows, None)
        )
    for r, dr in enumerate(steps):
        rows = part(dr, HALO, side_rows)

        def take_rows(r=r, rows=rows):
            row_copy(1 - r, 2).wait_recv()
            fill(rows, tiles_of(0), HALO, row_land.at[r])

        when(has(dr, 0), take_rows)
        when(
            jnp.logical_not(has(dr, 0)), lambda rows=rows: fill(rows, tiles_of(0), HALO, None)
        )
    for r, dr in enumerate(steps):
        rows = part(dr, HALO, side_rows)
        for s, dc in enumerate(steps):

            def take_corner(r=r, s=s, dc=dc, rows=rows):
                corner_copy(r, 1 - s).wait_recv()
                fill(rows, tiles_of(dc), HALO, corner_land.at[r, s])

            when(has(dr, dc), take_corner)
            when(
                jnp.logical_not(has(dr, dc)),
                lambda dc=dc, rows=rows: fill(rows, tiles_of(dc), HALO, None),
            )

    for s, d in enumerate(steps):
        for p in range(3):
            when(has(d, 0), lambda s=s, p=p: row_copy(s, p).wait_send())
        for p in range(2):
            when(has(0, d), lambda s=s, p=p: col_copy(s, p).wait_send())
        when(relays(d), lambda s=s: relay_copy(s).wait_send())
        for r, dr in enumerate(steps):
            when(has(dr, d), lambda r=r, s=s: corner_copy(r, s).wait_send())


def halo_call(object_field, probe_size):
    planes, side_rows, side_cols = object_field.shape
    kind = object_field.dtype
    vmem = pl.BlockSpec(memory_space=pltpu.VMEM)
    tiled = jax.ShapeDtypeStruct(
        (planes, (side_cols + 2 * HALO) // LANES + 1, side_rows + 2 * HALO, LANES), jnp.float32
    )
    direct = DIRECT * side_rows // 4
    return pl.pallas_call(
        halo_kernel,
        out_shape=(
            tiled,
            tiled,
            jax.ShapeDtypeStruct((probe_size // LANES, LANES), jnp.float32),
        ),
        in_specs=[pl.BlockSpec(memory_space=pltpu.HBM)],
        out_specs=3 * (vmem,),
        scratch_shapes=[
            pltpu.VMEM(object_field.shape, kind),
            pltpu.SemaphoreType.DMA,
            pltpu.VMEM((2, planes, HALO, side_cols), kind),
            pltpu.VMEM((2, planes, side_rows, HALO), kind),
            pltpu.VMEM((2, 2, planes, HALO, HALO), kind),
            pltpu.VMEM((2, planes, side_rows - direct, HALO), kind),
            pltpu.SemaphoreType.DMA((2, 6)),
            pltpu.SemaphoreType.DMA((2, 4)),
            pltpu.SemaphoreType.DMA((2, 4)),
            pltpu.SemaphoreType.DMA((2, 2)),
        ],
        compiler_params=pltpu.CompilerParams(
            collective_id=0, has_side_effects=True, vmem_limit_bytes=HALO_LIMIT * 1024 * 1024
        ),
        cost_estimate=pl.CostEstimate(flops=10**10, bytes_accessed=0, transcendentals=0),
        name="halo",
    )(pltpu.with_memory_space_constraint(object_field, pltpu.HBM))


def reduce_kernel(scale, acc_ref, pacc_ref, grad_ref, flat_ref, *scratch):
    count = len(SIDES)
    sends, landings, rest = scratch[:count], scratch[count : 2 * count], scratch[2 * count :]
    psend, pair_recv, merged, precv, sums, zbuf, full = rest[:7]
    side_sems, strip_sems, pair_sems, col_sems, row_sems = rest[7:]
    row, col, n_row, n_col = position()
    side_rows, side_cols = grad_ref.shape[1:]
    margin = HALO // LANES
    inner = side_cols // LANES
    part_rows = psend.shape[2]
    share = PARTS * part_rows
    chip, core = col // 2, lax.rem(col, 2)
    n_chip = n_col // 2
    sibling = (row, 2 * chip + 1 - core)

    barrier = pltpu.get_barrier_semaphore()
    waits = jnp.int32(n_row + n_chip - 1)
    pl.semaphore_signal(barrier, inc=1, device_id=sibling, device_id_type=MESH)
    for k in range(1, n_chip):
        peer = (row, 2 * lax.rem(chip + k, n_chip) + core)
        pl.semaphore_signal(barrier, inc=1, device_id=peer, device_id_type=MESH)
    for k in range(1, n_row):
        pl.semaphore_signal(
            barrier, inc=1, device_id=(lax.rem(row + k, n_row), col), device_id_type=MESH
        )
    for side in SIDES:
        if side[0] == 0:

            @pl.when(exists(side))
            def _(side=side):
                pl.semaphore_signal(barrier, inc=1, device_id=at_side(side), device_id_type=MESH)

            waits = waits + exists(side).astype(jnp.int32)

    def stage_side(index):
        dr, dc = SIDES[index]
        tiles = range(inner + 2 * margin)[part(dc, margin, inner)]
        for k, t in enumerate(tiles):
            sends[index][:, k] = acc_ref[:, t, part(dr, HALO, side_rows), :].astype(jnp.bfloat16)

    def stage_sides(chosen):
        for index, side in enumerate(SIDES):
            if chosen(side):
                stage_side(index)

    def to_peer(source, landing, sems, which, k, device):
        return pltpu.make_async_remote_copy(
            src_ref=source,
            dst_ref=landing,
            send_sem=sems.at[which, k],
            recv_sem=sems.at[which + 1, k],
            device_id=device,
            device_id_type=MESH,
        )

    def chip_at(k):
        return lax.rem(chip + k, n_chip)

    def chip_from(k):
        return lax.rem(chip + n_chip - k, n_chip)

    def chip_peer(k):
        return (row, 2 * chip_at(k) + core)

    def rows_of(index, h):
        return pl.ds(pl.multiple_of(index * share + h * part_rows, part_rows), part_rows)

    def pair_copy(h, k):
        return to_peer(
            psend.at[h, k], pair_recv.at[h, k], pair_sems, 0, h * n_chip + k, sibling
        )

    def scatter_copy(h, k):
        at = h * (n_chip - 1) + k - 1
        return to_peer(merged.at[h, k - 1], precv.at[h, k - 1], col_sems, 0, at, chip_peer(k))

    def row_copy(h, k, owner):
        at = h * (n_row - 1) + k - 1
        peer = (lax.rem(row + k, n_row), col)
        return to_peer(zbuf.at[h, row], zbuf.at[h, owner], row_sems, 0, at, peer)

    def gather_copy(h, k, owner):
        at = h * (n_chip - 1) + k - 1
        source, landing = full.at[rows_of(col, h), :], full.at[rows_of(owner, h), :]
        return to_peer(source, landing, col_sems, 2, at, chip_peer(k))

    def forward_copy(h, k, side):
        source = full.at[rows_of(2 * chip_from(k) + core, h), :]
        landing = full.at[rows_of(2 * chip_from(k) + side, h), :]
        return to_peer(source, landing, pair_sems, 2, h * n_chip + k, sibling)

    def side_copy(index):
        side = (0, SIDES[index][1])
        return to_side(
            side, index, sends[index], landings[index], side_sems.at[0], side_sems.at[1]
        )

    strips = [index for index, side in enumerate(SIDES) if side[1] == 0]
    pieces = (slice(margin, inner - margin), slice(0, margin), slice(inner - margin, inner))

    def strip_copy(r, p):
        index = strips[r]
        source, landing = sends[index].at[:, pieces[p]], landings[index].at[:, pieces[p]]
        return to_peer(source, landing, strip_sems, 0, 3 * r + p, at_side(SIDES[index]))

    def start_middles():
        for r, index in enumerate(strips):
            dr = SIDES[index][0]
            for k in range(margin, inner - margin):
                sends[index][:, k] = acc_ref[:, margin + k, part(dr, HALO, side_rows), :].astype(
                    jnp.bfloat16
                )

            @pl.when(exists(SIDES[index]))
            def _(r=r):
                strip_copy(r, 0).start()

    def start_edges():
        for r, index in enumerate(strips):
            dr = SIDES[index][0]
            for p, dc in ((1, -1), (2, 1)):
                corner = SIDES.index((dr, -dc))
                tiles = range(inner)[pieces[p]]
                rows = part(dr, HALO, side_rows)

                @pl.when(exists((dr, dc)))
                def _(index=index, corner=corner, tiles=tiles, rows=rows):
                    side_copy(corner).wait_recv()
                    for k, t in enumerate(tiles):
                        own = acc_ref[:, margin + t, rows, :]
                        sends[index][:, t] = (
                            own + landings[corner][:, k].astype(jnp.float32)
                        ).astype(jnp.bfloat16)

                @pl.when(jnp.logical_and(exists((dr, 0)), jnp.logical_not(exists((0, dc)))))
                def _(index=index, tiles=tiles, rows=rows):
                    for t in tiles:
                        sends[index][:, t] = acc_ref[:, margin + t, rows, :].astype(jnp.bfloat16)

                @pl.when(exists((dr, 0)))
                def _(r=r, p=p):
                    strip_copy(r, p).start()

    def add_rows():
        for r, index in enumerate(strips):
            dr = -SIDES[index][0]
            rows = edge(dr, HALO, side_rows)

            @pl.when(exists((dr, 0)))
            def _(r=r, index=index, rows=rows):
                for p in range(3):
                    strip_copy(r, p).wait_recv()
                for t in range(inner):
                    grad_ref[:, rows, t * LANES : (t + 1) * LANES] += landings[index][
                        :, t
                    ].astype(jnp.float32)

    def start_sides(chosen):
        for index, side in enumerate(SIDES):
            if chosen(side):

                @pl.when(exists(side))
                def _(index=index):
                    side_copy(index).start()

    def add_sides(chosen):
        for index, side in enumerate(SIDES):
            if not chosen(side):
                continue
            dr, dc = opposite(side)
            rows = edge(dr, HALO, side_rows)
            tiles = range(inner)[edge(dc, margin, inner)]

            @pl.when(exists((dr, dc)))
            def _(index=index, rows=rows, tiles=tiles):
                side_copy(index).wait_recv()
                for k, t in enumerate(tiles):
                    grad_ref[:, rows, t * LANES : (t + 1) * LANES] += landings[index][
                        :, k
                    ].astype(jnp.float32)

    over_cols = lambda side: side[0] == 0
    corners = lambda side: side[0] != 0 and side[1] != 0
    order = list(range(1, n_chip)) + [0]
    for h in range(PARTS):
        for k in order:
            psend[h, k] = pacc_ref[rows_of(2 * chip_at(k) + 1 - core, h), :].astype(jnp.bfloat16)
    stage_sides(corners)
    pl.semaphore_wait(barrier, waits)
    for h in range(PARTS):
        for k in order:
            pair_copy(h, k).start()
    start_middles()
    stage_sides(over_cols)

    def merge(h, k):
        pair_copy(h, k).wait_recv()
        own = pacc_ref[rows_of(2 * chip_at(k) + core, h), :]
        return own + pair_recv[h, k].astype(jnp.float32)

    for h in range(PARTS):
        for k in range(1, n_chip):
            merged[h, k - 1] = merge(h, k).astype(jnp.bfloat16)
            scatter_copy(h, k).start()
        sums[h] = merge(h, 0)
    start_sides(corners)
    start_sides(over_cols)
    for t in range(inner):
        grad_ref[:, :, t * LANES : (t + 1) * LANES] = acc_ref[
            :, margin + t, HALO : HALO + side_rows, :
        ]
    for h in range(PARTS):
        total = sums[h]
        for k in range(1, n_chip):
            scatter_copy(h, k).wait_recv()
            total = total + precv[h, k - 1].astype(jnp.float32)
        zbuf[h, row] = total.astype(jnp.bfloat16)
        for k in range(1, n_row):
            row_copy(h, k, row).start()
    start_edges()
    for h in range(PARTS):
        for k in range(1, n_row):
            row_copy(h, k, lax.rem(row + n_row - k, n_row)).wait_recv()
        total = zbuf[h, 0].astype(jnp.float32)
        for k in range(1, n_row):
            total = total + zbuf[h, k].astype(jnp.float32)
        full[rows_of(col, h), :] = (total * scale).astype(jnp.bfloat16)
        for k in range(1, n_chip):
            gather_copy(h, k, col).start()
        forward_copy(h, 0, core).start()

    def unpack(h, k, side):
        rows = rows_of(2 * chip_from(k) + side, h)
        flat_ref[rows, :] = full[rows, :].astype(jnp.float32)

    for h in range(PARTS):
        unpack(h, 0, core)
        for k in range(1, n_chip):
            gather_copy(h, k, 2 * chip_from(k) + core).wait_recv()
            forward_copy(h, k, core).start()
            unpack(h, k, core)
    add_rows()
    add_sides(over_cols)
    for h in range(PARTS):
        for k in range(n_chip):
            forward_copy(h, k, 1 - core).wait_recv()
            unpack(h, k, 1 - core)
    for h in range(PARTS):
        for k in range(1, n_chip):
            scatter_copy(h, k).wait_send()
            gather_copy(h, k, col).wait_send()
        for k in range(n_chip):
            pair_copy(h, k).wait_send()
            forward_copy(h, k, core).wait_send()
        for k in range(1, n_row):
            row_copy(h, k, row).wait_send()
    for index, side in enumerate(SIDES):

        @pl.when(exists(side))
        def _(index=index):
            if index in strips:
                for p in range(3):
                    strip_copy(strips.index(index), p).wait_send()
            else:
                side_copy(index).wait_send()


def reduce_call(acc, probe_flat, object_shape, scale):
    n_row, n_col = lax.axis_size("row"), lax.axis_size("col")
    _, side_rows, side_cols = object_shape
    inner = side_cols // LANES
    margin = HALO // LANES
    vmem = pl.BlockSpec(memory_space=pltpu.VMEM)
    buffers = []
    for dr, dc in SIDES:
        buffers.append(
            pltpu.VMEM(
                (2, margin if dc else inner, HALO if dr else side_rows, LANES), jnp.bfloat16
            )
        )
    total_rows = probe_flat.shape[0]
    piece = total_rows // n_col // PARTS
    n_chip = n_col // 2
    return pl.pallas_call(
        functools.partial(reduce_kernel, scale),
        out_shape=(
            jax.ShapeDtypeStruct(object_shape, jnp.float32),
            jax.ShapeDtypeStruct(probe_flat.shape, jnp.float32),
        ),
        in_specs=[vmem, vmem],
        out_specs=(vmem, vmem),
        scratch_shapes=buffers
        + buffers
        + [
            pltpu.VMEM((PARTS, n_chip, piece, LANES), jnp.bfloat16),
            pltpu.VMEM((PARTS, n_chip, piece, LANES), jnp.bfloat16),
            pltpu.VMEM((PARTS, n_chip - 1, piece, LANES), jnp.bfloat16),
            pltpu.VMEM((PARTS, n_chip - 1, piece, LANES), jnp.bfloat16),
            pltpu.VMEM((PARTS, piece, LANES), jnp.float32),
            pltpu.VMEM((PARTS, n_row, piece, LANES), jnp.bfloat16),
            pltpu.VMEM((total_rows, LANES), jnp.bfloat16),
            pltpu.SemaphoreType.DMA((2, len(SIDES))),
            pltpu.SemaphoreType.DMA((2, 6)),
            pltpu.SemaphoreType.DMA((4, PARTS * n_chip)),
            pltpu.SemaphoreType.DMA((4, PARTS * (n_chip - 1))),
            pltpu.SemaphoreType.DMA((2, PARTS * (n_row - 1))),
        ],
        compiler_params=pltpu.CompilerParams(
            collective_id=1, has_side_effects=True, vmem_limit_bytes=20 * 1024 * 1024
        ),
        name="reduce",
    )(acc, probe_flat)


def write_kernel(grad_in, flat_ref, grad_ref, probe_ref, sems):
    parts, modes, fs, width = probe_ref.shape
    copies = []
    for p in range(parts):
        for m in range(modes):
            for t in range(width // LANES):
                at = len(copies) * fs
                target = probe_ref.at[p, m, :, t * LANES : (t + 1) * LANES]
                sem = sems.at[len(copies)]
                copies.append(pltpu.make_async_copy(flat_ref.at[at : at + fs, :], target, sem))
    for p in range(grad_in.shape[0]):
        copies.append(pltpu.make_async_copy(grad_in.at[p], grad_ref.at[p], sems.at[len(copies)]))
    for copy in copies:
        copy.start()
    for copy in copies:
        copy.wait()


def write_call(grad, probe_flat, probe_shape):
    vmem = pl.BlockSpec(memory_space=pltpu.VMEM)
    hbm = pl.BlockSpec(memory_space=pltpu.HBM)
    count = probe_flat.shape[0] // probe_shape[2] + grad.shape[0]
    return pl.pallas_call(
        write_kernel,
        out_shape=(
            jax.ShapeDtypeStruct(grad.shape, grad.dtype),
            jax.ShapeDtypeStruct(probe_shape, jnp.float32),
        ),
        in_specs=[vmem, vmem],
        out_specs=(hbm, hbm),
        scratch_shapes=[pltpu.SemaphoreType.DMA((count,))],
        compiler_params=pltpu.CompilerParams(vmem_limit_bytes=8 * 1024 * 1024),
        name="write",
    )(grad, probe_flat)


def fourier_tables(frame_side):
    indices = np.arange(frame_side)
    product = indices[:, None] * indices[None, :] % frame_side
    angles = 2.0 * math.pi / frame_side * product
    norm_scale = 1.0 / math.sqrt(frame_side)
    real, imag = np.cos(angles) * norm_scale, -np.sin(angles) * norm_scale
    tables = (np.block([[real, -imag], [imag, real]]), np.block([[real, imag], [-imag, real]]))
    return tuple(jnp.asarray(table.astype(np.float32)).astype(jnp.bfloat16) for table in tables)


CHUNK = 32


def dot32(left, right):
    return jnp.dot(left, right, preferred_element_type=jnp.float32)


def frames_kernel(
    count_ref, at_ref, ext_ref, probe_ref, amp_ref, fwd, inv, zero_ref, pzero_ref,
    acc_ref, pacc_ref, *buffers,
):
    fs = probe_ref.shape[-1]
    modes = probe_ref.shape[1]
    lane_tiles = fs // LANES
    last_slot = amp_ref.shape[0] - 1
    live = count_ref[0, 0]
    even, odd = buffers[:4], buffers[4:]
    odd[2][...] = jnp.zeros(odd[2].shape, jnp.float32)
    odd[3][...] = jnp.zeros(odd[3].shape, jnp.float32)

    def two_sided(buffer, left_table, right_table):
        stage, half, wide, _ = buffer
        for m in range(modes):
            both = dot32(left_table[...], stage[:, m * fs : (m + 1) * fs])
            half[m * fs : (m + 1) * fs, :fs] = both[:fs].astype(jnp.bfloat16)
            half[m * fs : (m + 1) * fs, fs:] = both[fs:].astype(jnp.bfloat16)
        wide[...] = dot32(half[...], right_table[...])

    def make_exit(buffer, slot):
        stage, _, _, patch = buffer
        row_at = at_ref[0, slot]
        col_at = at_ref[1, slot]
        tile_at = col_at // LANES
        shift = col_at % LANES
        back_shift = (LANES - shift) % LANES
        lane = lax.broadcasted_iota(jnp.int32, (CHUNK, LANES), 1)
        keep_low = lane < LANES - shift
        for r in range(0, fs, CHUNK):
            rows = slice(r, r + CHUNK)
            values = []
            for plane in range(2):
                rolled = [
                    pltpu.roll(
                        ext_ref[plane, tile_at + t, pl.ds(row_at + r, CHUNK), :], back_shift, 1
                    )
                    for t in range(lane_tiles + 1)
                ]
                values.append(
                    [jnp.where(keep_low, rolled[t], rolled[t + 1]) for t in range(lane_tiles)]
                )
            for t in range(lane_tiles):
                cols = slice(t * LANES, (t + 1) * LANES)
                patch_real, patch_imag = values[0][t], values[1][t]
                patch[0, rows, cols] = patch_real
                patch[1, rows, cols] = patch_imag
                for m in range(modes):
                    probe_real = probe_ref[0, m, rows, cols]
                    probe_imag = probe_ref[1, m, rows, cols]
                    out = slice(m * fs + t * LANES, m * fs + (t + 1) * LANES)
                    stage[rows, out] = (
                        probe_real * patch_real - probe_imag * patch_imag
                    ).astype(jnp.bfloat16)
                    stage[fs + r : fs + r + CHUNK, out] = (
                        probe_real * patch_imag + probe_imag * patch_real
                    ).astype(jnp.bfloat16)

    def make_chi(buffer, slot, valid):
        stage, _, wide, _ = buffer
        for r in range(0, fs, CHUNK):
            for t in range(lane_tiles):
                cols = slice(t * LANES, (t + 1) * LANES)
                imag_cols = slice(fs + t * LANES, fs + (t + 1) * LANES)
                psi = []
                power = None
                for m in range(modes):
                    rows = slice(m * fs + r, m * fs + r + CHUNK)
                    real, imag = wide[rows, cols], wide[rows, imag_cols]
                    psi.append((real, imag))
                    own = real * real + imag * imag
                    power = own if power is None else power + own
                amp = amp_ref[slot, r : r + CHUNK, cols].astype(jnp.float32)
                factor = 1.0 - amp * lax.rsqrt(jnp.maximum(power, 0.25))
                if valid is not None:
                    factor = jnp.where(valid, factor, 0.0)
                for m in range(modes):
                    out = slice(m * fs + t * LANES, m * fs + (t + 1) * LANES)
                    stage[r : r + CHUNK, out] = (psi[m][0] * factor).astype(jnp.bfloat16)
                    stage[fs + r : fs + r + CHUNK, out] = (psi[m][1] * factor).astype(jnp.bfloat16)

    def add_grads(buffer, slot):
        _, _, wide, patch = buffer
        row_at = at_ref[0, slot]
        col_at = at_ref[1, slot]
        tile_at = col_at // LANES
        shift = col_at % LANES
        lane = lax.broadcasted_iota(jnp.int32, (CHUNK, LANES), 1)
        from_same = lane >= shift
        for r in range(0, fs, CHUNK):
            grads = [[], []]
            for t in range(lane_tiles):
                cols = slice(t * LANES, (t + 1) * LANES)
                imag_cols = slice(fs + t * LANES, fs + (t + 1) * LANES)
                patch_real = patch[0, r : r + CHUNK, cols]
                patch_imag = patch[1, r : r + CHUNK, cols]
                total_real = total_imag = None
                for m in range(modes):
                    rows = slice(m * fs + r, m * fs + r + CHUNK)
                    real, imag = wide[rows, cols], wide[rows, imag_cols]
                    probe_real = probe_ref[0, m, r : r + CHUNK, cols]
                    probe_imag = probe_ref[1, m, r : r + CHUNK, cols]
                    own_real = probe_real * real + probe_imag * imag
                    own_imag = probe_real * imag - probe_imag * real
                    total_real = own_real if m == 0 else total_real + own_real
                    total_imag = own_imag if m == 0 else total_imag + own_imag
                    at = (m * lane_tiles + t) * fs + r
                    pacc_ref[at : at + CHUNK, :] += patch_real * real + patch_imag * imag
                    at += modes * lane_tiles * fs
                    pacc_ref[at : at + CHUNK, :] += patch_real * imag - patch_imag * real
                grads[0].append(pltpu.roll(total_real, shift, 1))
                grads[1].append(pltpu.roll(total_imag, shift, 1))
            for plane in range(2):
                rolled = grads[plane]
                for t in range(lane_tiles + 1):
                    same = rolled[t] if t < lane_tiles else 0.0
                    before = rolled[t - 1] if t > 0 else 0.0
                    where = (plane, tile_at + t, pl.ds(row_at + r, CHUNK), slice(None))
                    acc_ref[where] += jnp.where(from_same, same, before)

    def advance(pair, carry):
        first = 2 * pair
        second = jnp.minimum(first + 1, last_slot)
        make_exit(even, first)
        two_sided(even, fwd, inv)
        add_grads(odd, jnp.maximum(first - 1, 0))
        make_exit(odd, second)
        two_sided(odd, fwd, inv)
        make_chi(even, first, None)
        two_sided(even, inv, fwd)
        make_chi(odd, second, first + 1 < live)
        two_sided(odd, inv, fwd)
        add_grads(even, first)
        return carry

    pairs = (live + 1) // 2
    lax.fori_loop(0, pairs, advance, 0)
    add_grads(odd, jnp.minimum(2 * pairs - 1, last_slot))


def frames_call(extended, zeros, probe_modes, amplitudes, positions, live_count, tables):
    fs = probe_modes.shape[-1]
    modes = probe_modes.shape[1]
    tiled = extended.shape
    vmem = pl.BlockSpec(memory_space=pltpu.VMEM)
    smem = pl.BlockSpec(memory_space=pltpu.SMEM)
    return pl.pallas_call(
        frames_kernel,
        out_shape=(
            jax.ShapeDtypeStruct(tiled, jnp.float32),
            jax.ShapeDtypeStruct((probe_modes.size // LANES, LANES), jnp.float32),
        ),
        in_specs=[smem, smem] + 7 * [vmem],
        out_specs=(vmem, vmem),
        input_output_aliases={7: 0, 8: 1},
        scratch_shapes=2
        * [
            pltpu.VMEM((2 * fs, modes * fs), jnp.bfloat16),
            pltpu.VMEM((modes * fs, 2 * fs), jnp.bfloat16),
            pltpu.VMEM((modes * fs, 2 * fs), jnp.float32),
            pltpu.VMEM((2, fs, fs), jnp.float32),
        ],
        compiler_params=pltpu.CompilerParams(vmem_limit_bytes=26 * 1024 * 1024),
        name="frames",
    )(live_count, positions, extended, probe_modes, amplitudes, *tables, *zeros)


def shards(object_field, probe_modes, measured_amp, scan_positions, frame_counts):
    slot_count = measured_amp.shape[2]
    extended, *zeros = halo_call(object_field, probe_modes.size)
    acc, probe_flat = frames_call(
        extended,
        zeros,
        probe_modes,
        measured_amp[0, 0],
        scan_positions[0, 0],
        frame_counts,
        fourier_tables(probe_modes.shape[-1]),
    )
    norm_scale = 1.0 / math.sqrt(lax.axis_size("row") * lax.axis_size("col") * slot_count)
    grad, probe_sum = reduce_call(acc, probe_flat, object_field.shape, norm_scale)
    return write_call(grad, probe_sum, probe_modes.shape)


def solution(mesh):
    in_specs = (
        P(None, "row", "col"),
        P(),
        P("row", "col", None, None, None),
        P("row", "col", None, None),
        P("row", "col"),
    )
    out_specs = (P(None, "row", "col"), P())
    return jax.shard_map(shards, mesh=mesh, in_specs=in_specs, out_specs=out_specs, check_vma=False)
```

```python
import functools
import math

import jax
import jax.numpy as jnp
import numpy as np
from jax import lax
from jax.experimental import pallas as pl
from jax.experimental.pallas import tpu as pltpu
from jax.sharding import PartitionSpec as P

HALO = 128
LANES = 128
PARTS = 2
HALO_LIMIT = 20


MESH = pl.DeviceIdType.MESH
SIDES = [(dr, dc) for dr in (-1, 0, 1) for dc in (-1, 0, 1) if (dr, dc) != (0, 0)]


def position():
    return (
        lax.axis_index("row"),
        lax.axis_index("col"),
        lax.axis_size("row"),
        lax.axis_size("col"),
    )


def exists(side):
    row, col, rows, cols = position()
    dr, dc = side
    inside = jnp.bool_(True)
    if dr:
        inside = row + dr >= 0 if dr < 0 else row + dr < rows
    if dc:
        other = col + dc >= 0 if dc < 0 else col + dc < cols
        inside = jnp.logical_and(inside, other) if dr else other
    return inside


def at_side(side):
    row, col, _, _ = position()
    return (row + side[0], col + side[1])


def opposite(side):
    return (-side[0], -side[1])


def part(step, margin, inner):
    return {-1: slice(0, margin), 0: slice(margin, margin + inner), 1: slice(margin + inner, None)}[
        step
    ]


def edge(step, margin, inner):
    return {-1: slice(0, margin), 0: slice(0, inner), 1: slice(inner - margin, inner)}[step]


def to_side(side, index, source, landing, send_sems, recv_sems):
    return pltpu.make_async_remote_copy(
        src_ref=source,
        dst_ref=landing,
        send_sem=send_sems.at[index],
        recv_sem=recv_sems.at[index],
        device_id=at_side(side),
        device_id_type=MESH,
    )


DIRECT = 2


def halo_kernel(whole_ref, ext_ref, acc_ref, pacc_ref, *scratch):
    object_ref, load_sem, row_land, col_land, corner_land, relay_land = scratch[:6]
    row_sems, col_sems, corner_sems, relay_sems = scratch[6:]
    row, col, n_row, n_col = position()
    side_rows, side_cols = object_ref.shape[1:]
    load = pltpu.make_async_copy(whole_ref, object_ref, load_sem)
    load.start()
    steps = (-1, 1)
    pieces = (slice(0, HALO), slice(side_cols - HALO, side_cols), slice(HALO, side_cols - HALO))
    direct = DIRECT * side_rows // 4
    parts = (slice(0, direct), slice(direct, side_rows))

    def has(dr, dc):
        return exists((dr, dc))

    def turns(d):
        return jnp.logical_and(has(0, d), lax.rem(col, 4) == (3 if d > 0 else 0))

    def relays(d):
        other = col - 3 * d
        inside = jnp.logical_and(other >= 0, other < n_col)
        return jnp.logical_and(inside, lax.rem(col, 4) == (2 if d > 0 else 1))

    def lands_by_relay(d):
        return jnp.logical_and(has(0, -d), lax.rem(col, 4) == (0 if d > 0 else 3))

    links = []
    for d in steps:
        links.append((has(d, 0), (row + d, col)))
        links.append((has(0, d), (row, col + d)))
        links.append((turns(d), (row, col + 3 * d)))
        links.append((relays(d), (row, col - 3 * d)))
        links.append((relays(d), (row, col - 2 * d)))
        links.append((lands_by_relay(d), (row, col + 2 * d)))
    barrier = pltpu.get_barrier_semaphore()
    count = jnp.int32(0)
    for there, device in links:

        @pl.when(there)
        def _(device=device):
            pl.semaphore_signal(barrier, inc=1, device_id=device, device_id_type=MESH)

        count = count + there.astype(jnp.int32)
    pl.semaphore_wait(barrier, count)

    def remote(source, landing, sems, index, device):
        return pltpu.make_async_remote_copy(
            src_ref=source,
            dst_ref=landing,
            send_sem=sems.at[0, index],
            recv_sem=sems.at[1, index],
            device_id=device,
            device_id_type=MESH,
        )

    def row_copy(s, p):
        d = steps[s]
        source = whole_ref.at[:, edge(d, HALO, side_rows), pieces[p]]
        return remote(
            source, row_land.at[1 - s, :, :, pieces[p]], row_sems, 3 * s + p, (row + d, col)
        )

    def col_copy(s, p, to_relay=False):
        d = steps[s]
        source = whole_ref.at[:, parts[p], edge(d, HALO, side_cols)]
        if to_relay:
            return pltpu.make_async_remote_copy(
                src_ref=source,
                dst_ref=relay_land.at[s],
                send_sem=col_sems.at[0, 2 * s + p],
                recv_sem=relay_sems.at[1, s],
                device_id=(row, col + 3 * d),
                device_id_type=MESH,
            )
        return remote(
            source, col_land.at[1 - s, :, parts[p], :], col_sems, 2 * s + p, (row, col + d)
        )

    def relay_copy(s):
        d = steps[s]
        return pltpu.make_async_remote_copy(
            src_ref=relay_land.at[s],
            dst_ref=col_land.at[1 - s, :, parts[1], :],
            send_sem=relay_sems.at[0, s],
            recv_sem=col_sems.at[1, 2 * s + 1],
            device_id=(row, col - 2 * d),
            device_id_type=MESH,
        )

    def corner_copy(r, s):
        source = row_land.at[r, :, :, pieces[s]]
        return remote(
            source, corner_land.at[r, 1 - s], corner_sems, 2 * r + s, (row, col + steps[s])
        )

    def when(condition, action):
        @pl.when(condition)
        def _():
            action()

    for p in range(2):
        for s, d in enumerate(steps):
            when(has(d, 0), lambda s=s, p=p: row_copy(s, p).start())
    for p in (1, 0):
        for s, d in enumerate(steps):
            if p:
                when(turns(d), lambda s=s: col_copy(s, 1, True).start())
                straight = jnp.logical_and(has(0, d), jnp.logical_not(turns(d)))
                when(straight, lambda s=s: col_copy(s, 1).start())
            else:
                when(has(0, d), lambda s=s: col_copy(s, 0).start())
    for s, d in enumerate(steps):
        when(has(d, 0), lambda s=s: row_copy(s, 2).start())

    acc_ref[...] = jnp.zeros(acc_ref.shape, jnp.float32)
    pacc_ref[...] = jnp.zeros(pacc_ref.shape, jnp.float32)
    spare = ext_ref.shape[1] - 1
    ext_ref[:, spare] = jnp.zeros((2, ext_ref.shape[2], LANES), jnp.float32)
    margin, inner = HALO // LANES, side_cols // LANES

    def tiles_of(d):
        return range(spare)[part(d, margin, inner)]

    def fill(rows, tiles, height, source):
        for k, t in enumerate(tiles):
            if source is None:
                ext_ref[:, t, rows, :] = jnp.zeros((2, height, LANES), ext_ref.dtype)
            else:
                ext_ref[:, t, rows, :] = source[:, :, k * LANES : (k + 1) * LANES].astype(
                    jnp.float32
                )

    load.wait()
    fill(part(0, HALO, side_rows), tiles_of(0), side_rows, object_ref)

    for s, d in enumerate(steps):

        def pass_on(s=s):
            relay_copy_in = col_copy(s, 1, True)
            relay_copy_in.wait_recv()
            relay_copy(s).start()

        when(relays(d), pass_on)
    for r, dr in enumerate(steps):
        for s, dc in enumerate(steps):

            def hand_over(r=r, s=s, dc=dc):
                row_copy(1 - r, s).wait_recv()
                when(has(0, dc), lambda: corner_copy(r, s).start())

            when(has(dr, 0), hand_over)
    for s, d in enumerate(steps):
        rows = part(0, HALO, side_rows)
        here = s

        def take(s=s, d=d, rows=rows):
            col_copy(1 - s, 0).wait_recv()
            col_copy(1 - s, 1).wait_recv()
            fill(rows, tiles_of(d), side_rows, col_land.at[s])

        when(has(0, d), take)
        when(
            jnp.logical_not(has(0, d)), lambda d=d, rows=rows: fill(rows, tiles_of(d), side_rows, None)
        )
    for r, dr in enumerate(steps):
        rows = part(dr, HALO, side_rows)

        def take_rows(r=r, rows=rows):
            row_copy(1 - r, 2).wait_recv()
            fill(rows, tiles_of(0), HALO, row_land.at[r])

        when(has(dr, 0), take_rows)
        when(
            jnp.logical_not(has(dr, 0)), lambda rows=rows: fill(rows, tiles_of(0), HALO, None)
        )
    for r, dr in enumerate(steps):
        rows = part(dr, HALO, side_rows)
        for s, dc in enumerate(steps):

            def take_corner(r=r, s=s, dc=dc, rows=rows):
                corner_copy(r, 1 - s).wait_recv()
                fill(rows, tiles_of(dc), HALO, corner_land.at[r, s])

            when(has(dr, dc), take_corner)
            when(
                jnp.logical_not(has(dr, dc)),
                lambda dc=dc, rows=rows: fill(rows, tiles_of(dc), HALO, None),
            )

    for s, d in enumerate(steps):
        for p in range(3):
            when(has(d, 0), lambda s=s, p=p: row_copy(s, p).wait_send())
        for p in range(2):
            when(has(0, d), lambda s=s, p=p: col_copy(s, p).wait_send())
        when(relays(d), lambda s=s: relay_copy(s).wait_send())
        for r, dr in enumerate(steps):
            when(has(dr, d), lambda r=r, s=s: corner_copy(r, s).wait_send())


def halo_call(object_field, probe_size):
    planes, side_rows, side_cols = object_field.shape
    kind = object_field.dtype
    vmem = pl.BlockSpec(memory_space=pltpu.VMEM)
    tiled = jax.ShapeDtypeStruct(
        (planes, (side_cols + 2 * HALO) // LANES + 1, side_rows + 2 * HALO, LANES), jnp.float32
    )
    direct = DIRECT * side_rows // 4
    return pl.pallas_call(
        halo_kernel,
        out_shape=(
            tiled,
            tiled,
            jax.ShapeDtypeStruct((probe_size // LANES, LANES), jnp.float32),
        ),
        in_specs=[pl.BlockSpec(memory_space=pltpu.HBM)],
        out_specs=3 * (vmem,),
        scratch_shapes=[
            pltpu.VMEM(object_field.shape, kind),
            pltpu.SemaphoreType.DMA,
            pltpu.VMEM((2, planes, HALO, side_cols), kind),
            pltpu.VMEM((2, planes, side_rows, HALO), kind),
            pltpu.VMEM((2, 2, planes, HALO, HALO), kind),
            pltpu.VMEM((2, planes, side_rows - direct, HALO), kind),
            pltpu.SemaphoreType.DMA((2, 6)),
            pltpu.SemaphoreType.DMA((2, 4)),
            pltpu.SemaphoreType.DMA((2, 4)),
            pltpu.SemaphoreType.DMA((2, 2)),
        ],
        compiler_params=pltpu.CompilerParams(
            collective_id=0, has_side_effects=True, vmem_limit_bytes=HALO_LIMIT * 1024 * 1024
        ),
        cost_estimate=pl.CostEstimate(flops=10**10, bytes_accessed=0, transcendentals=0),
        name="halo",
    )(pltpu.with_memory_space_constraint(object_field, pltpu.HBM))


def reduce_kernel(scale, acc_ref, pacc_ref, grad_ref, flat_ref, *scratch):
    count = len(SIDES)
    sends, landings, rest = scratch[:count], scratch[count : 2 * count], scratch[2 * count :]
    psend, pair_recv, merged, precv, sums, zbuf, full = rest[:7]
    side_sems, strip_sems, pair_sems, col_sems, row_sems = rest[7:]
    row, col, n_row, n_col = position()
    side_rows, side_cols = grad_ref.shape[1:]
    margin = HALO // LANES
    inner = side_cols // LANES
    part_rows = psend.shape[2]
    share = PARTS * part_rows
    chip, core = col // 2, lax.rem(col, 2)
    n_chip = n_col // 2
    sibling = (row, 2 * chip + 1 - core)

    barrier = pltpu.get_barrier_semaphore()
    waits = jnp.int32(n_row + n_chip - 1)
    pl.semaphore_signal(barrier, inc=1, device_id=sibling, device_id_type=MESH)
    for k in range(1, n_chip):
        peer = (row, 2 * lax.rem(chip + k, n_chip) + core)
        pl.semaphore_signal(barrier, inc=1, device_id=peer, device_id_type=MESH)
    for k in range(1, n_row):
        pl.semaphore_signal(
            barrier, inc=1, device_id=(lax.rem(row + k, n_row), col), device_id_type=MESH
        )
    for side in SIDES:
        if side[0] == 0:

            @pl.when(exists(side))
            def _(side=side):
                pl.semaphore_signal(barrier, inc=1, device_id=at_side(side), device_id_type=MESH)

            waits = waits + exists(side).astype(jnp.int32)

    def stage_side(index):
        dr, dc = SIDES[index]
        tiles = range(inner + 2 * margin)[part(dc, margin, inner)]
        for k, t in enumerate(tiles):
            sends[index][:, k] = acc_ref[:, t, part(dr, HALO, side_rows), :].astype(jnp.bfloat16)

    def stage_sides(chosen):
        for index, side in enumerate(SIDES):
            if chosen(side):
                stage_side(index)

    def to_peer(source, landing, sems, which, k, device):
        return pltpu.make_async_remote_copy(
            src_ref=source,
            dst_ref=landing,
            send_sem=sems.at[which, k],
            recv_sem=sems.at[which + 1, k],
            device_id=device,
            device_id_type=MESH,
        )

    def chip_at(k):
        return lax.rem(chip + k, n_chip)

    def chip_from(k):
        return lax.rem(chip + n_chip - k, n_chip)

    def chip_peer(k):
        return (row, 2 * chip_at(k) + core)

    def rows_of(index, h):
        return pl.ds(pl.multiple_of(index * share + h * part_rows, part_rows), part_rows)

    def pair_copy(h, k):
        return to_peer(
            psend.at[h, k], pair_recv.at[h, k], pair_sems, 0, h * n_chip + k, sibling
        )

    def scatter_copy(h, k):
        at = h * (n_chip - 1) + k - 1
        return to_peer(merged.at[h, k - 1], precv.at[h, k - 1], col_sems, 0, at, chip_peer(k))

    def row_copy(h, k, owner):
        at = h * (n_row - 1) + k - 1
        peer = (lax.rem(row + k, n_row), col)
        return to_peer(zbuf.at[h, row], zbuf.at[h, owner], row_sems, 0, at, peer)

    def gather_copy(h, k, owner):
        at = h * (n_chip - 1) + k - 1
        source, landing = full.at[rows_of(col, h), :], full.at[rows_of(owner, h), :]
        return to_peer(source, landing, col_sems, 2, at, chip_peer(k))

    def forward_copy(h, k, side):
        source = full.at[rows_of(2 * chip_from(k) + core, h), :]
        landing = full.at[rows_of(2 * chip_from(k) + side, h), :]
        return to_peer(source, landing, pair_sems, 2, h * n_chip + k, sibling)

    def side_copy(index):
        side = (0, SIDES[index][1])
        return to_side(
            side, index, sends[index], landings[index], side_sems.at[0], side_sems.at[1]
        )

    strips = [index for index, side in enumerate(SIDES) if side[1] == 0]
    pieces = (slice(margin, inner - margin), slice(0, margin), slice(inner - margin, inner))

    def strip_copy(r, p):
        index = strips[r]
        source, landing = sends[index].at[:, pieces[p]], landings[index].at[:, pieces[p]]
        return to_peer(source, landing, strip_sems, 0, 3 * r + p, at_side(SIDES[index]))

    def start_middles():
        for r, index in enumerate(strips):
            dr = SIDES[index][0]
            for k in range(margin, inner - margin):
                sends[index][:, k] = acc_ref[:, margin + k, part(dr, HALO, side_rows), :].astype(
                    jnp.bfloat16
                )

            @pl.when(exists(SIDES[index]))
            def _(r=r):
                strip_copy(r, 0).start()

    def start_edges():
        for r, index in enumerate(strips):
            dr = SIDES[index][0]
            for p, dc in ((1, -1), (2, 1)):
                corner = SIDES.index((dr, -dc))
                tiles = range(inner)[pieces[p]]
                rows = part(dr, HALO, side_rows)

                @pl.when(exists((dr, dc)))
                def _(index=index, corner=corner, tiles=tiles, rows=rows):
                    side_copy(corner).wait_recv()
                    for k, t in enumerate(tiles):
                        own = acc_ref[:, margin + t, rows, :]
                        sends[index][:, t] = (
                            own + landings[corner][:, k].astype(jnp.float32)
                        ).astype(jnp.bfloat16)

                @pl.when(jnp.logical_and(exists((dr, 0)), jnp.logical_not(exists((0, dc)))))
                def _(index=index, tiles=tiles, rows=rows):
                    for t in tiles:
                        sends[index][:, t] = acc_ref[:, margin + t, rows, :].astype(jnp.bfloat16)

                @pl.when(exists((dr, 0)))
                def _(r=r, p=p):
                    strip_copy(r, p).start()

    def add_rows():
        for r, index in enumerate(strips):
            dr = -SIDES[index][0]
            rows = edge(dr, HALO, side_rows)

            @pl.when(exists((dr, 0)))
            def _(r=r, index=index, rows=rows):
                for p in range(3):
                    strip_copy(r, p).wait_recv()
                for t in range(inner):
                    grad_ref[:, rows, t * LANES : (t + 1) * LANES] += landings[index][
                        :, t
                    ].astype(jnp.float32)

    def start_sides(chosen):
        for index, side in enumerate(SIDES):
            if chosen(side):

                @pl.when(exists(side))
                def _(index=index):
                    side_copy(index).start()

    def add_sides(chosen):
        for index, side in enumerate(SIDES):
            if not chosen(side):
                continue
            dr, dc = opposite(side)
            rows = edge(dr, HALO, side_rows)
            tiles = range(inner)[edge(dc, margin, inner)]

            @pl.when(exists((dr, dc)))
            def _(index=index, rows=rows, tiles=tiles):
                side_copy(index).wait_recv()
                for k, t in enumerate(tiles):
                    grad_ref[:, rows, t * LANES : (t + 1) * LANES] += landings[index][
                        :, k
                    ].astype(jnp.float32)

    over_cols = lambda side: side[0] == 0
    corners = lambda side: side[0] != 0 and side[1] != 0
    order = list(range(1, n_chip)) + [0]
    for h in range(PARTS):
        for k in order:
            psend[h, k] = pacc_ref[rows_of(2 * chip_at(k) + 1 - core, h), :].astype(jnp.bfloat16)
    stage_sides(corners)
    pl.semaphore_wait(barrier, waits)
    for h in range(PARTS):
        for k in order:
            pair_copy(h, k).start()
    start_middles()
    stage_sides(over_cols)

    def merge(h, k):
        pair_copy(h, k).wait_recv()
        own = pacc_ref[rows_of(2 * chip_at(k) + core, h), :]
        return own + pair_recv[h, k].astype(jnp.float32)

    for h in range(PARTS):
        for k in range(1, n_chip):
            merged[h, k - 1] = merge(h, k).astype(jnp.bfloat16)
            scatter_copy(h, k).start()
        sums[h] = merge(h, 0)
    start_sides(corners)
    start_sides(over_cols)
    for t in range(inner):
        grad_ref[:, :, t * LANES : (t + 1) * LANES] = acc_ref[
            :, margin + t, HALO : HALO + side_rows, :
        ]
    for h in range(PARTS):
        total = sums[h]
        for k in range(1, n_chip):
            scatter_copy(h, k).wait_recv()
            total = total + precv[h, k - 1].astype(jnp.float32)
        zbuf[h, row] = total.astype(jnp.bfloat16)
        for k in range(1, n_row):
            row_copy(h, k, row).start()
    start_edges()
    for h in range(PARTS):
        for k in range(1, n_row):
            row_copy(h, k, lax.rem(row + n_row - k, n_row)).wait_recv()
        total = zbuf[h, 0].astype(jnp.float32)
        for k in range(1, n_row):
            total = total + zbuf[h, k].astype(jnp.float32)
        full[rows_of(col, h), :] = (total * scale).astype(jnp.bfloat16)
        for k in range(1, n_chip):
            gather_copy(h, k, col).start()
        forward_copy(h, 0, core).start()

    def unpack(h, k, side):
        rows = rows_of(2 * chip_from(k) + side, h)
        flat_ref[rows, :] = full[rows, :].astype(jnp.float32)

    for h in range(PARTS):
        unpack(h, 0, core)
        for k in range(1, n_chip):
            gather_copy(h, k, 2 * chip_from(k) + core).wait_recv()
            forward_copy(h, k, core).start()
            unpack(h, k, core)
    add_rows()
    add_sides(over_cols)
    for h in range(PARTS):
        for k in range(n_chip):
            forward_copy(h, k, 1 - core).wait_recv()
            unpack(h, k, 1 - core)
    for h in range(PARTS):
        for k in range(1, n_chip):
            scatter_copy(h, k).wait_send()
            gather_copy(h, k, col).wait_send()
        for k in range(n_chip):
            pair_copy(h, k).wait_send()
            forward_copy(h, k, core).wait_send()
        for k in range(1, n_row):
            row_copy(h, k, row).wait_send()
    for index, side in enumerate(SIDES):

        @pl.when(exists(side))
        def _(index=index):
            if index in strips:
                for p in range(3):
                    strip_copy(strips.index(index), p).wait_send()
            else:
                side_copy(index).wait_send()


def reduce_call(acc, probe_flat, object_shape, scale):
    n_row, n_col = lax.axis_size("row"), lax.axis_size("col")
    _, side_rows, side_cols = object_shape
    inner = side_cols // LANES
    margin = HALO // LANES
    vmem = pl.BlockSpec(memory_space=pltpu.VMEM)
    buffers = []
    for dr, dc in SIDES:
        buffers.append(
            pltpu.VMEM(
                (2, margin if dc else inner, HALO if dr else side_rows, LANES), jnp.bfloat16
            )
        )
    total_rows = probe_flat.shape[0]
    piece = total_rows // n_col // PARTS
    n_chip = n_col // 2
    return pl.pallas_call(
        functools.partial(reduce_kernel, scale),
        out_shape=(
            jax.ShapeDtypeStruct(object_shape, jnp.float32),
            jax.ShapeDtypeStruct(probe_flat.shape, jnp.float32),
        ),
        in_specs=[vmem, vmem],
        out_specs=(vmem, vmem),
        scratch_shapes=buffers
        + buffers
        + [
            pltpu.VMEM((PARTS, n_chip, piece, LANES), jnp.bfloat16),
            pltpu.VMEM((PARTS, n_chip, piece, LANES), jnp.bfloat16),
            pltpu.VMEM((PARTS, n_chip - 1, piece, LANES), jnp.bfloat16),
            pltpu.VMEM((PARTS, n_chip - 1, piece, LANES), jnp.bfloat16),
            pltpu.VMEM((PARTS, piece, LANES), jnp.float32),
            pltpu.VMEM((PARTS, n_row, piece, LANES), jnp.bfloat16),
            pltpu.VMEM((total_rows, LANES), jnp.bfloat16),
            pltpu.SemaphoreType.DMA((2, len(SIDES))),
            pltpu.SemaphoreType.DMA((2, 6)),
            pltpu.SemaphoreType.DMA((4, PARTS * n_chip)),
            pltpu.SemaphoreType.DMA((4, PARTS * (n_chip - 1))),
            pltpu.SemaphoreType.DMA((2, PARTS * (n_row - 1))),
        ],
        compiler_params=pltpu.CompilerParams(
            collective_id=1, has_side_effects=True, vmem_limit_bytes=20 * 1024 * 1024
        ),
        name="reduce",
    )(acc, probe_flat)


def write_kernel(grad_in, flat_ref, grad_ref, probe_ref, sems):
    parts, modes, fs, width = probe_ref.shape
    copies = []
    for p in range(parts):
        for m in range(modes):
            for t in range(width // LANES):
                at = len(copies) * fs
                target = probe_ref.at[p, m, :, t * LANES : (t + 1) * LANES]
                sem = sems.at[len(copies)]
                copies.append(pltpu.make_async_copy(flat_ref.at[at : at + fs, :], target, sem))
    for p in range(grad_in.shape[0]):
        copies.append(pltpu.make_async_copy(grad_in.at[p], grad_ref.at[p], sems.at[len(copies)]))
    for copy in copies:
        copy.start()
    for copy in copies:
        copy.wait()


def write_call(grad, probe_flat, probe_shape):
    vmem = pl.BlockSpec(memory_space=pltpu.VMEM)
    hbm = pl.BlockSpec(memory_space=pltpu.HBM)
    count = probe_flat.shape[0] // probe_shape[2] + grad.shape[0]
    return pl.pallas_call(
        write_kernel,
        out_shape=(
            jax.ShapeDtypeStruct(grad.shape, grad.dtype),
            jax.ShapeDtypeStruct(probe_shape, jnp.float32),
        ),
        in_specs=[vmem, vmem],
        out_specs=(hbm, hbm),
        scratch_shapes=[pltpu.SemaphoreType.DMA((count,))],
        compiler_params=pltpu.CompilerParams(vmem_limit_bytes=8 * 1024 * 1024),
        name="write",
    )(grad, probe_flat)


def fourier_tables(frame_side):
    indices = np.arange(frame_side)
    product = indices[:, None] * indices[None, :] % frame_side
    angles = 2.0 * math.pi / frame_side * product
    norm_scale = 1.0 / math.sqrt(frame_side)
    real, imag = np.cos(angles) * norm_scale, -np.sin(angles) * norm_scale
    tables = (np.block([[real, -imag], [imag, real]]), np.block([[real, imag], [-imag, real]]))
    return tuple(jnp.asarray(table.astype(np.float32)).astype(jnp.bfloat16) for table in tables)


CHUNK = 16


def dot32(left, right):
    return jnp.dot(left, right, preferred_element_type=jnp.float32)


def frames_kernel(
    count_ref, at_ref, ext_ref, probe_ref, amp_ref, fwd, inv, zero_ref, pzero_ref,
    acc_ref, pacc_ref, *buffers,
):
    fs = probe_ref.shape[-1]
    modes = probe_ref.shape[1]
    lane_tiles = fs // LANES
    last_slot = amp_ref.shape[0] - 1
    live = count_ref[0, 0]
    even, odd = buffers[:4], buffers[4:]
    odd[2][...] = jnp.zeros(odd[2].shape, jnp.float32)
    odd[3][...] = jnp.zeros(odd[3].shape, jnp.float32)

    def two_sided(buffer, left_table, right_table):
        stage, half, wide, _ = buffer
        for m in range(modes):
            both = dot32(left_table[...], stage[:, m * fs : (m + 1) * fs])
            half[m * fs : (m + 1) * fs, :fs] = both[:fs].astype(jnp.bfloat16)
            half[m * fs : (m + 1) * fs, fs:] = both[fs:].astype(jnp.bfloat16)
        wide[...] = dot32(half[...], right_table[...])

    def make_exit(buffer, slot):
        stage, _, _, patch = buffer
        row_at = at_ref[0, slot]
        col_at = at_ref[1, slot]
        tile_at = col_at // LANES
        shift = col_at % LANES
        back_shift = (LANES - shift) % LANES
        lane = lax.broadcasted_iota(jnp.int32, (CHUNK, LANES), 1)
        keep_low = lane < LANES - shift
        for r in range(0, fs, CHUNK):
            rows = slice(r, r + CHUNK)
            values = []
            for plane in range(2):
                rolled = [
                    pltpu.roll(
                        ext_ref[plane, tile_at + t, pl.ds(row_at + r, CHUNK), :], back_shift, 1
                    )
                    for t in range(lane_tiles + 1)
                ]
                values.append(
                    [jnp.where(keep_low, rolled[t], rolled[t + 1]) for t in range(lane_tiles)]
                )
            for t in range(lane_tiles):
                cols = slice(t * LANES, (t + 1) * LANES)
                patch_real, patch_imag = values[0][t], values[1][t]
                patch[0, rows, cols] = patch_real
                patch[1, rows, cols] = patch_imag
                for m in range(modes):
                    probe_real = probe_ref[0, m, rows, cols]
                    probe_imag = probe_ref[1, m, rows, cols]
                    out = slice(m * fs + t * LANES, m * fs + (t + 1) * LANES)
                    stage[rows, out] = (
                        probe_real * patch_real - probe_imag * patch_imag
                    ).astype(jnp.bfloat16)
                    stage[fs + r : fs + r + CHUNK, out] = (
                        probe_real * patch_imag + probe_imag * patch_real
                    ).astype(jnp.bfloat16)

    def make_chi(buffer, slot, valid):
        stage, _, wide, _ = buffer
        for r in range(0, fs, CHUNK):
            for t in range(lane_tiles):
                cols = slice(t * LANES, (t + 1) * LANES)
                imag_cols = slice(fs + t * LANES, fs + (t + 1) * LANES)
                psi = []
                power = None
                for m in range(modes):
                    rows = slice(m * fs + r, m * fs + r + CHUNK)
                    real, imag = wide[rows, cols], wide[rows, imag_cols]
                    psi.append((real, imag))
                    own = real * real + imag * imag
                    power = own if power is None else power + own
                amp = amp_ref[slot, r : r + CHUNK, cols].astype(jnp.float32)
                factor = 1.0 - amp * lax.rsqrt(jnp.maximum(power, 0.25))
                if valid is not None:
                    factor = jnp.where(valid, factor, 0.0)
                for m in range(modes):
                    out = slice(m * fs + t * LANES, m * fs + (t + 1) * LANES)
                    stage[r : r + CHUNK, out] = (psi[m][0] * factor).astype(jnp.bfloat16)
                    stage[fs + r : fs + r + CHUNK, out] = (psi[m][1] * factor).astype(jnp.bfloat16)

    def add_grads(buffer, slot):
        _, _, wide, patch = buffer
        row_at = at_ref[0, slot]
        col_at = at_ref[1, slot]
        tile_at = col_at // LANES
        shift = col_at % LANES
        lane = lax.broadcasted_iota(jnp.int32, (CHUNK, LANES), 1)
        from_same = lane >= shift
        for r in range(0, fs, CHUNK):
            grads = [[], []]
            for t in range(lane_tiles):
                cols = slice(t * LANES, (t + 1) * LANES)
                imag_cols = slice(fs + t * LANES, fs + (t + 1) * LANES)
                patch_real = patch[0, r : r + CHUNK, cols]
                patch_imag = patch[1, r : r + CHUNK, cols]
                total_real = total_imag = None
                for m in range(modes):
                    rows = slice(m * fs + r, m * fs + r + CHUNK)
                    real, imag = wide[rows, cols], wide[rows, imag_cols]
                    probe_real = probe_ref[0, m, r : r + CHUNK, cols]
                    probe_imag = probe_ref[1, m, r : r + CHUNK, cols]
                    own_real = probe_real * real + probe_imag * imag
                    own_imag = probe_real * imag - probe_imag * real
                    total_real = own_real if m == 0 else total_real + own_real
                    total_imag = own_imag if m == 0 else total_imag + own_imag
                    at = (m * lane_tiles + t) * fs + r
                    pacc_ref[at : at + CHUNK, :] += patch_real * real + patch_imag * imag
                    at += modes * lane_tiles * fs
                    pacc_ref[at : at + CHUNK, :] += patch_real * imag - patch_imag * real
                grads[0].append(pltpu.roll(total_real, shift, 1))
                grads[1].append(pltpu.roll(total_imag, shift, 1))
            for plane in range(2):
                rolled = grads[plane]
                for t in range(lane_tiles + 1):
                    same = rolled[t] if t < lane_tiles else 0.0
                    before = rolled[t - 1] if t > 0 else 0.0
                    where = (plane, tile_at + t, pl.ds(row_at + r, CHUNK), slice(None))
                    acc_ref[where] += jnp.where(from_same, same, before)

    def advance(pair, carry):
        first = 2 * pair
        second = jnp.minimum(first + 1, last_slot)
        make_exit(even, first)
        two_sided(even, fwd, inv)
        add_grads(odd, jnp.maximum(first - 1, 0))
        make_exit(odd, second)
        two_sided(odd, fwd, inv)
        make_chi(even, first, None)
        two_sided(even, inv, fwd)
        make_chi(odd, second, first + 1 < live)
        two_sided(odd, inv, fwd)
        add_grads(even, first)
        return carry

    pairs = (live + 1) // 2
    lax.fori_loop(0, pairs, advance, 0)
    add_grads(odd, jnp.minimum(2 * pairs - 1, last_slot))


def frames_call(extended, zeros, probe_modes, amplitudes, positions, live_count, tables):
    fs = probe_modes.shape[-1]
    modes = probe_modes.shape[1]
    tiled = extended.shape
    vmem = pl.BlockSpec(memory_space=pltpu.VMEM)
    smem = pl.BlockSpec(memory_space=pltpu.SMEM)
    return pl.pallas_call(
        frames_kernel,
        out_shape=(
            jax.ShapeDtypeStruct(tiled, jnp.float32),
            jax.ShapeDtypeStruct((probe_modes.size // LANES, LANES), jnp.float32),
        ),
        in_specs=[smem, smem] + 7 * [vmem],
        out_specs=(vmem, vmem),
        input_output_aliases={7: 0, 8: 1},
        scratch_shapes=2
        * [
            pltpu.VMEM((2 * fs, modes * fs), jnp.bfloat16),
            pltpu.VMEM((modes * fs, 2 * fs), jnp.bfloat16),
            pltpu.VMEM((modes * fs, 2 * fs), jnp.float32),
            pltpu.VMEM((2, fs, fs), jnp.float32),
        ],
        compiler_params=pltpu.CompilerParams(vmem_limit_bytes=26 * 1024 * 1024),
        name="frames",
    )(live_count, positions, extended, probe_modes, amplitudes, *tables, *zeros)


def shards(object_field, probe_modes, measured_amp, scan_positions, frame_counts):
    slot_count = measured_amp.shape[2]
    extended, *zeros = halo_call(object_field, probe_modes.size)
    acc, probe_flat = frames_call(
        extended,
        zeros,
        probe_modes,
        measured_amp[0, 0],
        scan_positions[0, 0],
        frame_counts,
        fourier_tables(probe_modes.shape[-1]),
    )
    norm_scale = 1.0 / math.sqrt(lax.axis_size("row") * lax.axis_size("col") * slot_count)
    grad, probe_sum = reduce_call(acc, probe_flat, object_field.shape, norm_scale)
    return write_call(grad, probe_sum, probe_modes.shape)


def solution(mesh):
    in_specs = (
        P(None, "row", "col"),
        P(),
        P("row", "col", None, None, None),
        P("row", "col", None, None),
        P("row", "col"),
    )
    out_specs = (P(None, "row", "col"), P())
    return jax.shard_map(shards, mesh=mesh, in_specs=in_specs, out_specs=out_specs, check_vma=False)
```
